32 devices in a mesh: dp: 8 (over y, x, core), seq: 4 (over z).
Axes of the slice: x: 2, y: 2, z: 4, core: 2. Of those that a mesh axis runs over, the one named last changes fastest.
Arguments:
- inputs: bfloat16 [8, 1024, 768], P('dp', 'seq'), may hold values from -6 to 6
- d_out: bfloat16 [8, 1024, 768], P('dp', 'seq'), may hold values from -6 to 6
- segments: int32 [8, 1024], P('dp'), may hold values from 0 to 1023, as said below
- buckets: int32 [2048], replicated, may hold values from 0 to 31
- w_query: bfloat16 [768, 768], P(('dp', 'seq')), may hold values from -0.21875 to 0.21875
- w_key: bfloat16 [768, 768], P(('dp', 'seq')), may hold values from -0.21875 to 0.21875
- w_value: bfloat16 [768, 768], P(('dp', 'seq')), may hold values from -0.21875 to 0.21875
- w_out: bfloat16 [768, 768], P(('dp', 'seq')), may hold values from -1.75 to 1.75
- w_gate: bfloat16 [768, 2048], P(('dp', 'seq')), may hold values from -0.21875 to 0.21875
- w_up: bfloat16 [768, 2048], P(('dp', 'seq')), may hold values from -0.21875 to 0.21875
- w_down: bfloat16 [2048, 768], P(('dp', 'seq')), may hold values from -0.1875 to 0.1875
- gain_attn: float32 [768], replicated, may hold values from 0.1 to 1.9
- gain_ffn: float32 [768], replicated, may hold values from 0.1 to 1.9
- bias_table: float32 [32, 12], replicated, may hold values from -4 to 4
Outputs:
- output: bfloat16 [8, 1024, 768], P('dp', 'seq')
- d_inputs: float32 [8, 1024, 768], P('dp', 'seq')
- grad_query: float32 [768, 768], P(('dp', 'seq'))
- grad_key: float32 [768, 768], P(('dp', 'seq'))
- grad_value: float32 [768, 768], P(('dp', 'seq'))
- grad_out: float32 [768, 768], P(('dp', 'seq'))
- grad_gate: float32 [768, 2048], P(('dp', 'seq'))
- grad_up: float32 [768, 2048], P(('dp', 'seq'))
- grad_down: float32 [2048, 768], P(('dp', 'seq'))
- grad_gain_attn: float32 [768], replicated
- grad_gain_ffn: float32 [768], replicated
- grad_table: float32 [32, 12], replicated
The draws below stay inside these ranges and needn't reach their ends.
Inputs may be any that keep to these rules, and one draw needn't show every extreme that they name: `segments`: each row's label is the index of the last row of its document within the sequence; labels never fall along a sequence, and rows share a document exactly when they share a label.
All inputs are finite; a program needn't handle non-finite values.
Results may differ from the reference program's by a relative error of at most 0.015.
Values may be sent and summed in bfloat16 or wider, within the bound.
No kernel may reach another device: no remote copies, remote signals or barrier semaphores. Data moves between devices by JAX's collectives and lax.ppermute only.
A program may use at most 192 MiB of HBM per device.

```python
import jax
import jax.numpy as jnp
from jax import lax

D = 768
H = 12
DH = 64
FF = 2048
NB = 32
ROWS_DEV = 256
SEQ_DP = 1
LENGTH = 1024
SEQS = 8


def draw_segments(key, part):
    pick_key, left_key, right_key, flag_key = jax.random.split(key, 4)
    chosen = jax.random.randint(pick_key, (SEQS // SEQ_DP,), 0, SEQ_DP)
    spanning = jnp.arange(SEQS) % SEQ_DP == jnp.repeat(chosen, SEQ_DP)
    starts_at = jax.random.randint(left_key, (SEQS,), 1, ROWS_DEV)
    ends_at = LENGTH - 1 - jax.random.randint(right_key, (SEQS,), 1, ROWS_DEV)
    integer_draw = jax.random.randint(flag_key, (SEQS, LENGTH), 0, 48)
    positions = jnp.arange(LENGTH, dtype=jnp.int32)[None, :]
    at_edge = (positions < starts_at[:, None]) | (positions > ends_at[:, None] + 1)
    span_flags = at_edge & (integer_draw % 4 == 0) | (positions == starts_at[:, None]) | (positions == ends_at[:, None] + 1)
    other_flags = integer_draw == 0
    flag_rows = (jnp.where(spanning[:, None], span_flags, other_flags) | (positions == 1)) & (positions > 0)
    next_start = jnp.where(flag_rows, positions, LENGTH).astype(jnp.int32)
    shifted = jnp.concatenate([next_start[:, 1:], jnp.full((SEQS, 1), LENGTH, jnp.int32)], axis=1)
    return lax.cummin(shifted, axis=1, reverse=True) - 1


def plant(values, stream_key, low, high):
    longest = values.shape.index(max(values.shape))
    spots = []
    for shift in (0, 1):
        where = [jax.random.randint(jax.random.fold_in(stream_key, axis), (), 0, length) for axis, length in enumerate(values.shape)]
        where[longest] = (where[longest] + shift) % values.shape[longest]
        spots.append(tuple(where))
    return values.at[spots[0]].set(low).at[spots[1]].set(high)


def levels(rng, dims, pieces, low, largest):
    def one(position, parts):
        heights = jax.random.uniform(jax.random.fold_in(jax.random.fold_in(rng, 6), position), (parts,), jnp.float32, low / len(pieces), largest / len(pieces))
        return jnp.repeat(jnp.exp(heights), dims[position] // parts).reshape((-1,) + (1,) * (len(dims) - position - 1))

    level = one(*pieces[0])
    for cut in pieces[1:]:
        level = level * one(*cut)
    return level


def scatter_about(key, dims, deviation, limit, cuts=(), kind=jnp.bfloat16):
    loudness = levels(key, dims, cuts, -0.22, 0.18) if cuts else 1.0
    entries = jax.random.normal(key, dims, jnp.float32) * deviation * loudness
    return jnp.minimum(jnp.maximum(entries, -limit), limit).astype(kind)


def setup_inputs(seed: int = 0) -> dict:
    arg_keys = jax.random.split(jax.random.key(seed), 15)
    inputs = scatter_about(arg_keys[0], (SEQS, LENGTH, D), 1.0, 6.0, ((0, 8), (1, 4)))
    d_out = scatter_about(arg_keys[1], (SEQS, LENGTH, D), 1.0, 6.0, ((0, 8), (1, 4)))
    segments = draw_segments(jax.random.fold_in(arg_keys[14], 71), 0)
    buckets = plant(jax.random.randint(arg_keys[3], (2 * LENGTH,), 0, NB), jax.random.fold_in(arg_keys[3], 1), 0, NB - 1).astype(jnp.int32)
    w_query = scatter_about(arg_keys[4], (D, D), D ** -0.5, 0.21875, ((0, 32),))
    w_key = scatter_about(arg_keys[5], (D, D), D ** -0.5, 0.21875, ((0, 32),))
    w_value = scatter_about(arg_keys[6], (D, D), D ** -0.5, 0.21875, ((0, 32),))
    w_out = scatter_about(arg_keys[7], (D, D), (D // 64) ** -0.5, 1.75, ((0, 32),))
    w_gate = scatter_about(arg_keys[8], (D, FF), D ** -0.5, 0.21875, ((0, 32),))
    w_up = scatter_about(arg_keys[9], (D, FF), D ** -0.5, 0.21875, ((0, 32),))
    w_down = scatter_about(arg_keys[10], (FF, D), (FF // 2) ** -0.5, 0.1875, ((0, 32),))
    gain_attn = jnp.clip(1.0 + 0.18 * jax.random.normal(arg_keys[11], (D,), jnp.float32), 0.1, 1.9)
    gain_ffn = jnp.clip(1.0 + 0.18 * jax.random.normal(arg_keys[12], (D,), jnp.float32), 0.1, 1.9)
    bias_table = scatter_about(arg_keys[13], (NB, H), 1.0, 4.0, (), jnp.float32)
    return dict(inputs=inputs, d_out=d_out, segments=segments, buckets=buckets, w_query=w_query, w_key=w_key, w_value=w_value, w_out=w_out, w_gate=w_gate, w_up=w_up, w_down=w_down, gain_attn=gain_attn, gain_ffn=gain_ffn, bias_table=bias_table)


EPS = 1e-06
MASKED = -1000000000.0
HIGHEST = lax.Precision.HIGHEST

@jax.custom_vjp
def low(v):
    return lax.optimization_barrier(v.astype(jnp.bfloat16)).astype(jnp.float32)

@jax.custom_vjp
def low_back(v):
    return v

def low_keep(v):
    return (low(v), None)

def low_pass(kept, grad):
    return (grad,)

def back_keep(v):
    return (v, None)

def back_low(kept, grad):
    return (low(grad),)
low.defvjp(low_keep, low_pass)
low_back.defvjp(back_keep, back_low)

def rms_norm(values, gain):
    return values * lax.rsqrt(lax.optimization_barrier(jnp.mean(values * values, axis=-1, keepdims=True)) + EPS) * gain

def matmul(left, right):
    return jnp.dot(left, right, precision=HIGHEST)

def attention_seq(queries, keys, values, seg_row, buckets, table):
    seq_len = keys.shape[0]
    key_block = min(512, seq_len)
    block_count = seq_len // key_block
    query_heads = queries.reshape(block_count, key_block, H, DH)
    key_heads = keys.reshape(seq_len, H, DH)
    value_heads = values.reshape(seq_len, H, DH)
    scale = DH ** (-0.5)
    positions = jnp.arange(seq_len, dtype=jnp.int32)

    def one_block(packed):
        query_blk, start = packed
        row_ids = start + jnp.arange(key_block, dtype=jnp.int32)
        relative = positions[None, :] - row_ids[:, None] + seq_len
        bias_blk = jnp.transpose(table[buckets[relative]], (2, 0, 1))
        raw_scores = jnp.einsum('qhd,khd->hqk', query_blk, key_heads, precision=HIGHEST) * scale + bias_blk
        raw_scores = low_back(raw_scores)
        seg_query = lax.dynamic_slice_in_dim(seg_row, start, key_block)
        same_doc = (seg_query[:, None] == seg_row[None, :])[None]
        weights_exp = jnp.exp(jnp.where(same_doc, raw_scores, MASKED))
        totals = lax.optimization_barrier(jnp.sum(weights_exp, axis=-1))
        unnorm = low_back(jnp.einsum('hqk,khd->qhd', low(weights_exp), value_heads, precision=HIGHEST))
        return unnorm / jnp.transpose(totals)[:, :, None]
    starts = jnp.arange(block_count, dtype=jnp.int32) * key_block
    result = lax.map(jax.checkpoint(one_block), (query_heads, starts))
    return result.reshape(seq_len, H * DH)

def layer(inputs, seg_row, buckets, w_query, w_key, w_value, w_out, w_gate, w_up, w_down, gain_attn, gain_ffn, table):
    normed = low(rms_norm(inputs, gain_attn))
    queries = low_back(low(matmul(normed, w_query)))
    keys = low_back(low(matmul(normed, w_key)))
    values = low_back(low(matmul(normed, w_value)))
    attn_rows = low(attention_seq(queries, keys, values, seg_row, buckets, table))
    mixed_rows = inputs + low_back(matmul(attn_rows, w_out))
    normed_two = low(rms_norm(mixed_rows, gain_ffn))
    gate_act = low_back(matmul(normed_two, w_gate))
    up_act = low_back(matmul(normed_two, w_up))
    hidden = low(jax.nn.gelu(gate_act, approximate=True) * up_act)
    return mixed_rows + low_back(matmul(hidden, w_down))

def reference(inputs, d_out, segments, buckets, w_query, w_key, w_value, w_out, w_gate, w_up, w_down, gain_attn, gain_ffn, bias_table):
    float_in = inputs.astype(jnp.float32)
    weights = tuple((w.astype(jnp.float32) for w in (w_query, w_key, w_value, w_out, w_gate, w_up, w_down)))

    def forward(all_rows, wq_f, wk_f, wv_f, wo_f, wg_f, wu_f, wd_f, gain_one, gain_two, table):

        def step(state_in, packed):
            seq_rows, seg_row = packed
            return (state_in, layer(seq_rows, seg_row, buckets, wq_f, wk_f, wv_f, wo_f, wg_f, wu_f, wd_f, gain_one, gain_two, table))
        _, result = lax.scan(step, jnp.zeros((), jnp.float32), (all_rows, segments))
        return result
    result, back_fn = jax.vjp(forward, float_in, *weights, gain_attn, gain_ffn, bias_table)
    grads = back_fn(d_out.astype(jnp.float32))
    return (result.astype(jnp.bfloat16), grads[0], grads[1], grads[2], grads[3], grads[4], grads[5], grads[6], grads[7], grads[8], grads[9], grads[10])
```

```python
import jax
import jax.numpy as jnp
from jax import lax
from jax.experimental import pallas as pl
from jax.experimental.pallas import tpu as pltpu
from jax.sharding import PartitionSpec as P

EPS = 1e-06
MASKED = -1000000000.0
HIGHEST = lax.Precision.HIGHEST
GELU_A = 0.7978845608028654
GELU_B = 0.044715
VMEM_LIMIT = 56 * 1024 * 1024


def norm_rows(values, gain):
    return values * lax.rsqrt(jnp.mean(values * values, axis=-1, keepdims=True) + EPS) * gain


def geglu(gate_act, up_act):
    return jax.nn.gelu(gate_act, approximate=True) * up_act


def matmul(left, right):
    return jnp.dot(left, right, preferred_element_type=jnp.float32)


def left_matmul(left, right):
    return lax.dot_general(
        left, right, (((0,), (0,)), ((), ())), preferred_element_type=jnp.float32
    )


def right_matmul(left, right):
    return lax.dot_general(
        left, right, (((1,), (1,)), ((), ())), preferred_element_type=jnp.float32
    )


def shifted_bias(per_dist, query_count, key_count):
    head_count, width = per_dist.shape
    flipped = per_dist[:, ::-1]
    tiled = jnp.tile(flipped, (1, query_count + 1))[:, : query_count * (width + 1)]
    rows = tiled.reshape(head_count, query_count, width + 1)[:, :, :key_count]
    return rows[:, :, ::-1]


def diagonal_sums(scores):
    head_count, row_count, col_count = scores.shape
    row_width = row_count + col_count
    padded = jnp.concatenate(
        [jnp.zeros((head_count, row_count, row_count), scores.dtype), scores], axis=2
    )
    flat_rows = jnp.concatenate(
        [
            padded.reshape(head_count, row_count * row_width),
            jnp.zeros((head_count, row_count), scores.dtype),
        ],
        axis=1,
    )
    skewed = flat_rows.reshape(head_count, row_count, row_width + 1)
    return jnp.sum(skewed, axis=1)[:, 1:row_width]


def block_parts(
    queries,
    key_heads,
    value_heads,
    seg_query,
    seg_all,
    buckets,
    table,
    first_row,
    blk_index,
    key_block,
):
    query_count = queries.shape[0]
    seq_len = key_heads.shape[0]
    scale = queries.shape[-1] ** (-0.5)
    key_start = blk_index * key_block
    key_blk = lax.dynamic_slice_in_dim(key_heads, key_start, key_block)
    value_blk = lax.dynamic_slice_in_dim(value_heads, key_start, key_block)
    seg_keys = lax.dynamic_slice_in_dim(seg_all, key_start, key_block)
    dist_base = key_start - first_row - query_count + 1 + seq_len
    window = lax.dynamic_slice_in_dim(buckets, dist_base, query_count + key_block - 1)
    onehot = (window[:, None] == jnp.arange(table.shape[0], dtype=jnp.int32)[None, :]).astype(
        jnp.float32
    )
    per_dist = jnp.dot(onehot, table, precision=HIGHEST).T
    bias_blk = shifted_bias(per_dist, query_count, key_block)
    raw_scores = (
        jnp.einsum("qhd,khd->hqk", queries, key_blk, preferred_element_type=jnp.float32) * scale
        + bias_blk
    )
    same_doc = (seg_query[:, None] == seg_keys[None, :])[None]
    weights_exp = jnp.exp(jnp.where(same_doc, raw_scores, MASKED))
    return (key_blk, value_blk, onehot, weights_exp)


def local(
    inputs,
    d_out,
    segments,
    buckets,
    w_query,
    w_key,
    w_value,
    w_out,
    w_gate,
    w_up,
    w_down,
    gain_attn,
    gain_ffn,
    bias_table,
):
    seq_count, row_count, model_width = inputs.shape
    seq_len = segments.shape[1]
    head_count = bias_table.shape[1]
    head_dim = model_width // head_count
    key_block = min(512, seq_len)
    block_count = seq_len // key_block
    token_count = seq_count * row_count
    scale = head_dim ** (-0.5)
    first_row = lax.axis_index("seq") * row_count
    blk_ids = jnp.arange(block_count, dtype=jnp.int32)
    gathered = (
        lax.all_gather(w_query, ("dp", "seq"), axis=0, tiled=True),
        lax.all_gather(w_key, ("dp", "seq"), axis=0, tiled=True),
        lax.all_gather(w_value, ("dp", "seq"), axis=0, tiled=True),
        lax.all_gather(w_out, ("dp", "seq"), axis=0, tiled=True),
        lax.all_gather(w_gate, ("dp", "seq"), axis=0, tiled=True),
        lax.all_gather(w_up, ("dp", "seq"), axis=0, tiled=True),
        lax.all_gather(w_down, ("dp", "seq"), axis=0, tiled=True),
    )
    full_query, full_key, full_value, full_out, full_gate, full_up, full_down = gathered
    flat_in = inputs.reshape(token_count, model_width).astype(jnp.float32)
    normed = norm_rows(flat_in, gain_attn).astype(jnp.bfloat16)
    queries = matmul(normed, full_query).astype(jnp.bfloat16)
    key_rows = (
        matmul(normed, full_key).astype(jnp.bfloat16).reshape(seq_count, row_count, model_width)
    )
    value_rows = (
        matmul(normed, full_value).astype(jnp.bfloat16).reshape(seq_count, row_count, model_width)
    )
    key_all, value_all = (
        lax.all_gather(key_rows, "seq", axis=1, tiled=True),
        lax.all_gather(value_rows, "seq", axis=1, tiled=True),
    )
    query_heads = queries.reshape(seq_count, row_count, head_count, head_dim)
    key_heads = key_all.reshape(seq_count, seq_len, head_count, head_dim)
    value_heads = value_all.reshape(seq_count, seq_len, head_count, head_dim)
    seg_queries = lax.dynamic_slice_in_dim(segments, first_row, row_count, axis=1)

    def attend(packed):
        query_one, key_one, value_one, seg_query, seg_all = packed

        def step(state_in, blk_index):
            totals, summed = state_in
            _, value_blk, _, weights_exp = block_parts(
                query_one,
                key_one,
                value_one,
                seg_query,
                seg_all,
                buckets,
                bias_table,
                first_row,
                blk_index,
                key_block,
            )
            summed = summed + jnp.einsum(
                "hqk,khd->qhd",
                weights_exp.astype(jnp.bfloat16),
                value_blk,
                preferred_element_type=jnp.float32,
            )
            totals = totals + jnp.sum(weights_exp, axis=-1)
            return ((totals, summed), None)

        start_state = (
            jnp.zeros((head_count, row_count), jnp.float32),
            jnp.zeros((row_count, head_count, head_dim), jnp.float32),
        )
        (totals, summed), _ = lax.scan(step, start_state, blk_ids)
        return (summed / jnp.transpose(totals)[:, :, None], totals)

    attn_f32, totals_all = lax.map(
        attend, (query_heads, key_heads, value_heads, seg_queries, segments)
    )
    attn_rows = attn_f32.reshape(token_count, model_width).astype(jnp.bfloat16)
    mixed_rows = flat_in + matmul(attn_rows, full_out)
    normed_two = norm_rows(mixed_rows, gain_ffn).astype(jnp.bfloat16)
    gate_act = matmul(normed_two, full_gate)
    up_act = matmul(normed_two, full_up)
    hidden = geglu(gate_act, up_act).astype(jnp.bfloat16)
    result = mixed_rows + matmul(hidden, full_down)
    output = result.astype(jnp.bfloat16).reshape(seq_count, row_count, model_width)
    back_weights = (
        lax.all_gather(w_query, ("dp", "seq"), axis=0, tiled=True),
        lax.all_gather(w_key, ("dp", "seq"), axis=0, tiled=True),
        lax.all_gather(w_value, ("dp", "seq"), axis=0, tiled=True),
        lax.all_gather(w_out, ("dp", "seq"), axis=0, tiled=True),
        lax.all_gather(w_gate, ("dp", "seq"), axis=0, tiled=True),
        lax.all_gather(w_up, ("dp", "seq"), axis=0, tiled=True),
        lax.all_gather(w_down, ("dp", "seq"), axis=0, tiled=True),
    )
    back_query, back_key, back_value, back_out, back_gate, back_up, back_down = back_weights
    d_res = d_out.reshape(token_count, model_width)
    grad_down = left_matmul(hidden, d_res)
    d_hidden = right_matmul(d_res, back_down)
    _, geglu_back = jax.vjp(geglu, gate_act, up_act)
    d_gate, d_up = geglu_back(d_hidden)
    d_gate = d_gate.astype(jnp.bfloat16)
    d_up = d_up.astype(jnp.bfloat16)
    grad_gate = left_matmul(normed_two, d_gate)
    grad_up = left_matmul(normed_two, d_up)
    d_normed_two = right_matmul(d_gate, back_gate) + right_matmul(d_up, back_up)
    _, norm_two_back = jax.vjp(norm_rows, mixed_rows, gain_ffn)
    d_mixed_norm, grad_gain_ffn = norm_two_back(d_normed_two)
    d_mixed = d_res.astype(jnp.float32) + d_mixed_norm
    d_branch = d_mixed.astype(jnp.bfloat16)
    grad_out = left_matmul(attn_rows, d_branch)
    d_attn = right_matmul(d_branch, back_out).reshape(seq_count, row_count, head_count, head_dim)
    totals_rows = jnp.transpose(totals_all, (0, 2, 1))
    d_unnorm_all = (d_attn / totals_rows[:, :, :, None]).astype(jnp.bfloat16)
    correction_all = -jnp.sum(d_attn * attn_f32, axis=-1) / totals_rows

    def attend_back(packed):
        query_one, key_one, value_one, seg_query, seg_all, d_unnorm, corr_rows = packed
        correction = jnp.transpose(corr_rows)

        def step(state_in, blk_index):
            d_query, d_table = state_in
            key_blk, value_blk, onehot, weights_exp = block_parts(
                query_one,
                key_one,
                value_one,
                seg_query,
                seg_all,
                buckets,
                bias_table,
                first_row,
                blk_index,
                key_block,
            )
            d_prob = jnp.einsum(
                "qhd,khd->hqk", d_unnorm, value_blk, preferred_element_type=jnp.float32
            )
            d_raw = (weights_exp * (d_prob + correction[:, :, None])).astype(jnp.bfloat16)
            d_query = (
                d_query
                + jnp.einsum("hqk,khd->qhd", d_raw, key_blk, preferred_element_type=jnp.float32)
                * scale
            )
            d_table = d_table + jnp.dot(
                diagonal_sums(d_raw.astype(jnp.float32)), onehot, precision=HIGHEST
            )
            d_key = (
                jnp.einsum("hqk,qhd->khd", d_raw, query_one, preferred_element_type=jnp.float32)
                * scale
            )
            d_value = jnp.einsum(
                "hqk,qhd->khd",
                weights_exp.astype(jnp.bfloat16),
                d_unnorm,
                preferred_element_type=jnp.float32,
            )
            return ((d_query, d_table), (d_key, d_value))

        start_state = (
            jnp.zeros((row_count, head_count, head_dim), jnp.float32),
            jnp.zeros((head_count, bias_table.shape[0]), jnp.float32),
        )
        (d_query, d_table), key_parts = lax.scan(step, start_state, blk_ids)
        d_key, d_value = key_parts
        return (
            d_query,
            d_table,
            d_key.reshape(seq_len, model_width),
            d_value.reshape(seq_len, model_width),
        )

    back_inputs = (
        query_heads,
        key_heads,
        value_heads,
        seg_queries,
        segments,
        d_unnorm_all,
        correction_all,
    )
    d_query_all, d_table_all, d_key_all, d_value_all = lax.map(attend_back, back_inputs)
    d_key_own, d_value_own = (
        lax.psum_scatter(
            d_key_all.astype(jnp.bfloat16), "seq", scatter_dimension=1, tiled=True
        ).astype(jnp.float32),
        lax.psum_scatter(
            d_value_all.astype(jnp.bfloat16), "seq", scatter_dimension=1, tiled=True
        ).astype(jnp.float32),
    )
    d_query_b = d_query_all.reshape(token_count, model_width).astype(jnp.bfloat16)
    d_key_b = d_key_own.reshape(token_count, model_width).astype(jnp.bfloat16)
    d_value_b = d_value_own.reshape(token_count, model_width).astype(jnp.bfloat16)
    grad_query = left_matmul(normed, d_query_b)
    grad_key = left_matmul(normed, d_key_b)
    grad_value = left_matmul(normed, d_value_b)
    d_normed = (
        right_matmul(d_query_b, back_query)
        + right_matmul(d_key_b, back_key)
        + right_matmul(d_value_b, back_value)
    )
    _, norm_one_back = jax.vjp(norm_rows, flat_in, gain_attn)
    d_in_norm, grad_gain_attn = norm_one_back(d_normed)
    d_inputs = (d_mixed + d_in_norm).reshape(seq_count, row_count, model_width)
    owned = (
        lax.psum_scatter(grad_query, ("dp", "seq"), scatter_dimension=0, tiled=True),
        lax.psum_scatter(grad_key, ("dp", "seq"), scatter_dimension=0, tiled=True),
        lax.psum_scatter(grad_value, ("dp", "seq"), scatter_dimension=0, tiled=True),
        lax.psum_scatter(grad_out, ("dp", "seq"), scatter_dimension=0, tiled=True),
        lax.psum_scatter(grad_gate, ("dp", "seq"), scatter_dimension=0, tiled=True),
        lax.psum_scatter(grad_up, ("dp", "seq"), scatter_dimension=0, tiled=True),
        lax.psum_scatter(grad_down, ("dp", "seq"), scatter_dimension=0, tiled=True),
    )
    table_local = jnp.transpose(jnp.sum(d_table_all, axis=0))
    gain_one, gain_two, table_grad = lax.psum(
        (grad_gain_attn, grad_gain_ffn, table_local), ("dp", "seq")
    )
    return (
        output,
        d_inputs,
        owned[0],
        owned[1],
        owned[2],
        owned[3],
        owned[4],
        owned[5],
        owned[6],
        gain_one,
        gain_two,
        table_grad,
    )


def pcall(body, outs, ins, scratch=(), grid=None, in_specs=None, out_specs=None, name=None):
    kwargs = {}
    if grid is not None:
        kwargs = dict(grid=grid, in_specs=in_specs, out_specs=out_specs)
    else:
        kwargs = dict(
            in_specs=[pl.BlockSpec(memory_space=pltpu.SMEM)]
            + [pl.BlockSpec(memory_space=pltpu.VMEM)] * (len(ins) - 1),
            out_specs=[pl.BlockSpec(memory_space=pltpu.VMEM)] * len(outs),
        )
    return pl.pallas_call(
        body,
        out_shape=outs,
        scratch_shapes=list(scratch),
        compiler_params=pltpu.CompilerParams(vmem_limit_bytes=VMEM_LIMIT),
        name=name,
        **kwargs,
    )(*ins)


def toeplitz(bucket_row, table_col, block):
    nb = table_col.shape[0]
    width = bucket_row.shape[1]
    ids = lax.broadcasted_iota(jnp.int32, (nb, width), 0)
    per_dist = jnp.sum(jnp.where(bucket_row == ids, table_col, 0.0), axis=0, keepdims=True)
    return pltpu.roll(
        jnp.broadcast_to(per_dist, (block, width)), 0, 1, stride=1, stride_axis=0
    )


def diagonals(acc):
    rows, width = acc.shape
    while rows > 8:
        rows //= 2
        acc = acc[:rows] + pltpu.roll(acc[rows:], width - rows, 1)
    row = lax.broadcasted_iota(jnp.int32, acc.shape, 0)
    for bit in (1, 2, 4):
        acc = jnp.where((row & bit) != 0, pltpu.roll(acc, width - bit, 1), acc)
    return jnp.sum(acc, axis=0, keepdims=True)


def attn_fwd_body(n, heads, head_dim, seq_len, rows):
    scale = head_dim ** (-0.5)

    def body(z_ref, *refs):
        x_refs = refs[:n]
        w_ref, gain_ref, segc_ref, segr_ref, bk_ref, tab_ref = refs[n : n + 6]
        h1_ref, qkv_ref, o_ref, l_ref = refs[n + 6 : n + 10]
        piece_refs = refs[n + 10 : 2 * n + 10]
        toe_ref = refs[2 * n + 10]
        z = z_ref[0]
        for k in range(n):
            start = pl.multiple_of(lax.rem(z + (n - k), n) * rows, rows)
            xv = x_refs[k][...].astype(jnp.float32)
            inv = lax.rsqrt(jnp.mean(xv * xv, axis=-1, keepdims=True) + EPS)
            h1 = (xv * inv * gain_ref[...]).astype(jnp.bfloat16)
            h1_ref[pl.ds(start, rows), :] = h1
            qkv = matmul(h1, w_ref[...]).astype(jnp.bfloat16)
            for i in range(3 * heads):
                qkv_ref[i, pl.ds(start, rows), :] = qkv[:, i * head_dim : (i + 1) * head_dim]
        for h in range(heads):
            toe_ref[h] = toeplitz(bk_ref[...], tab_ref[:, h : h + 1], rows)
        for k in range(n):
            start = pl.multiple_of(lax.rem(z + k, n) * rows, rows)
            seg_q = segc_ref[pl.ds(start, rows), :]
            outs = []
            for h in range(heads):
                s = right_matmul(qkv_ref[h, pl.ds(start, rows), :], qkv_ref[heads + h]) * scale
                col = pl.multiple_of(seq_len - start, rows)
                s = s + toe_ref[h, :, pl.ds(col, seq_len)]
                e = jnp.where(seg_q == segr_ref[...], jnp.exp(s), 0.0)
                l = jnp.sum(e, axis=-1, keepdims=True)
                o = matmul(e.astype(jnp.bfloat16), qkv_ref[2 * heads + h]) / l
                o_ref[h, pl.ds(start, rows), :] = o
                l_ref[h, pl.ds(start, rows), :] = l
                outs.append(o)
            piece_refs[k][...] = jnp.concatenate(outs, axis=1).astype(jnp.bfloat16)

    return body


def attn_bwd_body(n, heads, head_dim, seq_len, rows):
    scale = head_dim ** (-0.5)

    def body(z_ref, *refs):
        da_refs = refs[:n]
        h1_ref, qkv_ref, o_ref, l_ref, w_ref = refs[n : n + 5]
        segc_ref, segr_ref, bk_ref, tab_ref = refs[n + 5 : n + 9]
        gw_ref, gtab_ref = refs[n + 9 : n + 11]
        piece_refs = refs[n + 11 : 2 * n + 11]
        toe_ref, acc_ref, du_ref, dl_ref, dq_ref = refs[2 * n + 11 :]
        z = z_ref[0]
        for k in range(n):
            start = pl.multiple_of(lax.rem(z + (n - k), n) * rows, rows)
            da = da_refs[k][...].astype(jnp.float32)
            for h in range(heads):
                dah = da[:, h * head_dim : (h + 1) * head_dim]
                l = l_ref[h, pl.ds(start, rows), :]
                o = o_ref[h, pl.ds(start, rows), :]
                du_ref[h, pl.ds(start, rows), :] = (dah / l).astype(jnp.bfloat16)
                dl_ref[h, pl.ds(start, rows), :] = -jnp.sum(dah * o, axis=-1, keepdims=True) / l
        dq_all, dk_all, dv_all = [], [], []
        lane = lax.broadcasted_iota(jnp.int32, gtab_ref.shape, 1)
        gtab = jnp.zeros(gtab_ref.shape, jnp.float32)
        for h in range(heads):
            toe_ref[...] = toeplitz(bk_ref[...], tab_ref[:, h : h + 1], rows)
            acc_ref[...] = jnp.zeros_like(acc_ref)
            dk = jnp.zeros((head_dim, seq_len), jnp.float32)
            dv = jnp.zeros((head_dim, seq_len), jnp.float32)
            for i in range(n):
                block = pl.ds(i * rows, rows)
                q = qkv_ref[h, block, :]
                du = du_ref[h, block, :]
                cols = pl.ds(seq_len - i * rows, seq_len)
                s = right_matmul(q, qkv_ref[heads + h]) * scale + toe_ref[:, cols]
                e = jnp.where(segc_ref[block, :] == segr_ref[...], jnp.exp(s), 0.0)
                dp = right_matmul(du, qkv_ref[2 * heads + h]) + dl_ref[h, block, :]
                ds = (e * dp).astype(jnp.bfloat16)
                acc_ref[:, cols] += ds.astype(jnp.float32)
                dq = matmul(ds, qkv_ref[heads + h]) * scale
                dq_ref[block, h * head_dim : (h + 1) * head_dim] = dq.astype(jnp.bfloat16)
                dk = dk + left_matmul(q, ds)
                dv = dv + left_matmul(du, e.astype(jnp.bfloat16))
            first = (heads + h) * head_dim
            dq_ref[:, first : first + head_dim] = (dk * scale).T.astype(jnp.bfloat16)
            first = (2 * heads + h) * head_dim
            dq_ref[:, first : first + head_dim] = dv.T.astype(jnp.bfloat16)
            sums = diagonals(acc_ref[...])
            ids = lax.broadcasted_iota(jnp.int32, (gtab_ref.shape[0], sums.shape[1]), 0)
            col = jnp.sum(jnp.where(bk_ref[...] == ids, sums, 0.0), axis=1, keepdims=True)
            gtab = gtab + jnp.where(lane == h, col, 0.0)
        gtab_ref[...] = gtab
        gw_ref[...] = left_matmul(h1_ref[...], dq_ref[...]).astype(jnp.bfloat16)
        for k in range(n):
            start = pl.multiple_of(lax.rem(z + k, n) * rows, rows)
            part = right_matmul(dq_ref[pl.ds(start, rows), :], w_ref[...])
            piece_refs[k][...] = part.astype(jnp.bfloat16)

    return body


def mid_body(n, rows, width, ff, block, row_w, row_d):
    steps = ff // block
    per = block // row_d
    groups = -(-row_d // row_w)
    piece_w = width // n
    off_out = groups * width
    off_gate = off_out + width
    off_up = off_gate + ff

    def body(z_ref, *refs):
        p_refs = refs[:n]
        x_ref, c_ref, wd_ref, wo_ref, wg_ref, wu_ref, gain_ref = refs[n : n + 7]
        out_ref, dx1_ref = refs[n + 7 : n + 9]
        da_refs = refs[n + 9 : 2 * n + 9]
        gg_ref, grads_ref = refs[2 * n + 9 : 2 * n + 11]
        x1_s, h2_s, y_s, dh_s, gd_s, go_s, gg_s, gu_s, sems = refs[2 * n + 11 :]
        z = z_ref[0]
        j = pl.program_id(0)

        @pl.when(j == 0)
        def _():
            x1 = x_ref[...].astype(jnp.float32)
            for k in range(n):
                first = pl.multiple_of(lax.rem(z + (n - k), n) * piece_w, piece_w)
                x1 = x1 + matmul(p_refs[k][...], wo_ref[pl.ds(first, piece_w), :])
            x1_s[...] = x1
            inv = lax.rsqrt(jnp.mean(x1 * x1, axis=-1, keepdims=True) + EPS)
            h2_s[...] = (x1 * inv * gain_ref[...]).astype(jnp.bfloat16)
            y_s[...] = jnp.zeros_like(y_s)
            dh_s[...] = jnp.zeros_like(dh_s)

        h2 = h2_s[...]
        c = c_ref[...]
        wg = wg_ref[...]
        wu = wu_ref[...]
        packed = wd_ref[...].astype(jnp.float32)
        parts = []
        for r in range(per):
            for g in range(groups):
                size = min(row_w, row_d - g * row_w)
                parts.append(packed[r * row_w : r * row_w + size, g * width : (g + 1) * width])
        wd = jnp.concatenate(parts, axis=0).astype(jnp.bfloat16)
        gate = matmul(h2, wg)
        up = matmul(h2, wu)
        t = jnp.tanh(GELU_A * (gate + GELU_B * gate * gate * gate))
        gelu = 0.5 * gate * (1.0 + t)
        slope = 0.5 * (1.0 + t) + 0.5 * gate * (1.0 - t * t) * (
            GELU_A * (1.0 + 3.0 * GELU_B * gate * gate)
        )
        hidden = (gelu * up).astype(jnp.bfloat16)
        y_s[...] += matmul(hidden, wd)
        dz = right_matmul(c, wd)
        dgate = (dz * up * slope).astype(jnp.bfloat16)
        dup = (dz * gelu).astype(jnp.bfloat16)
        dh_s[...] += right_matmul(dgate, wg) + right_matmul(dup, wu)
        gdown = left_matmul(hidden, c)
        rows_out = []
        for r in range(per):
            cols_out = []
            for g in range(groups):
                size = min(row_w, row_d - g * row_w)
                first = r * row_d + g * row_w
                piece = gdown[first : first + size]
                if size < row_w:
                    piece = jnp.concatenate(
                        [piece, jnp.zeros((row_w - size, width), jnp.float32)], axis=0
                    )
                cols_out.append(piece)
            rows_out.append(jnp.concatenate(cols_out, axis=1))
        gd_s[j] = jnp.concatenate(rows_out, axis=0).astype(jnp.bfloat16)
        gg_s[j] = left_matmul(h2, dgate).astype(jnp.bfloat16)
        gu_s[j] = left_matmul(h2, dup).astype(jnp.bfloat16)

        def copies(i):
            high = per * row_w
            return (
                pltpu.make_async_copy(
                    gd_s.at[i],
                    grads_ref.at[pl.ds(i * high, high), pl.ds(0, off_out)],
                    sems.at[0, i],
                ),
                pltpu.make_async_copy(
                    gg_s.at[i],
                    grads_ref.at[:, pl.ds(off_gate + i * block, block)],
                    sems.at[1, i],
                ),
                pltpu.make_async_copy(
                    gu_s.at[i],
                    grads_ref.at[:, pl.ds(off_up + i * block, block)],
                    sems.at[2, i],
                ),
            )

        for copy in copies(j):
            copy.start()

        @pl.when(j == steps - 1)
        def _():
            x1 = x1_s[...]
            out_ref[...] = (x1 + y_s[...]).astype(jnp.bfloat16)
            inv = lax.rsqrt(jnp.mean(x1 * x1, axis=-1, keepdims=True) + EPS)
            hat = x1 * inv
            dh = dh_s[...]
            gg_ref[...] = jnp.sum(dh * hat, axis=0, keepdims=True)
            scaled = dh * gain_ref[...]
            dxn = inv * (scaled - hat * jnp.mean(scaled * hat, axis=-1, keepdims=True))
            dx1 = c_ref[...].astype(jnp.float32) + dxn
            dx1_ref[...] = dx1
            dy = dx1.astype(jnp.bfloat16)
            for k in range(n):
                first = pl.multiple_of(lax.rem(z + k, n) * piece_w, piece_w)
                da = right_matmul(dy, wo_ref[pl.ds(first, piece_w), :])
                da_refs[k][...] = da.astype(jnp.bfloat16)
            for k in range(n):
                first = pl.multiple_of(lax.rem(z + (n - k), n) * piece_w, piece_w)
                go_s[pl.ds(first, piece_w), :] = left_matmul(p_refs[k][...], dy).astype(
                    jnp.bfloat16
                )
            last = pltpu.make_async_copy(
                go_s, grads_ref.at[:, pl.ds(off_out, width)], sems.at[3, 0]
            )
            last.start()
            for i in range(steps):
                for copy in copies(i):
                    copy.wait()
            last.wait()

    return body


def final_body(n):
    def body(z_ref, *refs):
        part_refs = refs[:n]
        x_ref, dx1_ref, gain_ref, din_ref, gg_ref = refs[n:]
        dh = part_refs[0][...].astype(jnp.float32)
        for k in range(1, n):
            dh = dh + part_refs[k][...].astype(jnp.float32)
        xv = x_ref[...].astype(jnp.float32)
        inv = lax.rsqrt(jnp.mean(xv * xv, axis=-1, keepdims=True) + EPS)
        hat = xv * inv
        gg_ref[...] = jnp.sum(dh * hat, axis=0, keepdims=True)
        scaled = dh * gain_ref[...]
        dxn = inv * (scaled - hat * jnp.mean(scaled * hat, axis=-1, keepdims=True))
        din_ref[...] = dx1_ref[...] + dxn

    return body


def shifts(pieces, n):
    got = [pieces[0]]
    for k in range(1, n):
        got.append(lax.ppermute(pieces[k], "seq", [(i, (i + k) % n) for i in range(n)]))
    return got


def fast(
    inputs,
    d_out,
    segments,
    buckets,
    w_query,
    w_key,
    w_value,
    w_out,
    w_gate,
    w_up,
    w_down,
    gain_attn,
    gain_ffn,
    bias_table,
):
    bf16, f32 = jnp.bfloat16, jnp.float32
    n = lax.axis_size("seq")
    both = ("dp", "seq")
    _, rows, width = inputs.shape
    seq_len = segments.shape[1]
    nb, head_count = bias_table.shape
    head_dim = width // head_count
    heads = head_count // n
    piece_w = width // n
    ff = w_gate.shape[1]
    row_w, row_d = w_query.shape[0], w_down.shape[0]
    groups = -(-row_d // row_w)
    z = lax.axis_index("seq")
    z_arr = jnp.reshape(z, (1,)).astype(jnp.int32)
    sds = jax.ShapeDtypeStruct

    flat_in = inputs.reshape(rows, width)
    flat_c = d_out.reshape(rows, width)
    x_all = shifts([flat_in] * n, n)

    padded = jnp.concatenate([w_down, jnp.zeros((groups * row_w - row_d, width), bf16)], axis=0)
    down_cols = [padded[g * row_w : (g + 1) * row_w] for g in range(groups)]
    packed = jnp.concatenate(down_cols + [w_out, w_gate, w_up], axis=1)
    full = lax.all_gather(packed, both, axis=0, tiled=True)

    three = []
    for g in range(n):
        cut = slice(g * piece_w, (g + 1) * piece_w)
        three += [w_query[:, cut], w_key[:, cut], w_value[:, cut]]
    own_cols = lax.all_to_all(
        jnp.concatenate(three, axis=1), "seq", split_axis=1, concat_axis=0, tiled=True
    )
    w_qkv = lax.all_gather(own_cols, "dp", axis=0, tiled=True)

    seg_row = segments.reshape(1, seq_len)
    seg_col = segments.reshape(seq_len, 1)
    bucket_row = buckets.reshape(1, 2 * seq_len)
    table = lax.dynamic_slice_in_dim(bias_table, z * heads, heads, axis=1)
    gain_one = gain_attn.reshape(1, width)
    gain_two = gain_ffn.reshape(1, width)

    outs = pcall(
        attn_fwd_body(n, heads, head_dim, seq_len, rows),
        [
            sds((seq_len, width), bf16),
            sds((3 * heads, seq_len, head_dim), bf16),
            sds((heads, seq_len, head_dim), f32),
            sds((heads, seq_len, 1), f32),
        ]
        + [sds((rows, piece_w), bf16)] * n,
        [z_arr, *x_all, w_qkv, gain_one, seg_col, seg_row, bucket_row, table],
        [pltpu.VMEM((heads, rows, 2 * seq_len), f32)],
        name="attn_fwd",
    )
    h1, qkv, o_heads, l_heads = outs[:4]
    attn = shifts(outs[4:], n)

    block = 256
    steps = ff // block
    per = block // row_d
    const = lambda shape: pl.BlockSpec(shape, lambda j: (0,) * len(shape))
    total = (groups + 1) * width + 2 * ff
    gate_first = (groups + 1) * width // block
    outs = pcall(
        mid_body(n, rows, width, ff, block, row_w, row_d),
        [sds((rows, width), bf16), sds((rows, width), f32)]
        + [sds((rows, piece_w), bf16)] * n
        + [sds((1, width), f32), sds((width, total), bf16)],
        [z_arr, *attn, flat_in, flat_c, full, full, full, full, gain_two],
        [
            pltpu.VMEM((rows, width), f32),
            pltpu.VMEM((rows, width), bf16),
            pltpu.VMEM((rows, width), f32),
            pltpu.VMEM((rows, width), f32),
            pltpu.VMEM((steps, per * row_w, groups * width), bf16),
            pltpu.VMEM((width, width), bf16),
            pltpu.VMEM((steps, width, block), bf16),
            pltpu.VMEM((steps, width, block), bf16),
            pltpu.SemaphoreType.DMA((4, steps)),
        ],
        grid=(steps,),
        in_specs=[pl.BlockSpec(memory_space=pltpu.SMEM)]
        + [const((rows, piece_w))] * n
        + [
            const((rows, width)),
            const((rows, width)),
            pl.BlockSpec((per * row_w, groups * width), lambda j: (j, 0)),
            pl.BlockSpec((width, width), lambda j: (0, groups)),
            pl.BlockSpec((width, block), lambda j: (0, gate_first + j)),
            pl.BlockSpec((width, block), lambda j: (0, gate_first + steps + j)),
            const((1, width)),
        ],
        out_specs=[const((rows, width)), const((rows, width))]
        + [const((rows, piece_w))] * n
        + [const((1, width)), pl.BlockSpec(memory_space=pl.ANY)],
        name="mid",
    )
    output, dx1 = outs[:2]
    d_attn = shifts(outs[2 : n + 2], n)
    gain_two_grad, grads = outs[n + 2 :]
    reduced = lax.psum_scatter(grads, both, scatter_dimension=0, tiled=True).astype(f32)

    outs = pcall(
        attn_bwd_body(n, heads, head_dim, seq_len, rows),
        [sds((width, 3 * piece_w), bf16), sds((nb, 128), f32)] + [sds((rows, width), bf16)] * n,
        [z_arr, *d_attn, h1, qkv, o_heads, l_heads, w_qkv, seg_col, seg_row, bucket_row, table],
        [
            pltpu.VMEM((rows, 2 * seq_len), f32),
            pltpu.VMEM((rows, 2 * seq_len), f32),
            pltpu.VMEM((heads, seq_len, head_dim), bf16),
            pltpu.VMEM((heads, seq_len, 1), f32),
            pltpu.VMEM((seq_len, 3 * piece_w), bf16),
        ],
        name="attn_bwd",
    )
    grad_qkv, table_part = outs[:2]
    d_normed = shifts(outs[2:], n)

    dps = lax.axis_size("dp")
    spread = lax.all_to_all(grad_qkv, "dp", split_axis=0, concat_axis=0, tiled=True)
    summed = jnp.sum(spread.reshape(dps, width // dps, 3 * piece_w).astype(f32), axis=0)
    owned = lax.all_to_all(summed, "seq", split_axis=0, concat_axis=1, tiled=True)
    owned = owned.reshape(row_w, n, 3, piece_w)
    grad_query, grad_key, grad_value = (owned[:, :, i].reshape(row_w, width) for i in range(3))

    d_inputs, gain_one_grad = pcall(
        final_body(n),
        [sds((rows, width), f32), sds((1, width), f32)],
        [z_arr, *d_normed, flat_in, dx1, gain_one],
        name="final",
    )
    table_own = lax.dynamic_update_slice_in_dim(
        jnp.zeros((nb, head_count), f32), table_part[:, :heads], z * heads, axis=1
    )
    gain_one_sum, gain_two_sum, table_sum = lax.psum(
        (gain_one_grad.reshape(width), gain_two_grad.reshape(width), table_own), both
    )

    base = groups * width
    down_parts = []
    for g in range(groups):
        size = min(row_w, row_d - g * row_w)
        down_parts.append(reduced[:size, g * width : (g + 1) * width])
    grad_down = jnp.concatenate(down_parts, axis=0)
    return (
        output.reshape(inputs.shape),
        d_inputs.reshape(inputs.shape),
        grad_query,
        grad_key,
        grad_value,
        reduced[:, base : base + width],
        reduced[:, base + width : base + width + ff],
        reduced[:, base + width + ff :],
        grad_down,
        gain_one_sum,
        gain_two_sum,
        table_sum,
    )


def pick(
    inputs,
    d_out,
    segments,
    buckets,
    w_query,
    w_key,
    w_value,
    w_out,
    w_gate,
    w_up,
    w_down,
    gain_attn,
    gain_ffn,
    bias_table,
):
    n = lax.axis_size("seq")
    seqs, rows, width = inputs.shape
    row_w, row_d, ff = w_query.shape[0], w_down.shape[0], w_gate.shape[1]
    head_count = bias_table.shape[1]
    fits = (
        seqs == 1
        and head_count % n == 0
        and rows == 256
        and width % 256 == 0
        and width // head_count == 64
        and ff % 256 == 0
        and row_w % 8 == 0
        and row_d % 8 == 0
        and 256 % row_d == 0
        and (256 // row_d) * row_w * (ff // 256) == width
    )
    plan = fast if fits else local
    return plan(
        inputs,
        d_out,
        segments,
        buckets,
        w_query,
        w_key,
        w_value,
        w_out,
        w_gate,
        w_up,
        w_down,
        gain_attn,
        gain_ffn,
        bias_table,
    )


def solution(mesh):
    return jax.shard_map(
        pick,
        mesh=mesh,
        in_specs=(
            P("dp", "seq", None),
            P("dp", "seq", None),
            P("dp", None),
            P(),
            P(("dp", "seq"), None),
            P(("dp", "seq"), None),
            P(("dp", "seq"), None),
            P(("dp", "seq"), None),
            P(("dp", "seq"), None),
            P(("dp", "seq"), None),
            P(("dp", "seq"), None),
            P(),
            P(),
            P(),
        ),
        out_specs=(
            P("dp", "seq", None),
            P("dp", "seq", None),
            P(("dp", "seq"), None),
            P(("dp", "seq"), None),
            P(("dp", "seq"), None),
            P(("dp", "seq"), None),
            P(("dp", "seq"), None),
            P(("dp", "seq"), None),
            P(("dp", "seq"), None),
            P(),
            P(),
            P(),
        ),
        check_vma=False,
    )
```

```python
import jax
import jax.numpy as jnp
from jax import lax
from jax.experimental import pallas as pl
from jax.experimental.pallas import tpu as pltpu
from jax.sharding import PartitionSpec as P

EPS = 1e-06
MASKED = -1000000000.0
HIGHEST = lax.Precision.HIGHEST
GELU_A = 0.7978845608028654
GELU_B = 0.044715
VMEM_LIMIT = 56 * 1024 * 1024


def norm_rows(values, gain):
    return values * lax.rsqrt(jnp.mean(values * values, axis=-1, keepdims=True) + EPS) * gain


def geglu(gate_act, up_act):
    return jax.nn.gelu(gate_act, approximate=True) * up_act


def matmul(left, right):
    return jnp.dot(left, right, preferred_element_type=jnp.float32)


def left_matmul(left, right):
    return lax.dot_general(
        left, right, (((0,), (0,)), ((), ())), preferred_element_type=jnp.float32
    )


def right_matmul(left, right):
    return lax.dot_general(
        left, right, (((1,), (1,)), ((), ())), preferred_element_type=jnp.float32
    )


def shifted_bias(per_dist, query_count, key_count):
    head_count, width = per_dist.shape
    flipped = per_dist[:, ::-1]
    tiled = jnp.tile(flipped, (1, query_count + 1))[:, : query_count * (width + 1)]
    rows = tiled.reshape(head_count, query_count, width + 1)[:, :, :key_count]
    return rows[:, :, ::-1]


def diagonal_sums(scores):
    head_count, row_count, col_count = scores.shape
    row_width = row_count + col_count
    padded = jnp.concatenate(
        [jnp.zeros((head_count, row_count, row_count), scores.dtype), scores], axis=2
    )
    flat_rows = jnp.concatenate(
        [
            padded.reshape(head_count, row_count * row_width),
            jnp.zeros((head_count, row_count), scores.dtype),
        ],
        axis=1,
    )
    skewed = flat_rows.reshape(head_count, row_count, row_width + 1)
    return jnp.sum(skewed, axis=1)[:, 1:row_width]


def block_parts(
    queries,
    key_heads,
    value_heads,
    seg_query,
    seg_all,
    buckets,
    table,
    first_row,
    blk_index,
    key_block,
):
    query_count = queries.shape[0]
    seq_len = key_heads.shape[0]
    scale = queries.shape[-1] ** (-0.5)
    key_start = blk_index * key_block
    key_blk = lax.dynamic_slice_in_dim(key_heads, key_start, key_block)
    value_blk = lax.dynamic_slice_in_dim(value_heads, key_start, key_block)
    seg_keys = lax.dynamic_slice_in_dim(seg_all, key_start, key_block)
    dist_base = key_start - first_row - query_count + 1 + seq_len
    window = lax.dynamic_slice_in_dim(buckets, dist_base, query_count + key_block - 1)
    onehot = (window[:, None] == jnp.arange(table.shape[0], dtype=jnp.int32)[None, :]).astype(
        jnp.float32
    )
    per_dist = jnp.dot(onehot, table, precision=HIGHEST).T
    bias_blk = shifted_bias(per_dist, query_count, key_block)
    raw_scores = (
        jnp.einsum("qhd,khd->hqk", queries, key_blk, preferred_element_type=jnp.float32) * scale
        + bias_blk
    )
    same_doc = (seg_query[:, None] == seg_keys[None, :])[None]
    weights_exp = jnp.exp(jnp.where(same_doc, raw_scores, MASKED))
    return (key_blk, value_blk, onehot, weights_exp)


def local(
    inputs,
    d_out,
    segments,
    buckets,
    w_query,
    w_key,
    w_value,
    w_out,
    w_gate,
    w_up,
    w_down,
    gain_attn,
    gain_ffn,
    bias_table,
):
    seq_count, row_count, model_width = inputs.shape
    seq_len = segments.shape[1]
    head_count = bias_table.shape[1]
    head_dim = model_width // head_count
    key_block = min(512, seq_len)
    block_count = seq_len // key_block
    token_count = seq_count * row_count
    scale = head_dim ** (-0.5)
    first_row = lax.axis_index("seq") * row_count
    blk_ids = jnp.arange(block_count, dtype=jnp.int32)
    gathered = (
        lax.all_gather(w_query, ("dp", "seq"), axis=0, tiled=True),
        lax.all_gather(w_key, ("dp", "seq"), axis=0, tiled=True),
        lax.all_gather(w_value, ("dp", "seq"), axis=0, tiled=True),
        lax.all_gather(w_out, ("dp", "seq"), axis=0, tiled=True),
        lax.all_gather(w_gate, ("dp", "seq"), axis=0, tiled=True),
        lax.all_gather(w_up, ("dp", "seq"), axis=0, tiled=True),
        lax.all_gather(w_down, ("dp", "seq"), axis=0, tiled=True),
    )
    full_query, full_key, full_value, full_out, full_gate, full_up, full_down = gathered
    flat_in = inputs.reshape(token_count, model_width).astype(jnp.float32)
    normed = norm_rows(flat_in, gain_attn).astype(jnp.bfloat16)
    queries = matmul(normed, full_query).astype(jnp.bfloat16)
    key_rows = (
        matmul(normed, full_key).astype(jnp.bfloat16).reshape(seq_count, row_count, model_width)
    )
    value_rows = (
        matmul(normed, full_value).astype(jnp.bfloat16).reshape(seq_count, row_count, model_width)
    )
    key_all, value_all = (
        lax.all_gather(key_rows, "seq", axis=1, tiled=True),
        lax.all_gather(value_rows, "seq", axis=1, tiled=True),
    )
    query_heads = queries.reshape(seq_count, row_count, head_count, head_dim)
    key_heads = key_all.reshape(seq_count, seq_len, head_count, head_dim)
    value_heads = value_all.reshape(seq_count, seq_len, head_count, head_dim)
    seg_queries = lax.dynamic_slice_in_dim(segments, first_row, row_count, axis=1)

    def attend(packed):
        query_one, key_one, value_one, seg_query, seg_all = packed

        def step(state_in, blk_index):
            totals, summed = state_in
            _, value_blk, _, weights_exp = block_parts(
                query_one,
                key_one,
                value_one,
                seg_query,
                seg_all,
                buckets,
                bias_table,
                first_row,
                blk_index,
                key_block,
            )
            summed = summed + jnp.einsum(
                "hqk,khd->qhd",
                weights_exp.astype(jnp.bfloat16),
                value_blk,
                preferred_element_type=jnp.float32,
            )
            totals = totals + jnp.sum(weights_exp, axis=-1)
            return ((totals, summed), None)

        start_state = (
            jnp.zeros((head_count, row_count), jnp.float32),
            jnp.zeros((row_count, head_count, head_dim), jnp.float32),
        )
        (totals, summed), _ = lax.scan(step, start_state, blk_ids)
        return (summed / jnp.transpose(totals)[:, :, None], totals)

    attn_f32, totals_all = lax.map(
        attend, (query_heads, key_heads, value_heads, seg_queries, segments)
    )
    attn_rows = attn_f32.reshape(token_count, model_width).astype(jnp.bfloat16)
    mixed_rows = flat_in + matmul(attn_rows, full_out)
    normed_two = norm_rows(mixed_rows, gain_ffn).astype(jnp.bfloat16)
    gate_act = matmul(normed_two, full_gate)
    up_act = matmul(normed_two, full_up)
    hidden = geglu(gate_act, up_act).astype(jnp.bfloat16)
    result = mixed_rows + matmul(hidden, full_down)
    output = result.astype(jnp.bfloat16).reshape(seq_count, row_count, model_width)
    back_weights = (
        lax.all_gather(w_query, ("dp", "seq"), axis=0, tiled=True),
        lax.all_gather(w_key, ("dp", "seq"), axis=0, tiled=True),
        lax.all_gather(w_value, ("dp", "seq"), axis=0, tiled=True),
        lax.all_gather(w_out, ("dp", "seq"), axis=0, tiled=True),
        lax.all_gather(w_gate, ("dp", "seq"), axis=0, tiled=True),
        lax.all_gather(w_up, ("dp", "seq"), axis=0, tiled=True),
        lax.all_gather(w_down, ("dp", "seq"), axis=0, tiled=True),
    )
    back_query, back_key, back_value, back_out, back_gate, back_up, back_down = back_weights
    d_res = d_out.reshape(token_count, model_width)
    grad_down = left_matmul(hidden, d_res)
    d_hidden = right_matmul(d_res, back_down)
    _, geglu_back = jax.vjp(geglu, gate_act, up_act)
    d_gate, d_up = geglu_back(d_hidden)
    d_gate = d_gate.astype(jnp.bfloat16)
    d_up = d_up.astype(jnp.bfloat16)
    grad_gate = left_matmul(normed_two, d_gate)
    grad_up = left_matmul(normed_two, d_up)
    d_normed_two = right_matmul(d_gate, back_gate) + right_matmul(d_up, back_up)
    _, norm_two_back = jax.vjp(norm_rows, mixed_rows, gain_ffn)
    d_mixed_norm, grad_gain_ffn = norm_two_back(d_normed_two)
    d_mixed = d_res.astype(jnp.float32) + d_mixed_norm
    d_branch = d_mixed.astype(jnp.bfloat16)
    grad_out = left_matmul(attn_rows, d_branch)
    d_attn = right_matmul(d_branch, back_out).reshape(seq_count, row_count, head_count, head_dim)
    totals_rows = jnp.transpose(totals_all, (0, 2, 1))
    d_unnorm_all = (d_attn / totals_rows[:, :, :, None]).astype(jnp.bfloat16)
    correction_all = -jnp.sum(d_attn * attn_f32, axis=-1) / totals_rows

    def attend_back(packed):
        query_one, key_one, value_one, seg_query, seg_all, d_unnorm, corr_rows = packed
        correction = jnp.transpose(corr_rows)

        def step(state_in, blk_index):
            d_query, d_table = state_in
            key_blk, value_blk, onehot, weights_exp = block_parts(
                query_one,
                key_one,
                value_one,
                seg_query,
                seg_all,
                buckets,
                bias_table,
                first_row,
                blk_index,
                key_block,
            )
            d_prob = jnp.einsum(
                "qhd,khd->hqk", d_unnorm, value_blk, preferred_element_type=jnp.float32
            )
            d_raw = (weights_exp * (d_prob + correction[:, :, None])).astype(jnp.bfloat16)
            d_query = (
                d_query
                + jnp.einsum("hqk,khd->qhd", d_raw, key_blk, preferred_element_type=jnp.float32)
                * scale
            )
            d_table = d_table + jnp.dot(
                diagonal_sums(d_raw.astype(jnp.float32)), onehot, precision=HIGHEST
            )
            d_key = (
                jnp.einsum("hqk,qhd->khd", d_raw, query_one, preferred_element_type=jnp.float32)
                * scale
            )
            d_value = jnp.einsum(
                "hqk,qhd->khd",
                weights_exp.astype(jnp.bfloat16),
                d_unnorm,
                preferred_element_type=jnp.float32,
            )
            return ((d_query, d_table), (d_key, d_value))

        start_state = (
            jnp.zeros((row_count, head_count, head_dim), jnp.float32),
            jnp.zeros((head_count, bias_table.shape[0]), jnp.float32),
        )
        (d_query, d_table), key_parts = lax.scan(step, start_state, blk_ids)
        d_key, d_value = key_parts
        return (
            d_query,
            d_table,
            d_key.reshape(seq_len, model_width),
            d_value.reshape(seq_len, model_width),
        )

    back_inputs = (
        query_heads,
        key_heads,
        value_heads,
        seg_queries,
        segments,
        d_unnorm_all,
        correction_all,
    )
    d_query_all, d_table_all, d_key_all, d_value_all = lax.map(attend_back, back_inputs)
    d_key_own, d_value_own = (
        lax.psum_scatter(
            d_key_all.astype(jnp.bfloat16), "seq", scatter_dimension=1, tiled=True
        ).astype(jnp.float32),
        lax.psum_scatter(
            d_value_all.astype(jnp.bfloat16), "seq", scatter_dimension=1, tiled=True
        ).astype(jnp.float32),
    )
    d_query_b = d_query_all.reshape(token_count, model_width).astype(jnp.bfloat16)
    d_key_b = d_key_own.reshape(token_count, model_width).astype(jnp.bfloat16)
    d_value_b = d_value_own.reshape(token_count, model_width).astype(jnp.bfloat16)
    grad_query = left_matmul(normed, d_query_b)
    grad_key = left_matmul(normed, d_key_b)
    grad_value = left_matmul(normed, d_value_b)
    d_normed = (
        right_matmul(d_query_b, back_query)
        + right_matmul(d_key_b, back_key)
        + right_matmul(d_value_b, back_value)
    )
    _, norm_one_back = jax.vjp(norm_rows, flat_in, gain_attn)
    d_in_norm, grad_gain_attn = norm_one_back(d_normed)
    d_inputs = (d_mixed + d_in_norm).reshape(seq_count, row_count, model_width)
    owned = (
        lax.psum_scatter(grad_query, ("dp", "seq"), scatter_dimension=0, tiled=True),
        lax.psum_scatter(grad_key, ("dp", "seq"), scatter_dimension=0, tiled=True),
        lax.psum_scatter(grad_value, ("dp", "seq"), scatter_dimension=0, tiled=True),
        lax.psum_scatter(grad_out, ("dp", "seq"), scatter_dimension=0, tiled=True),
        lax.psum_scatter(grad_gate, ("dp", "seq"), scatter_dimension=0, tiled=True),
        lax.psum_scatter(grad_up, ("dp", "seq"), scatter_dimension=0, tiled=True),
        lax.psum_scatter(grad_down, ("dp", "seq"), scatter_dimension=0, tiled=True),
    )
    table_local = jnp.transpose(jnp.sum(d_table_all, axis=0))
    gain_one, gain_two, table_grad = lax.psum(
        (grad_gain_attn, grad_gain_ffn, table_local), ("dp", "seq")
    )
    return (
        output,
        d_inputs,
        owned[0],
        owned[1],
        owned[2],
        owned[3],
        owned[4],
        owned[5],
        owned[6],
        gain_one,
        gain_two,
        table_grad,
    )


def pcall(body, outs, ins, scratch=(), grid=None, in_specs=None, out_specs=None, name=None):
    kwargs = {}
    if grid is not None:
        kwargs = dict(grid=grid, in_specs=in_specs, out_specs=out_specs)
    else:
        kwargs = dict(
            in_specs=[pl.BlockSpec(memory_space=pltpu.SMEM)]
            + [pl.BlockSpec(memory_space=pltpu.VMEM)] * (len(ins) - 1),
            out_specs=[pl.BlockSpec(memory_space=pltpu.VMEM)] * len(outs),
        )
    return pl.pallas_call(
        body,
        out_shape=outs,
        scratch_shapes=list(scratch),
        compiler_params=pltpu.CompilerParams(vmem_limit_bytes=VMEM_LIMIT),
        name=name,
        **kwargs,
    )(*ins)


def toeplitz(bucket_row, table_col, block):
    nb = table_col.shape[0]
    width = bucket_row.shape[1]
    ids = lax.broadcasted_iota(jnp.int32, (nb, width), 0)
    per_dist = jnp.sum(jnp.where(bucket_row == ids, table_col, 0.0), axis=0, keepdims=True)
    return pltpu.roll(
        jnp.broadcast_to(per_dist, (block, width)), 0, 1, stride=1, stride_axis=0
    )


def diagonals(acc):
    rows, width = acc.shape
    while rows > 8:
        rows //= 2
        acc = acc[:rows] + pltpu.roll(acc[rows:], width - rows, 1)
    row = lax.broadcasted_iota(jnp.int32, acc.shape, 0)
    for bit in (1, 2, 4):
        acc = jnp.where((row & bit) != 0, pltpu.roll(acc, width - bit, 1), acc)
    return jnp.sum(acc, axis=0, keepdims=True)


def attn_fwd_body(n, heads, head_dim, seq_len, rows):
    scale = head_dim ** (-0.5)

    def body(z_ref, *refs):
        x_refs = refs[:n]
        w_ref, gain_ref, segc_ref, segr_ref, bk_ref, tab_ref = refs[n : n + 6]
        h1_ref, qkv_ref, o_ref, l_ref = refs[n + 6 : n + 10]
        piece_refs = refs[n + 10 : 2 * n + 10]
        toe_ref = refs[2 * n + 10]
        z = z_ref[0]
        for k in range(n):
            start = pl.multiple_of(lax.rem(z + (n - k), n) * rows, rows)
            xv = x_refs[k][...].astype(jnp.float32)
            inv = lax.rsqrt(jnp.mean(xv * xv, axis=-1, keepdims=True) + EPS)
            h1 = (xv * inv * gain_ref[...]).astype(jnp.bfloat16)
            h1_ref[pl.ds(start, rows), :] = h1
            qkv = matmul(h1, w_ref[...]).astype(jnp.bfloat16)
            for i in range(3 * heads):
                qkv_ref[i, pl.ds(start, rows), :] = qkv[:, i * head_dim : (i + 1) * head_dim]
        for h in range(heads):
            toe_ref[h] = toeplitz(bk_ref[...], tab_ref[:, h : h + 1], rows)
        for k in range(n):
            start = pl.multiple_of(lax.rem(z + k, n) * rows, rows)
            seg_q = segc_ref[pl.ds(start, rows), :]
            outs = []
            for h in range(heads):
                s = right_matmul(qkv_ref[h, pl.ds(start, rows), :], qkv_ref[heads + h]) * scale
                col = pl.multiple_of(seq_len - start, rows)
                s = s + toe_ref[h, :, pl.ds(col, seq_len)]
                e = jnp.where(seg_q == segr_ref[...], jnp.exp(s), 0.0)
                l = jnp.sum(e, axis=-1, keepdims=True)
                o = matmul(e.astype(jnp.bfloat16), qkv_ref[2 * heads + h]) / l
                o_ref[h, pl.ds(start, rows), :] = o
                l_ref[h, pl.ds(start, rows), :] = l
                outs.append(o)
            piece_refs[k][...] = jnp.concatenate(outs, axis=1).astype(jnp.bfloat16)

    return body


def attn_bwd_body(n, heads, head_dim, seq_len, rows):
    scale = head_dim ** (-0.5)

    def body(z_ref, *refs):
        da_refs = refs[:n]
        x_refs = refs[n : 2 * n]
        h1_ref, qkv_ref, o_ref, l_ref, w_ref = refs[2 * n : 2 * n + 5]
        segc_ref, segr_ref, bk_ref, tab_ref = refs[2 * n + 5 : 2 * n + 9]
        gw_ref, gtab_ref, gain_ref = refs[2 * n + 9 : 2 * n + 12]
        piece_refs = refs[2 * n + 12 : 3 * n + 12]
        toe_ref, acc_ref, du_ref, dl_ref, dq_ref = refs[3 * n + 12 :]
        z = z_ref[0]
        for k in range(n):
            start = pl.multiple_of(lax.rem(z + (n - k), n) * rows, rows)
            da = da_refs[k][...].astype(jnp.float32)
            for h in range(heads):
                dah = da[:, h * head_dim : (h + 1) * head_dim]
                l = l_ref[h, pl.ds(start, rows), :]
                o = o_ref[h, pl.ds(start, rows), :]
                du_ref[h, pl.ds(start, rows), :] = (dah / l).astype(jnp.bfloat16)
                dl_ref[h, pl.ds(start, rows), :] = -jnp.sum(dah * o, axis=-1, keepdims=True) / l
        dq_all, dk_all, dv_all = [], [], []
        lane = lax.broadcasted_iota(jnp.int32, gtab_ref.shape, 1)
        gtab = jnp.zeros(gtab_ref.shape, jnp.float32)
        for h in range(heads):
            toe_ref[...] = toeplitz(bk_ref[...], tab_ref[:, h : h + 1], rows)
            acc_ref[...] = jnp.zeros_like(acc_ref)
            dk = jnp.zeros((head_dim, seq_len), jnp.float32)
            dv = jnp.zeros((head_dim, seq_len), jnp.float32)
            for i in range(n):
                block = pl.ds(i * rows, rows)
                q = qkv_ref[h, block, :]
                du = du_ref[h, block, :]
                cols = pl.ds(seq_len - i * rows, seq_len)
                s = right_matmul(q, qkv_ref[heads + h]) * scale + toe_ref[:, cols]
                e = jnp.where(segc_ref[block, :] == segr_ref[...], jnp.exp(s), 0.0)
                dp = right_matmul(du, qkv_ref[2 * heads + h]) + dl_ref[h, block, :]
                ds = (e * dp).astype(jnp.bfloat16)
                acc_ref[:, cols] += ds.astype(jnp.float32)
                dq = matmul(ds, qkv_ref[heads + h]) * scale
                dq_ref[block, h * head_dim : (h + 1) * head_dim] = dq.astype(jnp.bfloat16)
                dk = dk + left_matmul(q, ds)
                dv = dv + left_matmul(du, e.astype(jnp.bfloat16))
            first = (heads + h) * head_dim
            dq_ref[:, first : first + head_dim] = (dk * scale).T.astype(jnp.bfloat16)
            first = (2 * heads + h) * head_dim
            dq_ref[:, first : first + head_dim] = dv.T.astype(jnp.bfloat16)
            sums = diagonals(acc_ref[...])
            ids = lax.broadcasted_iota(jnp.int32, (gtab_ref.shape[0], sums.shape[1]), 0)
            col = jnp.sum(jnp.where(bk_ref[...] == ids, sums, 0.0), axis=1, keepdims=True)
            gtab = gtab + jnp.where(lane == h, col, 0.0)
        gtab_ref[...] = gtab
        gw_ref[...] = left_matmul(h1_ref[...], dq_ref[...]).astype(jnp.bfloat16)
        gain = jnp.zeros(gain_ref.shape, jnp.float32)
        for k in range(n):
            start = pl.multiple_of(lax.rem(z + k, n) * rows, rows)
            part = right_matmul(dq_ref[pl.ds(start, rows), :], w_ref[...])
            piece_refs[k][...] = part.astype(jnp.bfloat16)
            xv = x_refs[(n - k) % n][...].astype(jnp.float32)
            inv = lax.rsqrt(jnp.mean(xv * xv, axis=-1, keepdims=True) + EPS)
            gain = gain + jnp.sum(part * (xv * inv), axis=0, keepdims=True)
        gain_ref[...] = gain

    return body


def proj_body(n, piece_w):
    def body(z_ref, *refs):
        p_refs = refs[:n]
        x_ref, wo_ref, gain_ref, x1_ref, h2_ref = refs[n:]
        z = z_ref[0]
        x1 = x_ref[...].astype(jnp.float32)
        for k in range(n):
            first = pl.multiple_of(lax.rem(z + (n - k), n) * piece_w, piece_w)
            x1 = x1 + matmul(p_refs[k][...], wo_ref[pl.ds(first, piece_w), :])
        x1_ref[...] = x1
        inv = lax.rsqrt(jnp.mean(x1 * x1, axis=-1, keepdims=True) + EPS)
        h2_ref[...] = (x1 * inv * gain_ref[...]).astype(jnp.bfloat16)

    return body


def ffn_body(n, dps, rows, width, unit, row_w, row_d):
    half = dps // 2

    def body(z_ref, *refs):
        gu_refs, wd_refs = refs[:n], refs[n : 2 * n]
        hm_ref, hn_ref, cm_ref, cn_ref = refs[2 * n : 2 * n + 4]
        ym_ref, yn_ref, dm_ref, dn_ref = refs[2 * n + 4 : 2 * n + 8]
        ggu_refs, gd_refs = refs[2 * n + 8 : 3 * n + 8], refs[3 * n + 8 : 4 * n + 8]
        wide_s, wg_s, wu_s, wd_s, gd_s = refs[4 * n + 8 :]
        z = z_ref[0]
        j = pl.program_id(0)

        @pl.when(j == 0)
        def _():
            for k in range(n):
                at = lax.rem(z + (n - k), n)
                piece = gu_refs[k][...].astype(jnp.float32)
                for d in range(dps):
                    first = pl.multiple_of(at * row_w + d * n * row_w, 8)
                    wide_s[pl.ds(first, row_w), :] = piece[d * row_w : (d + 1) * row_w]
                first = pl.multiple_of(at * row_d, row_d)
                wd_s[pl.ds(first, row_d), :] = wd_refs[k][...]
            wg_s[...] = wide_s[:, :unit].astype(jnp.bfloat16)
            wu_s[...] = wide_s[:, unit:].astype(jnp.bfloat16)
            wide_s[...] = jnp.zeros_like(wide_s)
            gd_s[...] = jnp.zeros_like(gd_s)

        def rows_of(h_ref, c_ref, y_ref, d_ref):
            h2, c = h_ref[...], c_ref[...]
            wg, wu, wd = wg_s[...], wu_s[...], wd_s[...]
            gate = matmul(h2, wg)
            up = matmul(h2, wu)
            t = jnp.tanh(GELU_A * (gate + GELU_B * gate * gate * gate))
            gelu = 0.5 * gate * (1.0 + t)
            slope = 0.5 * (1.0 + t) + 0.5 * gate * (1.0 - t * t) * (
                GELU_A * (1.0 + 3.0 * GELU_B * gate * gate)
            )
            hidden = (gelu * up).astype(jnp.bfloat16)
            y_ref[...] = matmul(hidden, wd).astype(jnp.bfloat16)
            dz = right_matmul(c, wd)
            dgate = (dz * up * slope).astype(jnp.bfloat16)
            dup = (dz * gelu).astype(jnp.bfloat16)
            dh = right_matmul(dgate, wg) + right_matmul(dup, wu)
            d_ref[...] = dh.astype(jnp.bfloat16)
            gd_s[...] += left_matmul(hidden, c)
            wide_s[:, :unit] += left_matmul(h2, dgate)
            wide_s[:, unit:] += left_matmul(h2, dup)

        @pl.when(j < half)
        def _():
            rows_of(hm_ref, cm_ref, ym_ref, dm_ref)

        @pl.when(j >= half)
        def _():
            rows_of(hn_ref, cn_ref, yn_ref, dn_ref)

        @pl.when(j == dps - 1)
        def _():
            for k in range(n):
                to = lax.rem(z + k, n)
                for d in range(dps):
                    first = pl.multiple_of(to * row_w + d * n * row_w, 8)
                    part = wide_s[pl.ds(first, row_w), :]
                    ggu_refs[k][d * row_w : (d + 1) * row_w, :] = part
                first = pl.multiple_of(to * row_d, row_d)
                gd_refs[k][...] = gd_s[pl.ds(first, row_d), :].astype(jnp.bfloat16)

    return body


def dproj_body(n, piece_w):
    def body(z_ref, *refs):
        p_refs = refs[:n]
        d_refs = refs[n : n + 4]
        x1_ref, c_ref, wo_ref, gain_ref, dx1_ref = refs[n + 4 : n + 9]
        da_refs = refs[n + 9 : 2 * n + 9]
        go_ref, gg_ref = refs[2 * n + 9 :]
        z = z_ref[0]
        x1 = x1_ref[...]
        inv = lax.rsqrt(jnp.mean(x1 * x1, axis=-1, keepdims=True) + EPS)
        hat = x1 * inv
        dh = d_refs[0][...].astype(jnp.float32)
        for ref in d_refs[1:]:
            dh = dh + ref[...].astype(jnp.float32)
        gg_ref[...] = jnp.sum(dh * hat, axis=0, keepdims=True)
        scaled = dh * gain_ref[...]
        dxn = inv * (scaled - hat * jnp.mean(scaled * hat, axis=-1, keepdims=True))
        dx1 = c_ref[...].astype(jnp.float32) + dxn
        dx1_ref[...] = dx1
        dy = dx1.astype(jnp.bfloat16)
        for k in range(n):
            first = pl.multiple_of(lax.rem(z + k, n) * piece_w, piece_w)
            da = right_matmul(dy, wo_ref[pl.ds(first, piece_w), :])
            da_refs[k][...] = da.astype(jnp.bfloat16)
        for k in range(n):
            first = pl.multiple_of(lax.rem(z + (n - k), n) * piece_w, piece_w)
            go_ref[pl.ds(first, piece_w), :] = left_matmul(p_refs[k][...], dy).astype(jnp.bfloat16)

    return body


def final_body(n):
    def body(z_ref, *refs):
        part_refs, y_refs = refs[:n], refs[n : n + 4]
        x_ref, x1_ref, dx1_ref, gain_ref, din_ref, out_ref = refs[n + 4 :]
        dh = part_refs[0][...].astype(jnp.float32)
        for k in range(1, n):
            dh = dh + part_refs[k][...].astype(jnp.float32)
        xv = x_ref[...].astype(jnp.float32)
        inv = lax.rsqrt(jnp.mean(xv * xv, axis=-1, keepdims=True) + EPS)
        hat = xv * inv
        scaled = dh * gain_ref[...]
        dxn = inv * (scaled - hat * jnp.mean(scaled * hat, axis=-1, keepdims=True))
        din_ref[...] = dx1_ref[...] + dxn
        out = x1_ref[...]
        for ref in y_refs:
            out = out + ref[...].astype(jnp.float32)
        out_ref[...] = out.astype(jnp.bfloat16)

    return body


def shifts(pieces, n):
    got = [pieces[0]]
    for k in range(1, n):
        got.append(lax.ppermute(pieces[k], "seq", [(i, (i + k) % n) for i in range(n)]))
    return got


def fast(
    inputs,
    d_out,
    segments,
    buckets,
    w_query,
    w_key,
    w_value,
    w_out,
    w_gate,
    w_up,
    w_down,
    gain_attn,
    gain_ffn,
    bias_table,
):
    bf16, f32 = jnp.bfloat16, jnp.float32
    n = lax.axis_size("seq")
    both = ("dp", "seq")
    _, rows, width = inputs.shape
    seq_len = segments.shape[1]
    nb, head_count = bias_table.shape
    head_dim = width // head_count
    heads = head_count // n
    piece_w = width // n
    ff = w_gate.shape[1]
    row_w, row_d = w_query.shape[0], w_down.shape[0]
    groups = -(-row_d // row_w)
    z = lax.axis_index("seq")
    z_arr = jnp.reshape(z, (1,)).astype(jnp.int32)
    sds = jax.ShapeDtypeStruct

    dps = lax.axis_size("dp")
    half = dps // 2
    unit = ff // dps
    flat_in = inputs.reshape(rows, width)
    flat_c = d_out.reshape(rows, width)

    three = []
    for g in range(n):
        cut = slice(g * piece_w, (g + 1) * piece_w)
        three += [w_query[:, cut], w_key[:, cut], w_value[:, cut]]
    own_cols = lax.all_to_all(
        jnp.concatenate(three, axis=1), "seq", split_axis=1, concat_axis=0, tiled=True
    )
    x_all = shifts([flat_in] * n, n)
    w_qkv = lax.all_gather(own_cols, "dp", axis=0, tiled=True)
    full_out = lax.all_gather(w_out, both, axis=0, tiled=True)

    pairs = []
    for d in range(dps):
        cut = slice(d * unit, (d + 1) * unit)
        pairs += [w_gate[:, cut], w_up[:, cut]]
    own_units = lax.all_to_all(
        jnp.concatenate(pairs, axis=1), "dp", split_axis=1, concat_axis=0, tiled=True
    )
    gate_up = shifts([own_units] * n, n)
    downs = shifts([w_down] * n, n)

    def swap(rows_in, mask):
        return lax.ppermute(rows_in, "dp", [(i, i ^ mask) for i in range(dps)])

    def plane(rows_in):
        near = jnp.concatenate([rows_in] + [swap(rows_in, 2 * i) for i in range(1, half)], axis=0)
        return near, swap(near, 1)

    def back(near, far):
        both_cores = near.astype(f32) + swap(far, 1).astype(f32)
        parts = both_cores.astype(bf16).reshape(half, rows, width)
        return [parts[0]] + [swap(parts[i], 2 * i) for i in range(1, half)]

    c_near, c_far = plane(flat_c)

    seg_row = segments.reshape(1, seq_len)
    seg_col = segments.reshape(seq_len, 1)
    bucket_row = buckets.reshape(1, 2 * seq_len)
    table = lax.dynamic_slice_in_dim(bias_table, z * heads, heads, axis=1)
    gain_one = gain_attn.reshape(1, width)
    gain_two = gain_ffn.reshape(1, width)

    outs = pcall(
        attn_fwd_body(n, heads, head_dim, seq_len, rows),
        [
            sds((seq_len, width), bf16),
            sds((3 * heads, seq_len, head_dim), bf16),
            sds((heads, seq_len, head_dim), f32),
            sds((heads, seq_len, 1), f32),
        ]
        + [sds((rows, piece_w), bf16)] * n,
        [z_arr, *x_all, w_qkv, gain_one, seg_col, seg_row, bucket_row, table],
        [pltpu.VMEM((heads, rows, 2 * seq_len), f32)],
        name="attn_fwd",
    )
    h1, qkv, o_heads, l_heads = outs[:4]
    attn = shifts(outs[4:], n)

    x1, h2 = pcall(
        proj_body(n, piece_w),
        [sds((rows, width), f32), sds((rows, width), bf16)],
        [z_arr, *attn, flat_in, full_out, gain_two],
        name="proj",
    )
    h_near, h_far = plane(h2)

    const = lambda shape: pl.BlockSpec(shape, lambda j: (0,) * len(shape))
    near_spec = pl.BlockSpec((rows, width), lambda j: (jnp.minimum(j, half - 1), 0))
    far_spec = pl.BlockSpec((rows, width), lambda j: (jnp.maximum(j - half, 0), 0))
    outs = pcall(
        ffn_body(n, dps, rows, width, unit, row_w, row_d),
        [sds((half * rows, width), bf16)] * 4
        + [sds((dps * row_w, 2 * unit), f32)] * n
        + [sds((row_d, width), bf16)] * n,
        [z_arr, *gate_up, *downs, h_near, h_far, c_near, c_far],
        [
            pltpu.VMEM((width, 2 * unit), f32),
            pltpu.VMEM((width, unit), bf16),
            pltpu.VMEM((width, unit), bf16),
            pltpu.VMEM((unit, width), bf16),
            pltpu.VMEM((unit, width), f32),
        ],
        grid=(dps,),
        in_specs=[pl.BlockSpec(memory_space=pltpu.SMEM)]
        + [const((dps * row_w, 2 * unit))] * n
        + [const((row_d, width))] * n
        + [near_spec, far_spec] * 2,
        out_specs=[near_spec, far_spec] * 2
        + [const((dps * row_w, 2 * unit))] * n
        + [const((row_d, width))] * n,
        name="ffn",
    )
    d_parts = back(outs[2], outs[3])
    y_near, y_far = outs[:2]
    wide_grads = [g.astype(bf16) for g in outs[4 : n + 4]]
    down_grads = outs[n + 4 :]

    outs = pcall(
        dproj_body(n, piece_w),
        [sds((rows, width), f32)]
        + [sds((rows, piece_w), bf16)] * n
        + [sds((width, width), bf16), sds((1, width), f32)],
        [z_arr, *attn, *d_parts, x1, flat_c, full_out, gain_two],
        name="dproj",
    )
    dx1 = outs[0]
    d_attn = shifts(outs[1 : n + 1], n)
    grad_out_part, gain_two_grad = outs[n + 1 :]

    outs = pcall(
        attn_bwd_body(n, heads, head_dim, seq_len, rows),
        [sds((width, 3 * piece_w), bf16), sds((nb, 128), f32), sds((1, width), f32)]
        + [sds((rows, width), bf16)] * n,
        [z_arr, *d_attn, *x_all, h1, qkv, o_heads, l_heads, w_qkv]
        + [seg_col, seg_row, bucket_row, table],
        [
            pltpu.VMEM((rows, 2 * seq_len), f32),
            pltpu.VMEM((rows, 2 * seq_len), f32),
            pltpu.VMEM((heads, seq_len, head_dim), bf16),
            pltpu.VMEM((heads, seq_len, 1), f32),
            pltpu.VMEM((seq_len, 3 * piece_w), bf16),
        ],
        name="attn_bwd",
    )
    grad_qkv, table_part, gain_one_grad = outs[:3]
    d_normed = shifts(outs[3:], n)

    table_own = lax.dynamic_update_slice_in_dim(
        jnp.zeros((nb, head_count), f32), table_part[:, :heads], z * heads, axis=1
    )
    small = jnp.concatenate(
        [gain_one_grad.reshape(width), gain_two_grad.reshape(width), table_own.reshape(-1)]
    )
    small = lax.psum(lax.psum(small, "dp"), "seq")

    wide = 3 * piece_w + width
    square = jnp.concatenate([grad_qkv, grad_out_part], axis=1)
    square = lax.all_to_all(square, "dp", split_axis=0, concat_axis=0, tiled=True)
    summed = jnp.sum(square.reshape(dps, width // dps, wide).astype(f32), axis=0)
    owned = lax.all_to_all(summed, "seq", split_axis=0, concat_axis=0, tiled=True)
    owned = owned.reshape(n, row_w, wide)
    grad_out = jnp.sum(owned[:, :, 3 * piece_w :], axis=0)
    qkv_own = owned[:, :, : 3 * piece_w].reshape(n, row_w, 3, piece_w)
    grad_query, grad_key, grad_value = (
        qkv_own[:, :, i].transpose(1, 0, 2).reshape(row_w, width) for i in range(3)
    )

    wide_got = shifts(wide_grads, n)
    down_got = shifts(down_grads, n)
    grad_down = sum(g.astype(f32) for g in down_got)
    units = sum(g.astype(f32) for g in wide_got)
    units = lax.all_to_all(units, "dp", split_axis=0, concat_axis=1, tiled=True)
    units = units.reshape(row_w, dps, 2, unit)
    grad_gate = units[:, :, 0].reshape(row_w, ff)
    grad_up = units[:, :, 1].reshape(row_w, ff)

    y_parts = back(y_near, y_far)
    d_inputs, output = pcall(
        final_body(n),
        [sds((rows, width), f32), sds((rows, width), bf16)],
        [z_arr, *d_normed, *y_parts, flat_in, x1, dx1, gain_one],
        name="final",
    )
    return (
        output.reshape(inputs.shape),
        d_inputs.reshape(inputs.shape),
        grad_query,
        grad_key,
        grad_value,
        grad_out,
        grad_gate,
        grad_up,
        grad_down,
        small[:width],
        small[width : 2 * width],
        small[2 * width :].reshape(nb, head_count),
    )


def pick(
    inputs,
    d_out,
    segments,
    buckets,
    w_query,
    w_key,
    w_value,
    w_out,
    w_gate,
    w_up,
    w_down,
    gain_attn,
    gain_ffn,
    bias_table,
):
    n = lax.axis_size("seq")
    seqs, rows, width = inputs.shape
    row_w, row_d, ff = w_query.shape[0], w_down.shape[0], w_gate.shape[1]
    head_count = bias_table.shape[1]
    dps = lax.axis_size("dp")
    fits = (
        seqs == 1
        and dps == 8
        and head_count % n == 0
        and rows == 256
        and width % 256 == 0
        and width // head_count == 64
        and ff % (128 * dps) == 0
        and row_w % 8 == 0
        and row_d % 16 == 0
    )
    plan = fast if fits else local
    return plan(
        inputs,
        d_out,
        segments,
        buckets,
        w_query,
        w_key,
        w_value,
        w_out,
        w_gate,
        w_up,
        w_down,
        gain_attn,
        gain_ffn,
        bias_table,
    )


def solution(mesh):
    return jax.shard_map(
        pick,
        mesh=mesh,
        in_specs=(
            P("dp", "seq", None),
            P("dp", "seq", None),
            P("dp", None),
            P(),
            P(("dp", "seq"), None),
            P(("dp", "seq"), None),
            P(("dp", "seq"), None),
            P(("dp", "seq"), None),
            P(("dp", "seq"), None),
            P(("dp", "seq"), None),
            P(("dp", "seq"), None),
            P(),
            P(),
            P(),
        ),
        out_specs=(
            P("dp", "seq", None),
            P("dp", "seq", None),
            P(("dp", "seq"), None),
            P(("dp", "seq"), None),
            P(("dp", "seq"), None),
            P(("dp", "seq"), None),
            P(("dp", "seq"), None),
            P(("dp", "seq"), None),
            P(("dp", "seq"), None),
            P(),
            P(),
            P(),
        ),
        check_vma=False,
    )
```

```python
import jax
import jax.numpy as jnp
from jax import lax
from jax.experimental import pallas as pl
from jax.experimental.pallas import tpu as pltpu
from jax.sharding import PartitionSpec as P

EPS = 1e-06
MASKED = -1000000000.0
HIGHEST = lax.Precision.HIGHEST
GELU_A = 0.7978845608028654
GELU_B = 0.044715
VMEM_LIMIT = 56 * 1024 * 1024
FLOPS_PER_US = 1
BYTES_PER_US = 1


def norm_rows(values, gain):
    return values * lax.rsqrt(jnp.mean(values * values, axis=-1, keepdims=True) + EPS) * gain


def geglu(gate_act, up_act):
    return jax.nn.gelu(gate_act, approximate=True) * up_act


def matmul(left, right):
    return jnp.dot(left, right, preferred_element_type=jnp.float32)


def left_matmul(left, right):
    return lax.dot_general(
        left, right, (((0,), (0,)), ((), ())), preferred_element_type=jnp.float32
    )


def right_matmul(left, right):
    return lax.dot_general(
        left, right, (((1,), (1,)), ((), ())), preferred_element_type=jnp.float32
    )


def shifted_bias(per_dist, query_count, key_count):
    head_count, width = per_dist.shape
    flipped = per_dist[:, ::-1]
    tiled = jnp.tile(flipped, (1, query_count + 1))[:, : query_count * (width + 1)]
    rows = tiled.reshape(head_count, query_count, width + 1)[:, :, :key_count]
    return rows[:, :, ::-1]


def diagonal_sums(scores):
    head_count, row_count, col_count = scores.shape
    row_width = row_count + col_count
    padded = jnp.concatenate(
        [jnp.zeros((head_count, row_count, row_count), scores.dtype), scores], axis=2
    )
    flat_rows = jnp.concatenate(
        [
            padded.reshape(head_count, row_count * row_width),
            jnp.zeros((head_count, row_count), scores.dtype),
        ],
        axis=1,
    )
    skewed = flat_rows.reshape(head_count, row_count, row_width + 1)
    return jnp.sum(skewed, axis=1)[:, 1:row_width]


def block_parts(
    queries,
    key_heads,
    value_heads,
    seg_query,
    seg_all,
    buckets,
    table,
    first_row,
    blk_index,
    key_block,
):
    query_count = queries.shape[0]
    seq_len = key_heads.shape[0]
    scale = queries.shape[-1] ** (-0.5)
    key_start = blk_index * key_block
    key_blk = lax.dynamic_slice_in_dim(key_heads, key_start, key_block)
    value_blk = lax.dynamic_slice_in_dim(value_heads, key_start, key_block)
    seg_keys = lax.dynamic_slice_in_dim(seg_all, key_start, key_block)
    dist_base = key_start - first_row - query_count + 1 + seq_len
    window = lax.dynamic_slice_in_dim(buckets, dist_base, query_count + key_block - 1)
    onehot = (window[:, None] == jnp.arange(table.shape[0], dtype=jnp.int32)[None, :]).astype(
        jnp.float32
    )
    per_dist = jnp.dot(onehot, table, precision=HIGHEST).T
    bias_blk = shifted_bias(per_dist, query_count, key_block)
    raw_scores = (
        jnp.einsum("qhd,khd->hqk", queries, key_blk, preferred_element_type=jnp.float32) * scale
        + bias_blk
    )
    same_doc = (seg_query[:, None] == seg_keys[None, :])[None]
    weights_exp = jnp.exp(jnp.where(same_doc, raw_scores, MASKED))
    return (key_blk, value_blk, onehot, weights_exp)


def local(
    inputs,
    d_out,
    segments,
    buckets,
    w_query,
    w_key,
    w_value,
    w_out,
    w_gate,
    w_up,
    w_down,
    gain_attn,
    gain_ffn,
    bias_table,
):
    seq_count, row_count, model_width = inputs.shape
    seq_len = segments.shape[1]
    head_count = bias_table.shape[1]
    head_dim = model_width // head_count
    key_block = min(512, seq_len)
    block_count = seq_len // key_block
    token_count = seq_count * row_count
    scale = head_dim ** (-0.5)
    first_row = lax.axis_index("seq") * row_count
    blk_ids = jnp.arange(block_count, dtype=jnp.int32)
    gathered = (
        lax.all_gather(w_query, ("dp", "seq"), axis=0, tiled=True),
        lax.all_gather(w_key, ("dp", "seq"), axis=0, tiled=True),
        lax.all_gather(w_value, ("dp", "seq"), axis=0, tiled=True),
        lax.all_gather(w_out, ("dp", "seq"), axis=0, tiled=True),
        lax.all_gather(w_gate, ("dp", "seq"), axis=0, tiled=True),
        lax.all_gather(w_up, ("dp", "seq"), axis=0, tiled=True),
        lax.all_gather(w_down, ("dp", "seq"), axis=0, tiled=True),
    )
    full_query, full_key, full_value, full_out, full_gate, full_up, full_down = gathered
    flat_in = inputs.reshape(token_count, model_width).astype(jnp.float32)
    normed = norm_rows(flat_in, gain_attn).astype(jnp.bfloat16)
    queries = matmul(normed, full_query).astype(jnp.bfloat16)
    key_rows = (
        matmul(normed, full_key).astype(jnp.bfloat16).reshape(seq_count, row_count, model_width)
    )
    value_rows = (
        matmul(normed, full_value).astype(jnp.bfloat16).reshape(seq_count, row_count, model_width)
    )
    key_all, value_all = (
        lax.all_gather(key_rows, "seq", axis=1, tiled=True),
        lax.all_gather(value_rows, "seq", axis=1, tiled=True),
    )
    query_heads = queries.reshape(seq_count, row_count, head_count, head_dim)
    key_heads = key_all.reshape(seq_count, seq_len, head_count, head_dim)
    value_heads = value_all.reshape(seq_count, seq_len, head_count, head_dim)
    seg_queries = lax.dynamic_slice_in_dim(segments, first_row, row_count, axis=1)

    def attend(packed):
        query_one, key_one, value_one, seg_query, seg_all = packed

        def step(state_in, blk_index):
            totals, summed = state_in
            _, value_blk, _, weights_exp = block_parts(
                query_one,
                key_one,
                value_one,
                seg_query,
                seg_all,
                buckets,
                bias_table,
                first_row,
                blk_index,
                key_block,
            )
            summed = summed + jnp.einsum(
                "hqk,khd->qhd",
                weights_exp.astype(jnp.bfloat16),
                value_blk,
                preferred_element_type=jnp.float32,
            )
            totals = totals + jnp.sum(weights_exp, axis=-1)
            return ((totals, summed), None)

        start_state = (
            jnp.zeros((head_count, row_count), jnp.float32),
            jnp.zeros((row_count, head_count, head_dim), jnp.float32),
        )
        (totals, summed), _ = lax.scan(step, start_state, blk_ids)
        return (summed / jnp.transpose(totals)[:, :, None], totals)

    attn_f32, totals_all = lax.map(
        attend, (query_heads, key_heads, value_heads, seg_queries, segments)
    )
    attn_rows = attn_f32.reshape(token_count, model_width).astype(jnp.bfloat16)
    mixed_rows = flat_in + matmul(attn_rows, full_out)
    normed_two = norm_rows(mixed_rows, gain_ffn).astype(jnp.bfloat16)
    gate_act = matmul(normed_two, full_gate)
    up_act = matmul(normed_two, full_up)
    hidden = geglu(gate_act, up_act).astype(jnp.bfloat16)
    result = mixed_rows + matmul(hidden, full_down)
    output = result.astype(jnp.bfloat16).reshape(seq_count, row_count, model_width)
    back_weights = (
        lax.all_gather(w_query, ("dp", "seq"), axis=0, tiled=True),
        lax.all_gather(w_key, ("dp", "seq"), axis=0, tiled=True),
        lax.all_gather(w_value, ("dp", "seq"), axis=0, tiled=True),
        lax.all_gather(w_out, ("dp", "seq"), axis=0, tiled=True),
        lax.all_gather(w_gate, ("dp", "seq"), axis=0, tiled=True),
        lax.all_gather(w_up, ("dp", "seq"), axis=0, tiled=True),
        lax.all_gather(w_down, ("dp", "seq"), axis=0, tiled=True),
    )
    back_query, back_key, back_value, back_out, back_gate, back_up, back_down = back_weights
    d_res = d_out.reshape(token_count, model_width)
    grad_down = left_matmul(hidden, d_res)
    d_hidden = right_matmul(d_res, back_down)
    _, geglu_back = jax.vjp(geglu, gate_act, up_act)
    d_gate, d_up = geglu_back(d_hidden)
    d_gate = d_gate.astype(jnp.bfloat16)
    d_up = d_up.astype(jnp.bfloat16)
    grad_gate = left_matmul(normed_two, d_gate)
    grad_up = left_matmul(normed_two, d_up)
    d_normed_two = right_matmul(d_gate, back_gate) + right_matmul(d_up, back_up)
    _, norm_two_back = jax.vjp(norm_rows, mixed_rows, gain_ffn)
    d_mixed_norm, grad_gain_ffn = norm_two_back(d_normed_two)
    d_mixed = d_res.astype(jnp.float32) + d_mixed_norm
    d_branch = d_mixed.astype(jnp.bfloat16)
    grad_out = left_matmul(attn_rows, d_branch)
    d_attn = right_matmul(d_branch, back_out).reshape(seq_count, row_count, head_count, head_dim)
    totals_rows = jnp.transpose(totals_all, (0, 2, 1))
    d_unnorm_all = (d_attn / totals_rows[:, :, :, None]).astype(jnp.bfloat16)
    correction_all = -jnp.sum(d_attn * attn_f32, axis=-1) / totals_rows

    def attend_back(packed):
        query_one, key_one, value_one, seg_query, seg_all, d_unnorm, corr_rows = packed
        correction = jnp.transpose(corr_rows)

        def step(state_in, blk_index):
            d_query, d_table = state_in
            key_blk, value_blk, onehot, weights_exp = block_parts(
                query_one,
                key_one,
                value_one,
                seg_query,
                seg_all,
                buckets,
                bias_table,
                first_row,
                blk_index,
                key_block,
            )
            d_prob = jnp.einsum(
                "qhd,khd->hqk", d_unnorm, value_blk, preferred_element_type=jnp.float32
            )
            d_raw = (weights_exp * (d_prob + correction[:, :, None])).astype(jnp.bfloat16)
            d_query = (
                d_query
                + jnp.einsum("hqk,khd->qhd", d_raw, key_blk, preferred_element_type=jnp.float32)
                * scale
            )
            d_table = d_table + jnp.dot(
                diagonal_sums(d_raw.astype(jnp.float32)), onehot, precision=HIGHEST
            )
            d_key = (
                jnp.einsum("hqk,qhd->khd", d_raw, query_one, preferred_element_type=jnp.float32)
                * scale
            )
            d_value = jnp.einsum(
                "hqk,qhd->khd",
                weights_exp.astype(jnp.bfloat16),
                d_unnorm,
                preferred_element_type=jnp.float32,
            )
            return ((d_query, d_table), (d_key, d_value))

        start_state = (
            jnp.zeros((row_count, head_count, head_dim), jnp.float32),
            jnp.zeros((head_count, bias_table.shape[0]), jnp.float32),
        )
        (d_query, d_table), key_parts = lax.scan(step, start_state, blk_ids)
        d_key, d_value = key_parts
        return (
            d_query,
            d_table,
            d_key.reshape(seq_len, model_width),
            d_value.reshape(seq_len, model_width),
        )

    back_inputs = (
        query_heads,
        key_heads,
        value_heads,
        seg_queries,
        segments,
        d_unnorm_all,
        correction_all,
    )
    d_query_all, d_table_all, d_key_all, d_value_all = lax.map(attend_back, back_inputs)
    d_key_own, d_value_own = (
        lax.psum_scatter(
            d_key_all.astype(jnp.bfloat16), "seq", scatter_dimension=1, tiled=True
        ).astype(jnp.float32),
        lax.psum_scatter(
            d_value_all.astype(jnp.bfloat16), "seq", scatter_dimension=1, tiled=True
        ).astype(jnp.float32),
    )
    d_query_b = d_query_all.reshape(token_count, model_width).astype(jnp.bfloat16)
    d_key_b = d_key_own.reshape(token_count, model_width).astype(jnp.bfloat16)
    d_value_b = d_value_own.reshape(token_count, model_width).astype(jnp.bfloat16)
    grad_query = left_matmul(normed, d_query_b)
    grad_key = left_matmul(normed, d_key_b)
    grad_value = left_matmul(normed, d_value_b)
    d_normed = (
        right_matmul(d_query_b, back_query)
        + right_matmul(d_key_b, back_key)
        + right_matmul(d_value_b, back_value)
    )
    _, norm_one_back = jax.vjp(norm_rows, flat_in, gain_attn)
    d_in_norm, grad_gain_attn = norm_one_back(d_normed)
    d_inputs = (d_mixed + d_in_norm).reshape(seq_count, row_count, model_width)
    owned = (
        lax.psum_scatter(grad_query, ("dp", "seq"), scatter_dimension=0, tiled=True),
        lax.psum_scatter(grad_key, ("dp", "seq"), scatter_dimension=0, tiled=True),
        lax.psum_scatter(grad_value, ("dp", "seq"), scatter_dimension=0, tiled=True),
        lax.psum_scatter(grad_out, ("dp", "seq"), scatter_dimension=0, tiled=True),
        lax.psum_scatter(grad_gate, ("dp", "seq"), scatter_dimension=0, tiled=True),
        lax.psum_scatter(grad_up, ("dp", "seq"), scatter_dimension=0, tiled=True),
        lax.psum_scatter(grad_down, ("dp", "seq"), scatter_dimension=0, tiled=True),
    )
    table_local = jnp.transpose(jnp.sum(d_table_all, axis=0))
    gain_one, gain_two, table_grad = lax.psum(
        (grad_gain_attn, grad_gain_ffn, table_local), ("dp", "seq")
    )
    return (
        output,
        d_inputs,
        owned[0],
        owned[1],
        owned[2],
        owned[3],
        owned[4],
        owned[5],
        owned[6],
        gain_one,
        gain_two,
        table_grad,
    )


def pcall(
    body, outs, ins, scratch=(), grid=None, in_specs=None, out_specs=None, name=None, micros=1
):
    kwargs = {}
    if grid is not None:
        kwargs = dict(grid=grid, in_specs=in_specs, out_specs=out_specs)
    else:
        kwargs = dict(
            in_specs=[pl.BlockSpec(memory_space=pltpu.SMEM)]
            + [pl.BlockSpec(memory_space=pltpu.VMEM)] * (len(ins) - 1),
            out_specs=[pl.BlockSpec(memory_space=pltpu.VMEM)] * len(outs),
        )
    return pl.pallas_call(
        body,
        out_shape=outs,
        scratch_shapes=list(scratch),
        compiler_params=pltpu.CompilerParams(vmem_limit_bytes=VMEM_LIMIT),
        cost_estimate=pl.CostEstimate(
            flops=micros * FLOPS_PER_US, bytes_accessed=micros * BYTES_PER_US, transcendentals=0
        ),
        name=name,
        **kwargs,
    )(*ins)


def toeplitz(bucket_row, table_col, block):
    nb = table_col.shape[0]
    width = bucket_row.shape[1]
    ids = lax.broadcasted_iota(jnp.int32, (nb, width), 0)
    per_dist = jnp.sum(jnp.where(bucket_row == ids, table_col, 0.0), axis=0, keepdims=True)
    return pltpu.roll(
        jnp.broadcast_to(per_dist, (block, width)), 0, 1, stride=1, stride_axis=0
    )


def diagonals(acc):
    rows, width = acc.shape
    while rows > 8:
        rows //= 2
        acc = acc[:rows] + pltpu.roll(acc[rows:], width - rows, 1)
    row = lax.broadcasted_iota(jnp.int32, acc.shape, 0)
    for bit in (1, 2, 4):
        acc = jnp.where((row & bit) != 0, pltpu.roll(acc, width - bit, 1), acc)
    return jnp.sum(acc, axis=0, keepdims=True)


def attn_fwd_body(n, heads, head_dim, seq_len, rows):
    scale = head_dim ** (-0.5)

    def body(z_ref, *refs):
        x_refs = refs[:n]
        w_ref, gain_ref, segc_ref, segr_ref, bk_ref, tab_ref = refs[n : n + 6]
        h1_ref, qkv_ref, o_ref, l_ref = refs[n + 6 : n + 10]
        piece_refs = refs[n + 10 : 2 * n + 10]
        toe_ref = refs[2 * n + 10]
        z = z_ref[0]
        for k in range(n):
            start = pl.multiple_of(lax.rem(z + (n - k), n) * rows, rows)
            xv = x_refs[k][...].astype(jnp.float32)
            inv = lax.rsqrt(jnp.mean(xv * xv, axis=-1, keepdims=True) + EPS)
            h1 = (xv * inv * gain_ref[...]).astype(jnp.bfloat16)
            h1_ref[pl.ds(start, rows), :] = h1
            qkv = matmul(h1, w_ref[...]).astype(jnp.bfloat16)
            for i in range(3 * heads):
                qkv_ref[i, pl.ds(start, rows), :] = qkv[:, i * head_dim : (i + 1) * head_dim]
        for h in range(heads):
            toe_ref[h] = toeplitz(bk_ref[...], tab_ref[:, h : h + 1], rows)
        for k in range(n):
            start = pl.multiple_of(lax.rem(z + k, n) * rows, rows)
            seg_q = segc_ref[pl.ds(start, rows), :]
            outs = []
            for h in range(heads):
                s = right_matmul(qkv_ref[h, pl.ds(start, rows), :], qkv_ref[heads + h]) * scale
                col = pl.multiple_of(seq_len - start, rows)
                s = s + toe_ref[h, :, pl.ds(col, seq_len)]
                e = jnp.where(seg_q == segr_ref[...], jnp.exp(s), 0.0)
                l = jnp.sum(e, axis=-1, keepdims=True)
                o = matmul(e.astype(jnp.bfloat16), qkv_ref[2 * heads + h]) / l
                o_ref[h, pl.ds(start, rows), :] = o
                l_ref[h, pl.ds(start, rows), :] = l
                outs.append(o)
            piece_refs[k][...] = jnp.concatenate(outs, axis=1).astype(jnp.bfloat16)

    return body


def attn_bwd_body(n, heads, head_dim, seq_len, rows):
    scale = head_dim ** (-0.5)

    def body(z_ref, *refs):
        da_refs = refs[:n]
        x_refs = refs[n : 2 * n]
        h1_ref, qkv_ref, o_ref, l_ref, w_ref = refs[2 * n : 2 * n + 5]
        segc_ref, segr_ref, bk_ref, tab_ref = refs[2 * n + 5 : 2 * n + 9]
        gw_ref, gtab_ref, gain_ref = refs[2 * n + 9 : 2 * n + 12]
        piece_refs = refs[2 * n + 12 : 3 * n + 12]
        toe_ref, acc_ref, du_ref, dl_ref, dq_ref = refs[3 * n + 12 :]
        z = z_ref[0]
        for k in range(n):
            start = pl.multiple_of(lax.rem(z + (n - k), n) * rows, rows)
            da = da_refs[k][...].astype(jnp.float32)
            for h in range(heads):
                dah = da[:, h * head_dim : (h + 1) * head_dim]
                l = l_ref[h, pl.ds(start, rows), :]
                o = o_ref[h, pl.ds(start, rows), :]
                du_ref[h, pl.ds(start, rows), :] = (dah / l).astype(jnp.bfloat16)
                dl_ref[h, pl.ds(start, rows), :] = -jnp.sum(dah * o, axis=-1, keepdims=True) / l
        dq_all, dk_all, dv_all = [], [], []
        lane = lax.broadcasted_iota(jnp.int32, gtab_ref.shape, 1)
        gtab = jnp.zeros(gtab_ref.shape, jnp.float32)
        for h in range(heads):
            toe_ref[...] = toeplitz(bk_ref[...], tab_ref[:, h : h + 1], rows)
            acc_ref[...] = jnp.zeros_like(acc_ref)
            dk = jnp.zeros((head_dim, seq_len), jnp.float32)
            dv = jnp.zeros((head_dim, seq_len), jnp.float32)
            for i in range(n):
                block = pl.ds(i * rows, rows)
                q = qkv_ref[h, block, :]
                du = du_ref[h, block, :]
                cols = pl.ds(seq_len - i * rows, seq_len)
                s = right_matmul(q, qkv_ref[heads + h]) * scale + toe_ref[:, cols]
                e = jnp.where(segc_ref[block, :] == segr_ref[...], jnp.exp(s), 0.0)
                dp = right_matmul(du, qkv_ref[2 * heads + h]) + dl_ref[h, block, :]
                ds = (e * dp).astype(jnp.bfloat16)
                acc_ref[:, cols] += ds.astype(jnp.float32)
                dq = matmul(ds, qkv_ref[heads + h]) * scale
                dq_ref[block, h * head_dim : (h + 1) * head_dim] = dq.astype(jnp.bfloat16)
                dk = dk + left_matmul(q, ds)
                dv = dv + left_matmul(du, e.astype(jnp.bfloat16))
            first = (heads + h) * head_dim
            dq_ref[:, first : first + head_dim] = (dk * scale).T.astype(jnp.bfloat16)
            first = (2 * heads + h) * head_dim
            dq_ref[:, first : first + head_dim] = dv.T.astype(jnp.bfloat16)
            sums = diagonals(acc_ref[...])
            ids = lax.broadcasted_iota(jnp.int32, (gtab_ref.shape[0], sums.shape[1]), 0)
            col = jnp.sum(jnp.where(bk_ref[...] == ids, sums, 0.0), axis=1, keepdims=True)
            gtab = gtab + jnp.where(lane == h, col, 0.0)
        gtab_ref[...] = gtab
        gw_ref[...] = left_matmul(h1_ref[...], dq_ref[...]).astype(jnp.bfloat16)
        gain = jnp.zeros(gain_ref.shape, jnp.float32)
        for k in range(n):
            start = pl.multiple_of(lax.rem(z + k, n) * rows, rows)
            part = right_matmul(dq_ref[pl.ds(start, rows), :], w_ref[...])
            piece_refs[k][...] = part.astype(jnp.bfloat16)
            xv = x_refs[(n - k) % n][...].astype(jnp.float32)
            inv = lax.rsqrt(jnp.mean(xv * xv, axis=-1, keepdims=True) + EPS)
            gain = gain + jnp.sum(part * (xv * inv), axis=0, keepdims=True)
        gain_ref[...] = gain

    return body


def proj_body(n, piece_w, half):
    def body(at_ref, *refs):
        p_refs = refs[:n]
        x_ref, near_ref, far_ref, gain_ref, x1_ref, h2_ref, wo_ref = refs[n:]
        z = at_ref[1]
        tall = near_ref.shape[1]
        for i in range(half):
            for ref, mask in ((near_ref, 2 * i), (far_ref, 2 * i + 1)):
                first = pl.multiple_of(lax.bitwise_xor(at_ref[0], mask) * tall, tall)
                wo_ref[pl.ds(first, tall), :] = ref[i]
        x1 = x_ref[...].astype(jnp.float32)
        for k in range(n):
            first = pl.multiple_of(lax.rem(z + (n - k), n) * piece_w, piece_w)
            x1 = x1 + matmul(p_refs[k][...], wo_ref[pl.ds(first, piece_w), :])
        x1_ref[...] = x1
        inv = lax.rsqrt(jnp.mean(x1 * x1, axis=-1, keepdims=True) + EPS)
        h2_ref[...] = (x1 * inv * gain_ref[...]).astype(jnp.bfloat16)

    return body


def ffn_body(n, dps, rows, width, unit, row_w, row_d):
    half = dps // 2
    tall = dps * row_w

    def body(at_ref, *refs):
        w_refs = refs[:n]
        hm_ref, hn_ref, c_ref = refs[n : n + 3]
        y_ref, dm_ref, dn_ref = refs[n + 3 : n + 6]
        grads_refs = refs[n + 6 : 2 * n + 6]
        wide_s, wg_s, wu_s, wd_s, gd_s = refs[2 * n + 6 :]
        j = pl.program_id(0)

        @pl.when(j == 0)
        def _():
            for k in range(n):
                i = lax.rem(at_ref[1] + (n - k), n)
                piece = w_refs[k][:, : 2 * unit].astype(jnp.float32)
                for d in range(dps):
                    first = pl.multiple_of((d * n + i) * row_w, 8)
                    wide_s[pl.ds(first, row_w), :] = piece[d * row_w : (d + 1) * row_w]
                first = pl.multiple_of(i * row_d, row_d)
                for g in range(width // unit):
                    wd_s[pl.ds(first, row_d), g * unit : (g + 1) * unit] = w_refs[k][
                        g * row_d : (g + 1) * row_d, 2 * unit :
                    ]
            wg_s[...] = wide_s[:, :unit].astype(jnp.bfloat16)
            wu_s[...] = wide_s[:, unit:].astype(jnp.bfloat16)
            wide_s[...] = jnp.zeros_like(wide_s)
            gd_s[...] = jnp.zeros_like(gd_s)

        def rows_of(h_ref, d_ref, mask):
            owner = lax.bitwise_xor(at_ref[0], mask)
            h2, c = h_ref[...], c_ref[owner]
            wg, wu, wd = wg_s[...], wu_s[...], wd_s[...]
            gate = matmul(h2, wg)
            up = matmul(h2, wu)
            t = jnp.tanh(GELU_A * (gate + GELU_B * gate * gate * gate))
            gelu = 0.5 * gate * (1.0 + t)
            slope = 0.5 * (1.0 + t) + 0.5 * gate * (1.0 - t * t) * (
                GELU_A * (1.0 + 3.0 * GELU_B * gate * gate)
            )
            hidden = (gelu * up).astype(jnp.bfloat16)
            y_ref[owner] = matmul(hidden, wd).astype(jnp.bfloat16)
            dz = right_matmul(c, wd)
            dgate = (dz * up * slope).astype(jnp.bfloat16)
            dup = (dz * gelu).astype(jnp.bfloat16)
            dh = right_matmul(dgate, wg) + right_matmul(dup, wu)
            d_ref[...] = dh.astype(jnp.bfloat16)
            gd_s[...] += left_matmul(hidden, c)
            wide_s[:, :unit] += left_matmul(h2, dgate)
            wide_s[:, unit:] += left_matmul(h2, dup)

        @pl.when(j < half)
        def _():
            rows_of(hm_ref, dm_ref, 2 * j)

        @pl.when(j >= half)
        def _():
            rows_of(hn_ref, dn_ref, 2 * (j - half) + 1)

        @pl.when(j == dps - 1)
        def _():
            for k in range(n):
                i = lax.rem(at_ref[1] + k, n)
                parts = []
                for d in range(dps):
                    first = pl.multiple_of((d * n + i) * row_w, 8)
                    parts.append(wide_s[pl.ds(first, row_w), :])
                part = jnp.concatenate(parts, axis=0).astype(jnp.bfloat16)
                grads_refs[k][:, : 2 * unit] = part
                first = pl.multiple_of(i * row_d, row_d)
                for g in range(width // unit):
                    grads_refs[k][g * row_d : (g + 1) * row_d, 2 * unit :] = gd_s[
                        pl.ds(first, row_d), g * unit : (g + 1) * unit
                    ].astype(jnp.bfloat16)

    return body


def dproj_body(n, piece_w):
    def body(z_ref, *refs):
        p_refs = refs[:n]
        d_refs = refs[n : n + 4]
        x1_ref, c_ref, wo_ref, gain_ref, dx1_ref = refs[n + 4 : n + 9]
        da_refs = refs[n + 9 : 2 * n + 9]
        go_ref, gg_ref = refs[2 * n + 9 :]
        z = z_ref[0]
        x1 = x1_ref[...]
        inv = lax.rsqrt(jnp.mean(x1 * x1, axis=-1, keepdims=True) + EPS)
        hat = x1 * inv
        dh = d_refs[0][...].astype(jnp.float32)
        for ref in d_refs[1:]:
            dh = dh + ref[...].astype(jnp.float32)
        gg_ref[...] = jnp.sum(dh * hat, axis=0, keepdims=True)
        scaled = dh * gain_ref[...]
        dxn = inv * (scaled - hat * jnp.mean(scaled * hat, axis=-1, keepdims=True))
        dx1 = c_ref[...].astype(jnp.float32) + dxn
        dx1_ref[...] = dx1
        dy = dx1.astype(jnp.bfloat16)
        for k in range(n):
            first = pl.multiple_of(lax.rem(z + k, n) * piece_w, piece_w)
            da = right_matmul(dy, wo_ref[pl.ds(first, piece_w), :])
            da_refs[k][...] = da.astype(jnp.bfloat16)
        for k in range(n):
            first = pl.multiple_of(lax.rem(z + (n - k), n) * piece_w, piece_w)
            go_ref[pl.ds(first, piece_w), :] = left_matmul(p_refs[k][...], dy).astype(jnp.bfloat16)

    return body


def final_body(n):
    def body(z_ref, *refs):
        part_refs = refs[:n]
        x_ref, dx1_ref, gain_ref, din_ref = refs[n:]
        dh = part_refs[0][...].astype(jnp.float32)
        for k in range(1, n):
            dh = dh + part_refs[k][...].astype(jnp.float32)
        xv = x_ref[...].astype(jnp.float32)
        inv = lax.rsqrt(jnp.mean(xv * xv, axis=-1, keepdims=True) + EPS)
        hat = xv * inv
        scaled = dh * gain_ref[...]
        dxn = inv * (scaled - hat * jnp.mean(scaled * hat, axis=-1, keepdims=True))
        din_ref[...] = dx1_ref[...] + dxn

    return body


def shift(piece, k, n):
    return lax.ppermute(piece, "seq", [(i, (i + k) % n) for i in range(n)])


def shifts(pieces, n):
    return [pieces[0]] + [shift(pieces[k], k, n) for k in range(1, n)]


def fast(
    inputs,
    d_out,
    segments,
    buckets,
    w_query,
    w_key,
    w_value,
    w_out,
    w_gate,
    w_up,
    w_down,
    gain_attn,
    gain_ffn,
    bias_table,
):
    bf16, f32 = jnp.bfloat16, jnp.float32
    n = lax.axis_size("seq")
    both = ("dp", "seq")
    _, rows, width = inputs.shape
    seq_len = segments.shape[1]
    nb, head_count = bias_table.shape
    head_dim = width // head_count
    heads = head_count // n
    piece_w = width // n
    ff = w_gate.shape[1]
    row_w, row_d = w_query.shape[0], w_down.shape[0]
    groups = -(-row_d // row_w)
    z = lax.axis_index("seq")
    z_arr = jnp.reshape(z, (1,)).astype(jnp.int32)
    at_arr = jnp.stack([lax.axis_index("dp"), z]).astype(jnp.int32)
    sds = jax.ShapeDtypeStruct

    dps = lax.axis_size("dp")
    half = dps // 2
    unit = ff // dps
    flat_in = inputs.reshape(rows, width)
    flat_c = d_out.reshape(rows, width)

    three = []
    for g in range(n):
        cut = slice(g * piece_w, (g + 1) * piece_w)
        three += [w_query[:, cut], w_key[:, cut], w_value[:, cut]]
    three = jnp.concatenate(three, axis=1)
    flat_in, three = lax.optimization_barrier((flat_in, three))
    def swap(rows_in, mask):
        return lax.ppermute(rows_in, "dp", [(i, i ^ mask) for i in range(dps)])

    c_all = lax.all_gather(flat_c, "dp", axis=0, tiled=False)
    at_seq = [lax.rem(z + k, n) for k in range(n)]
    three = three.reshape(row_w, n, 3 * piece_w)
    for_them = [
        jnp.concatenate([lax.dynamic_index_in_dim(three, g, 1, keepdims=False), w_out], axis=1)
        for g in at_seq
    ]
    from_them = shifts(for_them, n)
    first_step = shift(flat_in, 1, n)
    from_them, first_step, later = lax.optimization_barrier((from_them, first_step, flat_in))
    x_all = [flat_in, first_step] + [shift(later, k, n) for k in range(2, n)]
    stack = jnp.stack([from_them[(n - k) % n] for k in range(n)])
    stack = jnp.concatenate([stack, stack], axis=0)
    stack = lax.dynamic_slice_in_dim(stack, lax.rem(n - z, n), n, axis=0)
    stack = stack.reshape(n * row_w, 3 * piece_w + width)
    own_cols, out_rows = stack[:, : 3 * piece_w], stack[:, 3 * piece_w :]
    out_near = jnp.stack([out_rows] + [swap(out_rows, 2 * i) for i in range(1, half)])
    out_far = swap(out_near, 1)
    pairs = []
    for d in range(dps):
        cut = slice(d * unit, (d + 1) * unit)
        pairs += [w_gate[:, cut], w_up[:, cut]]
    own_units = lax.all_to_all(
        jnp.concatenate(pairs, axis=1), "dp", split_axis=1, concat_axis=0, tiled=True
    )
    stacked = [w_down[:, g * unit : (g + 1) * unit] for g in range(width // unit)]
    unit_part = jnp.concatenate([own_units, jnp.concatenate(stacked, axis=0)], axis=1)
    w_qkv = lax.all_gather(own_cols, "dp", axis=0, tiled=True)
    x_all, w_qkv, unit_part, out_near, out_far = lax.optimization_barrier(
        (x_all, w_qkv, unit_part, out_near, out_far)
    )

    def plane(rows_in, others):
        got = [rows_in] + [swap(rows_in, 2 * i) for i in range(1, half)]
        got, others = lax.optimization_barrier((got, others))
        near = jnp.concatenate(got, axis=0)
        return near, swap(near, 1), others

    def back(near, far):
        both_cores = near.astype(f32) + swap(far, 1).astype(f32)
        parts = both_cores.astype(bf16).reshape(half, rows, width)
        return [parts[0]] + [swap(parts[i], 2 * i) for i in range(1, half)]


    seg_row = segments.reshape(1, seq_len)
    seg_col = segments.reshape(seq_len, 1)
    bucket_row = buckets.reshape(1, 2 * seq_len)
    table = lax.dynamic_slice_in_dim(bias_table, z * heads, heads, axis=1)
    gain_one = gain_attn.reshape(1, width)
    gain_two = gain_ffn.reshape(1, width)

    outs = pcall(
        attn_fwd_body(n, heads, head_dim, seq_len, rows),
        [
            sds((seq_len, width), bf16),
            sds((3 * heads, seq_len, head_dim), bf16),
            sds((heads, seq_len, head_dim), f32),
            sds((heads, seq_len, 1), f32),
        ]
        + [sds((rows, piece_w), bf16)] * n,
        [z_arr, *x_all, w_qkv, gain_one, seg_col, seg_row, bucket_row, table],
        [pltpu.VMEM((heads, rows, 2 * seq_len), f32)],
        name="attn_fwd",
        micros=12,
    )
    h1, qkv, o_heads, l_heads = outs[:4]
    attn = shifts(outs[4:], n)
    attn, unit_part = lax.optimization_barrier((attn, unit_part))
    unit_weights = shifts([unit_part] * n, n)

    x1, h2, full_out = pcall(
        proj_body(n, piece_w, half),
        [sds((rows, width), f32), sds((rows, width), bf16), sds((width, width), bf16)],
        [at_arr, *attn, flat_in, out_near, out_far, gain_two],
        name="proj",
        micros=3,
    )
    h_near, h_far, (unit_weights, c_all) = plane(h2, (unit_weights, c_all))

    const = lambda shape: pl.BlockSpec(shape, lambda j: (0,) * len(shape))
    near_spec = pl.BlockSpec((rows, width), lambda j: (jnp.minimum(j, half - 1), 0))
    far_spec = pl.BlockSpec((rows, width), lambda j: (jnp.maximum(j - half, 0), 0))
    outs = pcall(
        ffn_body(n, dps, rows, width, unit, row_w, row_d),
        [sds((dps, rows, width), bf16)]
        + [sds((half * rows, width), bf16)] * 2
        + [sds((dps * row_w, 3 * unit), bf16)] * n,
        [at_arr, *unit_weights, h_near, h_far, c_all],
        [
            pltpu.VMEM((width, 2 * unit), f32),
            pltpu.VMEM((width, unit), bf16),
            pltpu.VMEM((width, unit), bf16),
            pltpu.VMEM((unit, width), bf16),
            pltpu.VMEM((unit, width), f32),
        ],
        grid=(dps,),
        in_specs=[
            pl.BlockSpec(memory_space=pltpu.SMEM),
            *[const((dps * row_w, 3 * unit))] * n,
            near_spec,
            far_spec,
            const((dps, rows, width)),
        ],
        out_specs=[
            const((dps, rows, width)),
            near_spec,
            far_spec,
            *[const((dps * row_w, 3 * unit))] * n,
        ],
        name="ffn",
        micros=16,
    )
    y_parts, d_near, d_far = outs[:3]
    d_parts, unit_got, y_parts = lax.optimization_barrier(
        (back(d_near, d_far), shifts(outs[3:], n), y_parts)
    )
    unit_own = sum(g.astype(f32) for g in unit_got).astype(bf16)
    outs = pcall(
        dproj_body(n, piece_w),
        [sds((rows, width), f32)]
        + [sds((rows, piece_w), bf16)] * n
        + [sds((width, width), bf16), sds((1, width), f32)],
        [z_arr, *attn, *d_parts, x1, flat_c, full_out, gain_two],
        name="dproj",
        micros=5,
    )
    dx1 = outs[0]
    d_pieces = outs[1 : n + 1]
    grad_out_part, gain_two_grad = outs[n + 1 :]
    d_attn = shifts(d_pieces, n)
    lanes = 2 * unit * row_w * dps // width
    folded = [unit_own[:, i * lanes : (i + 1) * lanes] for i in range(2 * unit // lanes)]
    folded = [f.reshape(dps, row_w, lanes) for f in folded]
    folded = jnp.concatenate(folded, axis=1).reshape(width, lanes)

    outs = pcall(
        attn_bwd_body(n, heads, head_dim, seq_len, rows),
        [sds((width, 3 * piece_w), bf16), sds((nb, 128), f32), sds((1, width), f32)]
        + [sds((rows, width), bf16)] * n,
        [z_arr, *d_attn, *x_all, h1, qkv, o_heads, l_heads, w_qkv]
        + [seg_col, seg_row, bucket_row, table],
        [
            pltpu.VMEM((rows, 2 * seq_len), f32),
            pltpu.VMEM((rows, 2 * seq_len), f32),
            pltpu.VMEM((heads, seq_len, head_dim), bf16),
            pltpu.VMEM((heads, seq_len, 1), f32),
            pltpu.VMEM((seq_len, 3 * piece_w), bf16),
        ],
        name="attn_bwd",
        micros=20,
    )
    grad_qkv, table_part, gain_one_grad = outs[:3]
    d_normed = shifts(outs[3:], n)

    wide = 3 * piece_w
    table_own = lax.dynamic_update_slice_in_dim(
        jnp.zeros((nb, head_count), f32), table_part[:, :heads], z * heads, axis=1
    )
    small = jnp.concatenate(
        [gain_one_grad.reshape(width), gain_two_grad.reshape(width), table_own.reshape(-1)]
    )
    small = lax.psum(lax.psum(small, "dp"), "seq")
    y_own = lax.psum_scatter(
        y_parts.reshape(dps * rows, width), "dp", scatter_dimension=0, tiled=True
    )
    square = lax.all_to_all(
        jnp.concatenate([grad_qkv, grad_out_part, folded], axis=1),
        "dp",
        split_axis=0,
        concat_axis=0,
        tiled=True,
    )
    square, y_own, d_normed, small = lax.optimization_barrier((square, y_own, d_normed, small))
    output = (x1 + y_own.astype(f32)).astype(bf16)
    square = square.reshape(dps, width // dps, wide + width + lanes).astype(f32)
    summed = jnp.sum(square[:, :, : wide + width], axis=0).astype(bf16)
    owned = lax.all_to_all(summed, "seq", split_axis=0, concat_axis=0, tiled=True)
    owned = owned.reshape(n, row_w, wide + width).astype(f32)
    grad_out = jnp.sum(owned[:, :, wide:], axis=0)
    qkv_own = owned[:, :, :wide].reshape(n, row_w, 3, piece_w)
    grad_query, grad_key, grad_value = (
        qkv_own[:, :, i].transpose(1, 0, 2).reshape(row_w, width) for i in range(3)
    )

    stacked = unit_own[:, 2 * unit :].astype(f32).reshape(width // unit, row_d, unit)
    grad_down = jnp.concatenate([stacked[g] for g in range(width // unit)], axis=1)
    folded = square[:, :, wide + width :].reshape(dps, 2 * unit // lanes, row_w, lanes)
    per = unit // lanes
    grad_gate, grad_up = (
        jnp.concatenate(
            [folded[d, half_at + i] for d in range(dps) for i in range(per)], axis=1
        )
        for half_at in (0, per)
    )

    (d_inputs,) = pcall(
        final_body(n),
        [sds((rows, width), f32)],
        [z_arr, *d_normed, flat_in, dx1, gain_one],
        name="final",
        micros=3,
    )
    return (
        output.reshape(inputs.shape),
        d_inputs.reshape(inputs.shape),
        grad_query,
        grad_key,
        grad_value,
        grad_out,
        grad_gate,
        grad_up,
        grad_down,
        small[:width],
        small[width : 2 * width],
        small[2 * width :].reshape(nb, head_count),
    )


def pick(
    inputs,
    d_out,
    segments,
    buckets,
    w_query,
    w_key,
    w_value,
    w_out,
    w_gate,
    w_up,
    w_down,
    gain_attn,
    gain_ffn,
    bias_table,
):
    n = lax.axis_size("seq")
    seqs, rows, width = inputs.shape
    row_w, row_d, ff = w_query.shape[0], w_down.shape[0], w_gate.shape[1]
    head_count = bias_table.shape[1]
    dps = lax.axis_size("dp")
    fits = (
        seqs == 1
        and dps == 8
        and head_count % n == 0
        and rows == 256
        and width % 256 == 0
        and width // head_count == 64
        and ff == 256 * dps
        and width == 3 * (ff // dps)
        and row_w * dps == 3 * row_d
        and row_w % 8 == 0
        and row_d % 16 == 0
    )
    plan = fast if fits else local
    return plan(
        inputs,
        d_out,
        segments,
        buckets,
        w_query,
        w_key,
        w_value,
        w_out,
        w_gate,
        w_up,
        w_down,
        gain_attn,
        gain_ffn,
        bias_table,
    )


def solution(mesh):
    return jax.shard_map(
        pick,
        mesh=mesh,
        in_specs=(
            P("dp", "seq", None),
            P("dp", "seq", None),
            P("dp", None),
            P(),
            P(("dp", "seq"), None),
            P(("dp", "seq"), None),
            P(("dp", "seq"), None),
            P(("dp", "seq"), None),
            P(("dp", "seq"), None),
            P(("dp", "seq"), None),
            P(("dp", "seq"), None),
            P(),
            P(),
            P(),
        ),
        out_specs=(
            P("dp", "seq", None),
            P("dp", "seq", None),
            P(("dp", "seq"), None),
            P(("dp", "seq"), None),
            P(("dp", "seq"), None),
            P(("dp", "seq"), None),
            P(("dp", "seq"), None),
            P(("dp", "seq"), None),
            P(("dp", "seq"), None),
            P(),
            P(),
            P(),
        ),
        check_vma=False,
    )
```

```python
import jax
import jax.numpy as jnp
from jax import lax
from jax.experimental import pallas as pl
from jax.experimental.pallas import tpu as pltpu
from jax.sharding import PartitionSpec as P

EPS = 1e-06
MASKED = -1000000000.0
HIGHEST = lax.Precision.HIGHEST
GELU_A = 0.7978845608028654
GELU_B = 0.044715
VMEM_LIMIT = 56 * 1024 * 1024
FLOPS_PER_US = 1_150_000_000
BYTES_PER_US = 3_600_000


def norm_rows(values, gain):
    return values * lax.rsqrt(jnp.mean(values * values, axis=-1, keepdims=True) + EPS) * gain


def geglu(gate_act, up_act):
    return jax.nn.gelu(gate_act, approximate=True) * up_act


def matmul(left, right):
    return jnp.dot(left, right, preferred_element_type=jnp.float32)


def left_matmul(left, right):
    return lax.dot_general(
        left, right, (((0,), (0,)), ((), ())), preferred_element_type=jnp.float32
    )


def right_matmul(left, right):
    return lax.dot_general(
        left, right, (((1,), (1,)), ((), ())), preferred_element_type=jnp.float32
    )


def shifted_bias(per_dist, query_count, key_count):
    head_count, width = per_dist.shape
    flipped = per_dist[:, ::-1]
    tiled = jnp.tile(flipped, (1, query_count + 1))[:, : query_count * (width + 1)]
    rows = tiled.reshape(head_count, query_count, width + 1)[:, :, :key_count]
    return rows[:, :, ::-1]


def diagonal_sums(scores):
    head_count, row_count, col_count = scores.shape
    row_width = row_count + col_count
    padded = jnp.concatenate(
        [jnp.zeros((head_count, row_count, row_count), scores.dtype), scores], axis=2
    )
    flat_rows = jnp.concatenate(
        [
            padded.reshape(head_count, row_count * row_width),
            jnp.zeros((head_count, row_count), scores.dtype),
        ],
        axis=1,
    )
    skewed = flat_rows.reshape(head_count, row_count, row_width + 1)
    return jnp.sum(skewed, axis=1)[:, 1:row_width]


def block_parts(
    queries,
    key_heads,
    value_heads,
    seg_query,
    seg_all,
    buckets,
    table,
    first_row,
    blk_index,
    key_block,
):
    query_count = queries.shape[0]
    seq_len = key_heads.shape[0]
    scale = queries.shape[-1] ** (-0.5)
    key_start = blk_index * key_block
    key_blk = lax.dynamic_slice_in_dim(key_heads, key_start, key_block)
    value_blk = lax.dynamic_slice_in_dim(value_heads, key_start, key_block)
    seg_keys = lax.dynamic_slice_in_dim(seg_all, key_start, key_block)
    dist_base = key_start - first_row - query_count + 1 + seq_len
    window = lax.dynamic_slice_in_dim(buckets, dist_base, query_count + key_block - 1)
    onehot = (window[:, None] == jnp.arange(table.shape[0], dtype=jnp.int32)[None, :]).astype(
        jnp.float32
    )
    per_dist = jnp.dot(onehot, table, precision=HIGHEST).T
    bias_blk = shifted_bias(per_dist, query_count, key_block)
    raw_scores = (
        jnp.einsum("qhd,khd->hqk", queries, key_blk, preferred_element_type=jnp.float32) * scale
        + bias_blk
    )
    same_doc = (seg_query[:, None] == seg_keys[None, :])[None]
    weights_exp = jnp.exp(jnp.where(same_doc, raw_scores, MASKED))
    return (key_blk, value_blk, onehot, weights_exp)


def local(
    inputs,
    d_out,
    segments,
    buckets,
    w_query,
    w_key,
    w_value,
    w_out,
    w_gate,
    w_up,
    w_down,
    gain_attn,
    gain_ffn,
    bias_table,
):
    seq_count, row_count, model_width = inputs.shape
    seq_len = segments.shape[1]
    head_count = bias_table.shape[1]
    head_dim = model_width // head_count
    key_block = min(512, seq_len)
    block_count = seq_len // key_block
    token_count = seq_count * row_count
    scale = head_dim ** (-0.5)
    first_row = lax.axis_index("seq") * row_count
    blk_ids = jnp.arange(block_count, dtype=jnp.int32)
    gathered = (
        lax.all_gather(w_query, ("dp", "seq"), axis=0, tiled=True),
        lax.all_gather(w_key, ("dp", "seq"), axis=0, tiled=True),
        lax.all_gather(w_value, ("dp", "seq"), axis=0, tiled=True),
        lax.all_gather(w_out, ("dp", "seq"), axis=0, tiled=True),
        lax.all_gather(w_gate, ("dp", "seq"), axis=0, tiled=True),
        lax.all_gather(w_up, ("dp", "seq"), axis=0, tiled=True),
        lax.all_gather(w_down, ("dp", "seq"), axis=0, tiled=True),
    )
    full_query, full_key, full_value, full_out, full_gate, full_up, full_down = gathered
    flat_in = inputs.reshape(token_count, model_width).astype(jnp.float32)
    normed = norm_rows(flat_in, gain_attn).astype(jnp.bfloat16)
    queries = matmul(normed, full_query).astype(jnp.bfloat16)
    key_rows = (
        matmul(normed, full_key).astype(jnp.bfloat16).reshape(seq_count, row_count, model_width)
    )
    value_rows = (
        matmul(normed, full_value).astype(jnp.bfloat16).reshape(seq_count, row_count, model_width)
    )
    key_all, value_all = (
        lax.all_gather(key_rows, "seq", axis=1, tiled=True),
        lax.all_gather(value_rows, "seq", axis=1, tiled=True),
    )
    query_heads = queries.reshape(seq_count, row_count, head_count, head_dim)
    key_heads = key_all.reshape(seq_count, seq_len, head_count, head_dim)
    value_heads = value_all.reshape(seq_count, seq_len, head_count, head_dim)
    seg_queries = lax.dynamic_slice_in_dim(segments, first_row, row_count, axis=1)

    def attend(packed):
        query_one, key_one, value_one, seg_query, seg_all = packed

        def step(state_in, blk_index):
            totals, summed = state_in
            _, value_blk, _, weights_exp = block_parts(
                query_one,
                key_one,
                value_one,
                seg_query,
                seg_all,
                buckets,
                bias_table,
                first_row,
                blk_index,
                key_block,
            )
            summed = summed + jnp.einsum(
                "hqk,khd->qhd",
                weights_exp.astype(jnp.bfloat16),
                value_blk,
                preferred_element_type=jnp.float32,
            )
            totals = totals + jnp.sum(weights_exp, axis=-1)
            return ((totals, summed), None)

        start_state = (
            jnp.zeros((head_count, row_count), jnp.float32),
            jnp.zeros((row_count, head_count, head_dim), jnp.float32),
        )
        (totals, summed), _ = lax.scan(step, start_state, blk_ids)
        return (summed / jnp.transpose(totals)[:, :, None], totals)

    attn_f32, totals_all = lax.map(
        attend, (query_heads, key_heads, value_heads, seg_queries, segments)
    )
    attn_rows = attn_f32.reshape(token_count, model_width).astype(jnp.bfloat16)
    mixed_rows = flat_in + matmul(attn_rows, full_out)
    normed_two = norm_rows(mixed_rows, gain_ffn).astype(jnp.bfloat16)
    gate_act = matmul(normed_two, full_gate)
    up_act = matmul(normed_two, full_up)
    hidden = geglu(gate_act, up_act).astype(jnp.bfloat16)
    result = mixed_rows + matmul(hidden, full_down)
    output = result.astype(jnp.bfloat16).reshape(seq_count, row_count, model_width)
    back_weights = (
        lax.all_gather(w_query, ("dp", "seq"), axis=0, tiled=True),
        lax.all_gather(w_key, ("dp", "seq"), axis=0, tiled=True),
        lax.all_gather(w_value, ("dp", "seq"), axis=0, tiled=True),
        lax.all_gather(w_out, ("dp", "seq"), axis=0, tiled=True),
        lax.all_gather(w_gate, ("dp", "seq"), axis=0, tiled=True),
        lax.all_gather(w_up, ("dp", "seq"), axis=0, tiled=True),
        lax.all_gather(w_down, ("dp", "seq"), axis=0, tiled=True),
    )
    back_query, back_key, back_value, back_out, back_gate, back_up, back_down = back_weights
    d_res = d_out.reshape(token_count, model_width)
    grad_down = left_matmul(hidden, d_res)
    d_hidden = right_matmul(d_res, back_down)
    _, geglu_back = jax.vjp(geglu, gate_act, up_act)
    d_gate, d_up = geglu_back(d_hidden)
    d_gate = d_gate.astype(jnp.bfloat16)
    d_up = d_up.astype(jnp.bfloat16)
    grad_gate = left_matmul(normed_two, d_gate)
    grad_up = left_matmul(normed_two, d_up)
    d_normed_two = right_matmul(d_gate, back_gate) + right_matmul(d_up, back_up)
    _, norm_two_back = jax.vjp(norm_rows, mixed_rows, gain_ffn)
    d_mixed_norm, grad_gain_ffn = norm_two_back(d_normed_two)
    d_mixed = d_res.astype(jnp.float32) + d_mixed_norm
    d_branch = d_mixed.astype(jnp.bfloat16)
    grad_out = left_matmul(attn_rows, d_branch)
    d_attn = right_matmul(d_branch, back_out).reshape(seq_count, row_count, head_count, head_dim)
    totals_rows = jnp.transpose(totals_all, (0, 2, 1))
    d_unnorm_all = (d_attn / totals_rows[:, :, :, None]).astype(jnp.bfloat16)
    correction_all = -jnp.sum(d_attn * attn_f32, axis=-1) / totals_rows

    def attend_back(packed):
        query_one, key_one, value_one, seg_query, seg_all, d_unnorm, corr_rows = packed
        correction = jnp.transpose(corr_rows)

        def step(state_in, blk_index):
            d_query, d_table = state_in
            key_blk, value_blk, onehot, weights_exp = block_parts(
                query_one,
                key_one,
                value_one,
                seg_query,
                seg_all,
                buckets,
                bias_table,
                first_row,
                blk_index,
                key_block,
            )
            d_prob = jnp.einsum(
                "qhd,khd->hqk", d_unnorm, value_blk, preferred_element_type=jnp.float32
            )
            d_raw = (weights_exp * (d_prob + correction[:, :, None])).astype(jnp.bfloat16)
            d_query = (
                d_query
                + jnp.einsum("hqk,khd->qhd", d_raw, key_blk, preferred_element_type=jnp.float32)
                * scale
            )
            d_table = d_table + jnp.dot(
                diagonal_sums(d_raw.astype(jnp.float32)), onehot, precision=HIGHEST
            )
            d_key = (
                jnp.einsum("hqk,qhd->khd", d_raw, query_one, preferred_element_type=jnp.float32)
                * scale
            )
            d_value = jnp.einsum(
                "hqk,qhd->khd",
                weights_exp.astype(jnp.bfloat16),
                d_unnorm,
                preferred_element_type=jnp.float32,
            )
            return ((d_query, d_table), (d_key, d_value))

        start_state = (
            jnp.zeros((row_count, head_count, head_dim), jnp.float32),
            jnp.zeros((head_count, bias_table.shape[0]), jnp.float32),
        )
        (d_query, d_table), key_parts = lax.scan(step, start_state, blk_ids)
        d_key, d_value = key_parts
        return (
            d_query,
            d_table,
            d_key.reshape(seq_len, model_width),
            d_value.reshape(seq_len, model_width),
        )

    back_inputs = (
        query_heads,
        key_heads,
        value_heads,
        seg_queries,
        segments,
        d_unnorm_all,
        correction_all,
    )
    d_query_all, d_table_all, d_key_all, d_value_all = lax.map(attend_back, back_inputs)
    d_key_own, d_value_own = (
        lax.psum_scatter(
            d_key_all.astype(jnp.bfloat16), "seq", scatter_dimension=1, tiled=True
        ).astype(jnp.float32),
        lax.psum_scatter(
            d_value_all.astype(jnp.bfloat16), "seq", scatter_dimension=1, tiled=True
        ).astype(jnp.float32),
    )
    d_query_b = d_query_all.reshape(token_count, model_width).astype(jnp.bfloat16)
    d_key_b = d_key_own.reshape(token_count, model_width).astype(jnp.bfloat16)
    d_value_b = d_value_own.reshape(token_count, model_width).astype(jnp.bfloat16)
    grad_query = left_matmul(normed, d_query_b)
    grad_key = left_matmul(normed, d_key_b)
    grad_value = left_matmul(normed, d_value_b)
    d_normed = (
        right_matmul(d_query_b, back_query)
        + right_matmul(d_key_b, back_key)
        + right_matmul(d_value_b, back_value)
    )
    _, norm_one_back = jax.vjp(norm_rows, flat_in, gain_attn)
    d_in_norm, grad_gain_attn = norm_one_back(d_normed)
    d_inputs = (d_mixed + d_in_norm).reshape(seq_count, row_count, model_width)
    owned = (
        lax.psum_scatter(grad_query, ("dp", "seq"), scatter_dimension=0, tiled=True),
        lax.psum_scatter(grad_key, ("dp", "seq"), scatter_dimension=0, tiled=True),
        lax.psum_scatter(grad_value, ("dp", "seq"), scatter_dimension=0, tiled=True),
        lax.psum_scatter(grad_out, ("dp", "seq"), scatter_dimension=0, tiled=True),
        lax.psum_scatter(grad_gate, ("dp", "seq"), scatter_dimension=0, tiled=True),
        lax.psum_scatter(grad_up, ("dp", "seq"), scatter_dimension=0, tiled=True),
        lax.psum_scatter(grad_down, ("dp", "seq"), scatter_dimension=0, tiled=True),
    )
    table_local = jnp.transpose(jnp.sum(d_table_all, axis=0))
    gain_one, gain_two, table_grad = lax.psum(
        (grad_gain_attn, grad_gain_ffn, table_local), ("dp", "seq")
    )
    return (
        output,
        d_inputs,
        owned[0],
        owned[1],
        owned[2],
        owned[3],
        owned[4],
        owned[5],
        owned[6],
        gain_one,
        gain_two,
        table_grad,
    )


def pcall(
    body, outs, ins, scratch=(), grid=None, in_specs=None, out_specs=None, name=None, micros=1
):
    kwargs = {}
    if grid is not None:
        kwargs = dict(grid=grid, in_specs=in_specs, out_specs=out_specs)
    else:
        kwargs = dict(
            in_specs=[pl.BlockSpec(memory_space=pltpu.SMEM)]
            + [pl.BlockSpec(memory_space=pltpu.VMEM)] * (len(ins) - 1),
            out_specs=[pl.BlockSpec(memory_space=pltpu.VMEM)] * len(outs),
        )
    return pl.pallas_call(
        body,
        out_shape=outs,
        scratch_shapes=list(scratch),
        compiler_params=pltpu.CompilerParams(vmem_limit_bytes=VMEM_LIMIT),
        cost_estimate=pl.CostEstimate(
            flops=micros * FLOPS_PER_US, bytes_accessed=micros * BYTES_PER_US, transcendentals=0
        ),
        name=name,
        **kwargs,
    )(*ins)


def toeplitz(bucket_row, table_col, block):
    nb = table_col.shape[0]
    width = bucket_row.shape[1]
    ids = lax.broadcasted_iota(jnp.int32, (nb, width), 0)
    per_dist = jnp.sum(jnp.where(bucket_row == ids, table_col, 0.0), axis=0, keepdims=True)
    return pltpu.roll(
        jnp.broadcast_to(per_dist, (block, width)), 0, 1, stride=1, stride_axis=0
    )


def diagonals(acc):
    rows, width = acc.shape
    while rows > 8:
        rows //= 2
        acc = acc[:rows] + pltpu.roll(acc[rows:], width - rows, 1)
    row = lax.broadcasted_iota(jnp.int32, acc.shape, 0)
    for bit in (1, 2, 4):
        acc = jnp.where((row & bit) != 0, pltpu.roll(acc, width - bit, 1), acc)
    return jnp.sum(acc, axis=0, keepdims=True)


def attn_fwd_body(n, heads, head_dim, seq_len, rows):
    scale = head_dim ** (-0.5)

    def body(z_ref, *refs):
        x_refs = refs[:n]
        w_ref, gain_ref, segc_ref, segr_ref, bk_ref, tab_ref = refs[n : n + 6]
        h1_ref, qkv_ref, o_ref, l_ref = refs[n + 6 : n + 10]
        piece_refs = refs[n + 10 : 2 * n + 10]
        toe_ref = refs[2 * n + 10]
        z = z_ref[0]
        for k in range(n):
            start = pl.multiple_of(lax.rem(z + (n - k), n) * rows, rows)
            xv = x_refs[k][...].astype(jnp.float32)
            inv = lax.rsqrt(jnp.mean(xv * xv, axis=-1, keepdims=True) + EPS)
            h1 = (xv * inv * gain_ref[...]).astype(jnp.bfloat16)
            h1_ref[pl.ds(start, rows), :] = h1
            qkv = matmul(h1, w_ref[...]).astype(jnp.bfloat16)
            for i in range(3 * heads):
                qkv_ref[i, pl.ds(start, rows), :] = qkv[:, i * head_dim : (i + 1) * head_dim]
        for h in range(heads):
            toe_ref[h] = toeplitz(bk_ref[...], tab_ref[:, h : h + 1], rows)
        for k in range(n):
            start = pl.multiple_of(lax.rem(z + k, n) * rows, rows)
            seg_q = segc_ref[pl.ds(start, rows), :]
            outs = []
            for h in range(heads):
                s = right_matmul(qkv_ref[h, pl.ds(start, rows), :], qkv_ref[heads + h]) * scale
                col = pl.multiple_of(seq_len - start, rows)
                s = s + toe_ref[h, :, pl.ds(col, seq_len)]
                e = jnp.where(seg_q == segr_ref[...], jnp.exp(s), 0.0)
                l = jnp.sum(e, axis=-1, keepdims=True)
                o = matmul(e.astype(jnp.bfloat16), qkv_ref[2 * heads + h]) / l
                o_ref[h, pl.ds(start, rows), :] = o
                l_ref[h, pl.ds(start, rows), :] = l
                outs.append(o)
            piece_refs[k][...] = jnp.concatenate(outs, axis=1).astype(jnp.bfloat16)

    return body


def attn_bwd_body(n, heads, head_dim, seq_len, rows):
    scale = head_dim ** (-0.5)

    def body(z_ref, *refs):
        da_refs = refs[:n]
        x_refs = refs[n : 2 * n]
        h1_ref, qkv_ref, o_ref, l_ref, w_ref = refs[2 * n : 2 * n + 5]
        segc_ref, segr_ref, bk_ref, tab_ref = refs[2 * n + 5 : 2 * n + 9]
        gw_ref, gtab_ref, gain_ref = refs[2 * n + 9 : 2 * n + 12]
        piece_refs = refs[2 * n + 12 : 3 * n + 12]
        toe_ref, acc_ref, du_ref, dl_ref, dq_ref = refs[3 * n + 12 :]
        z = z_ref[0]
        for k in range(n):
            start = pl.multiple_of(lax.rem(z + (n - k), n) * rows, rows)
            da = da_refs[k][...].astype(jnp.float32)
            for h in range(heads):
                dah = da[:, h * head_dim : (h + 1) * head_dim]
                l = l_ref[h, pl.ds(start, rows), :]
                o = o_ref[h, pl.ds(start, rows), :]
                du_ref[h, pl.ds(start, rows), :] = (dah / l).astype(jnp.bfloat16)
                dl_ref[h, pl.ds(start, rows), :] = -jnp.sum(dah * o, axis=-1, keepdims=True) / l
        dq_all, dk_all, dv_all = [], [], []
        lane = lax.broadcasted_iota(jnp.int32, gtab_ref.shape, 1)
        gtab = jnp.zeros(gtab_ref.shape, jnp.float32)
        for h in range(heads):
            toe_ref[...] = toeplitz(bk_ref[...], tab_ref[:, h : h + 1], rows)
            acc_ref[...] = jnp.zeros_like(acc_ref)
            dk = jnp.zeros((head_dim, seq_len), jnp.float32)
            dv = jnp.zeros((head_dim, seq_len), jnp.float32)
            for i in range(n):
                block = pl.ds(i * rows, rows)
                q = qkv_ref[h, block, :]
                du = du_ref[h, block, :]
                cols = pl.ds(seq_len - i * rows, seq_len)
                s = right_matmul(q, qkv_ref[heads + h]) * scale + toe_ref[:, cols]
                e = jnp.where(segc_ref[block, :] == segr_ref[...], jnp.exp(s), 0.0)
                dp = right_matmul(du, qkv_ref[2 * heads + h]) + dl_ref[h, block, :]
                ds = (e * dp).astype(jnp.bfloat16)
                acc_ref[:, cols] += ds.astype(jnp.float32)
                dq = matmul(ds, qkv_ref[heads + h]) * scale
                dq_ref[block, h * head_dim : (h + 1) * head_dim] = dq.astype(jnp.bfloat16)
                dk = dk + left_matmul(q, ds)
                dv = dv + left_matmul(du, e.astype(jnp.bfloat16))
            first = (heads + h) * head_dim
            dq_ref[:, first : first + head_dim] = (dk * scale).T.astype(jnp.bfloat16)
            first = (2 * heads + h) * head_dim
            dq_ref[:, first : first + head_dim] = dv.T.astype(jnp.bfloat16)
            sums = diagonals(acc_ref[...])
            ids = lax.broadcasted_iota(jnp.int32, (gtab_ref.shape[0], sums.shape[1]), 0)
            col = jnp.sum(jnp.where(bk_ref[...] == ids, sums, 0.0), axis=1, keepdims=True)
            gtab = gtab + jnp.where(lane == h, col, 0.0)
        gtab_ref[...] = gtab
        gw_ref[...] = left_matmul(h1_ref[...], dq_ref[...]).astype(jnp.bfloat16)
        gain = jnp.zeros(gain_ref.shape, jnp.float32)
        for k in range(n):
            start = pl.multiple_of(lax.rem(z + k, n) * rows, rows)
            part = right_matmul(dq_ref[pl.ds(start, rows), :], w_ref[...])
            piece_refs[k][...] = part.astype(jnp.bfloat16)
            xv = x_refs[(n - k) % n][...].astype(jnp.float32)
            inv = lax.rsqrt(jnp.mean(xv * xv, axis=-1, keepdims=True) + EPS)
            gain = gain + jnp.sum(part * (xv * inv), axis=0, keepdims=True)
        gain_ref[...] = gain

    return body


def proj_body(n, piece_w):
    def body(z_ref, *refs):
        p_refs = refs[:n]
        x_ref, wo_ref, gain_ref, x1_ref, h2_ref = refs[n:]
        z = z_ref[0]
        x1 = x_ref[...].astype(jnp.float32)
        for k in range(n):
            first = pl.multiple_of(lax.rem(z + (n - k), n) * piece_w, piece_w)
            x1 = x1 + matmul(p_refs[k][...], wo_ref[pl.ds(first, piece_w), :])
        x1_ref[...] = x1
        inv = lax.rsqrt(jnp.mean(x1 * x1, axis=-1, keepdims=True) + EPS)
        h2_ref[...] = (x1 * inv * gain_ref[...]).astype(jnp.bfloat16)

    return body


def ffn_body(n, dps, rows, width, unit, row_w, row_d):
    steps = dps // 2

    def body(at_ref, *refs):
        w_refs = refs[:n]
        hm_ref, hn_ref, c_ref = refs[n : n + 3]
        y_ref, dm_ref, dn_ref = refs[n + 3 : n + 6]
        grads_refs = refs[n + 6 : 2 * n + 6]
        wide_s, wgu_s, wd_s, gd_s = refs[2 * n + 6 :]
        j = pl.program_id(0)
        mine = lax.rem(at_ref[0] // 2, 2)

        @pl.when(j == 0)
        def _():
            for k in range(n):
                i = lax.rem(at_ref[1] + (n - k), n)
                piece = w_refs[k][:, : 2 * unit].astype(jnp.float32)
                for d in range(dps):
                    first = pl.multiple_of((d * n + i) * row_w, 8)
                    wide_s[pl.ds(first, row_w), :] = piece[d * row_w : (d + 1) * row_w]
                first = pl.multiple_of(i * row_d, row_d)
                for g in range(width // unit):
                    wd_s[pl.ds(first, row_d), g * unit : (g + 1) * unit] = w_refs[k][
                        g * row_d : (g + 1) * row_d, 2 * unit :
                    ]
            wgu_s[...] = wide_s[...].astype(jnp.bfloat16)
            wide_s[...] = jnp.zeros_like(wide_s)
            gd_s[...] = jnp.zeros_like(gd_s)

        def rows_of(h_ref, d_ref):
            h2 = h_ref[...]
            c = jnp.concatenate([c_ref[0, mine, 0], c_ref[0, 1 - mine, 0]], axis=0)
            wgu, wd = wgu_s[...], wd_s[...]
            both = matmul(h2, wgu)
            gate, up = both[:, :unit], both[:, unit:]
            half = 0.5 + 0.5 * jnp.tanh(GELU_A * (gate + GELU_B * gate * gate * gate))
            gelu = gate * half
            slope = half + 2.0 * gelu * (1.0 - half) * (
                GELU_A * (1.0 + 3.0 * GELU_B * gate * gate)
            )
            hidden = (gelu * up).astype(jnp.bfloat16)
            y = matmul(hidden, wd).astype(jnp.bfloat16)
            y_ref[0, mine, 0] = y[:rows]
            y_ref[0, 1 - mine, 0] = y[rows:]
            dz = right_matmul(c, wd)
            dgu = jnp.concatenate(
                [(dz * up * slope).astype(jnp.bfloat16), (dz * gelu).astype(jnp.bfloat16)], axis=1
            )
            d_ref[...] = right_matmul(dgu, wgu).astype(jnp.bfloat16)
            gd_s[...] += left_matmul(hidden, c)
            wide_s[...] += left_matmul(h2, dgu)

        @pl.when(j < steps // 2)
        def _():
            rows_of(hm_ref, dm_ref)

        @pl.when(j >= steps // 2)
        def _():
            rows_of(hn_ref, dn_ref)

        @pl.when(j == steps - 1)
        def _():
            for k in range(n):
                i = lax.rem(at_ref[1] + k, n)
                parts = []
                for d in range(dps):
                    first = pl.multiple_of((d * n + i) * row_w, 8)
                    parts.append(wide_s[pl.ds(first, row_w), :])
                part = jnp.concatenate(parts, axis=0).astype(jnp.bfloat16)
                grads_refs[k][:, : 2 * unit] = part
                first = pl.multiple_of(i * row_d, row_d)
                for g in range(width // unit):
                    grads_refs[k][g * row_d : (g + 1) * row_d, 2 * unit :] = gd_s[
                        pl.ds(first, row_d), g * unit : (g + 1) * unit
                    ].astype(jnp.bfloat16)

    return body


def ffn(n, dps, rows, width, unit, row_w, row_d, at_arr, unit_weights, h_near, h_far, c_all):
    bf16, f32 = jnp.bfloat16, jnp.float32
    sds = jax.ShapeDtypeStruct
    steps = dps // 2
    half = steps // 2
    tall = dps * row_w
    const = lambda shape: pl.BlockSpec(shape, lambda j, at: (0,) * len(shape))
    near = pl.BlockSpec((2 * rows, width), lambda j, at: (jnp.minimum(j, half - 1), 0))
    far = pl.BlockSpec((2 * rows, width), lambda j, at: (jnp.maximum(j - half, 0), 0))
    owned = pl.BlockSpec(
        (1, 2, 1, rows, width),
        lambda j, at: (
            lax.bitwise_xor(at[0] // 4, lax.rem(j, half)),
            0,
            lax.bitwise_xor(lax.rem(at[0], 2), j // half),
            0,
            0,
        ),
    )
    shape = (dps // 4, 2, 2, rows, width)
    outs = pl.pallas_call(
        ffn_body(n, dps, rows, width, unit, row_w, row_d),
        out_shape=[sds(shape, bf16)]
        + [sds((half * 2 * rows, width), bf16)] * 2
        + [sds((tall, 3 * unit), bf16)] * n,
        grid_spec=pltpu.PrefetchScalarGridSpec(
            num_scalar_prefetch=1,
            grid=(steps,),
            in_specs=[const((tall, 3 * unit))] * n + [near, far, owned],
            out_specs=[owned, near, far] + [const((tall, 3 * unit))] * n,
            scratch_shapes=[
                pltpu.VMEM((width, 2 * unit), f32),
                pltpu.VMEM((width, 2 * unit), bf16),
                pltpu.VMEM((unit, width), bf16),
                pltpu.VMEM((unit, width), f32),
            ],
        ),
        compiler_params=pltpu.CompilerParams(vmem_limit_bytes=VMEM_LIMIT),
        cost_estimate=pl.CostEstimate(flops=0, bytes_accessed=0, transcendentals=0),
        name="ffn",
    )(at_arr, *unit_weights, h_near, h_far, c_all.reshape(shape))
    return outs


def dproj_body(n, piece_w):
    def body(z_ref, *refs):
        p_refs = refs[:n]
        d_refs = refs[n : n + 4]
        x1_ref, c_ref, wo_ref, gain_ref, dx1_ref = refs[n + 4 : n + 9]
        da_refs = refs[n + 9 : 2 * n + 9]
        go_ref, gg_ref = refs[2 * n + 9 :]
        z = z_ref[0]
        x1 = x1_ref[...]
        inv = lax.rsqrt(jnp.mean(x1 * x1, axis=-1, keepdims=True) + EPS)
        hat = x1 * inv
        dh = d_refs[0][...].astype(jnp.float32)
        for ref in d_refs[1:]:
            dh = dh + ref[...].astype(jnp.float32)
        gg_ref[...] = jnp.sum(dh * hat, axis=0, keepdims=True)
        scaled = dh * gain_ref[...]
        dxn = inv * (scaled - hat * jnp.mean(scaled * hat, axis=-1, keepdims=True))
        dx1 = c_ref[...].astype(jnp.float32) + dxn
        dx1_ref[...] = dx1
        dy = dx1.astype(jnp.bfloat16)
        for k in range(n):
            first = pl.multiple_of(lax.rem(z + k, n) * piece_w, piece_w)
            da = right_matmul(dy, wo_ref[pl.ds(first, piece_w), :])
            da_refs[k][...] = da.astype(jnp.bfloat16)
        for k in range(n):
            first = pl.multiple_of(lax.rem(z + (n - k), n) * piece_w, piece_w)
            go_ref[pl.ds(first, piece_w), :] = left_matmul(p_refs[k][...], dy).astype(jnp.bfloat16)

    return body


def final_body(n):
    def body(z_ref, *refs):
        part_refs = refs[:n]
        x_ref, dx1_ref, gain_ref, din_ref = refs[n:]
        dh = part_refs[0][...].astype(jnp.float32)
        for k in range(1, n):
            dh = dh + part_refs[k][...].astype(jnp.float32)
        xv = x_ref[...].astype(jnp.float32)
        inv = lax.rsqrt(jnp.mean(xv * xv, axis=-1, keepdims=True) + EPS)
        hat = xv * inv
        scaled = dh * gain_ref[...]
        dxn = inv * (scaled - hat * jnp.mean(scaled * hat, axis=-1, keepdims=True))
        din_ref[...] = dx1_ref[...] + dxn

    return body


def shift(piece, k, n):
    return lax.ppermute(piece, "seq", [(i, (i + k) % n) for i in range(n)])


def shifts(pieces, n):
    return [pieces[0]] + [shift(pieces[k], k, n) for k in range(1, n)]


def fast(
    inputs,
    d_out,
    segments,
    buckets,
    w_query,
    w_key,
    w_value,
    w_out,
    w_gate,
    w_up,
    w_down,
    gain_attn,
    gain_ffn,
    bias_table,
):
    bf16, f32 = jnp.bfloat16, jnp.float32
    n = lax.axis_size("seq")
    both = ("dp", "seq")
    _, rows, width = inputs.shape
    seq_len = segments.shape[1]
    nb, head_count = bias_table.shape
    head_dim = width // head_count
    heads = head_count // n
    piece_w = width // n
    ff = w_gate.shape[1]
    row_w, row_d = w_query.shape[0], w_down.shape[0]
    groups = -(-row_d // row_w)
    z = lax.axis_index("seq")
    z_arr = jnp.reshape(z, (1,)).astype(jnp.int32)
    at_arr = jnp.stack([lax.axis_index("dp"), z]).astype(jnp.int32)
    sds = jax.ShapeDtypeStruct

    dps = lax.axis_size("dp")
    half = dps // 2
    unit = ff // dps
    flat_in = inputs.reshape(rows, width)
    flat_c = d_out.reshape(rows, width)

    three = []
    for g in range(n):
        cut = slice(g * piece_w, (g + 1) * piece_w)
        three += [w_query[:, cut], w_key[:, cut], w_value[:, cut]]
    three = jnp.concatenate(three, axis=1)
    flat_in, three = lax.optimization_barrier((flat_in, three))
    def swap(rows_in, mask):
        return lax.ppermute(rows_in, "dp", [(i, i ^ mask) for i in range(dps)])

    at_seq = [lax.rem(z + k, n) for k in range(n)]
    three = three.reshape(row_w, n, 3 * piece_w)
    for_them = [
        jnp.concatenate([lax.dynamic_index_in_dim(three, g, 1, keepdims=False), w_out], axis=1)
        for g in at_seq
    ]
    from_them = shifts(for_them, n)
    pairs = []
    for d in range(dps):
        cut = slice(d * unit, (d + 1) * unit)
        pairs += [w_gate[:, cut], w_up[:, cut]]
    pairs, early = lax.optimization_barrier((jnp.concatenate(pairs, axis=1), flat_in))
    first_step = shift(early, 1, n)
    from_them, later = lax.optimization_barrier((from_them, flat_in))
    x_all = [flat_in, first_step] + [shift(later, k, n) for k in range(2, n)]
    stack = jnp.stack([from_them[(n - k) % n] for k in range(n)])
    stack = jnp.concatenate([stack, stack], axis=0)
    stack = lax.dynamic_slice_in_dim(stack, lax.rem(n - z, n), n, axis=0)
    stack = stack.reshape(n * row_w, 3 * piece_w + width)
    own_cols, out_rows = stack[:, : 3 * piece_w], stack[:, 3 * piece_w :]
    own_units = lax.all_to_all(pairs, "dp", split_axis=1, concat_axis=0, tiled=True)
    stacked = [w_down[:, g * unit : (g + 1) * unit] for g in range(width // unit)]
    unit_part = jnp.concatenate([own_units, jnp.concatenate(stacked, axis=0)], axis=1)
    w_qkv = lax.all_gather(own_cols, "dp", axis=0, tiled=True)
    full_out = lax.all_gather(out_rows, "dp", axis=0, tiled=True)
    x_all, w_qkv, unit_part, full_out, flat_c = lax.optimization_barrier(
        (x_all, w_qkv, unit_part, full_out, flat_c)
    )

    def plane(rows_in, others):
        got = [rows_in] + [swap(rows_in, 2 * i) for i in range(1, half)]
        got, others = lax.optimization_barrier((got, others))
        near = jnp.concatenate(got, axis=0)
        return near, swap(near, 1), others

    def back(near, far):
        both_cores = near.astype(f32) + swap(far, 1).astype(f32)
        parts = both_cores.astype(bf16).reshape(half, rows, width)
        return [parts[0]] + [swap(parts[i], 2 * i) for i in range(1, half)]


    seg_row = segments.reshape(1, seq_len)
    seg_col = segments.reshape(seq_len, 1)
    bucket_row = buckets.reshape(1, 2 * seq_len)
    table = lax.dynamic_slice_in_dim(bias_table, z * heads, heads, axis=1)
    gain_one = gain_attn.reshape(1, width)
    gain_two = gain_ffn.reshape(1, width)

    outs = pcall(
        attn_fwd_body(n, heads, head_dim, seq_len, rows),
        [
            sds((seq_len, width), bf16),
            sds((3 * heads, seq_len, head_dim), bf16),
            sds((heads, seq_len, head_dim), f32),
            sds((heads, seq_len, 1), f32),
        ]
        + [sds((rows, piece_w), bf16)] * n,
        [z_arr, *x_all, w_qkv, gain_one, seg_col, seg_row, bucket_row, table],
        [pltpu.VMEM((heads, rows, 2 * seq_len), f32)],
        name="attn_fwd",
        micros=0,
    )
    h1, qkv, o_heads, l_heads = outs[:4]
    attn = shifts(outs[4:], n)
    c_all = lax.all_gather(flat_c, "dp", axis=0, tiled=False)
    attn, unit_part = lax.optimization_barrier((attn, unit_part))
    unit_weights = shifts([unit_part] * n, n)

    x1, h2 = pcall(
        proj_body(n, piece_w),
        [sds((rows, width), f32), sds((rows, width), bf16)],
        [z_arr, *attn, flat_in, full_out, gain_two],
        name="proj",
        micros=0,
    )
    h_near, h_far, (unit_weights, c_all) = plane(h2, (unit_weights, c_all))

    outs = ffn(
        n, dps, rows, width, unit, row_w, row_d, at_arr, unit_weights, h_near, h_far, c_all
    )
    y_parts, d_near, d_far = outs[:3]
    d_parts, unit_got, y_parts = lax.optimization_barrier(
        (back(d_near, d_far), shifts(outs[3:], n), y_parts)
    )
    unit_own = sum(g.astype(f32) for g in unit_got).astype(bf16)
    outs = pcall(
        dproj_body(n, piece_w),
        [sds((rows, width), f32)]
        + [sds((rows, piece_w), bf16)] * n
        + [sds((width, width), bf16), sds((1, width), f32)],
        [z_arr, *attn, *d_parts, x1, flat_c, full_out, gain_two],
        name="dproj",
        micros=0,
    )
    dx1 = outs[0]
    d_pieces = outs[1 : n + 1]
    grad_out_part, gain_two_grad = outs[n + 1 :]
    d_attn = shifts(d_pieces, n)
    lanes = 2 * unit * row_w * dps // width
    folded = [unit_own[:, i * lanes : (i + 1) * lanes] for i in range(2 * unit // lanes)]
    folded = [f.reshape(dps, row_w, lanes) for f in folded]
    folded = jnp.concatenate(folded, axis=1).reshape(width, lanes)
    out_units = lax.all_to_all(
        jnp.concatenate([grad_out_part, folded], axis=1),
        "dp",
        split_axis=0,
        concat_axis=0,
        tiled=True,
    )

    outs = pcall(
        attn_bwd_body(n, heads, head_dim, seq_len, rows),
        [sds((width, 3 * piece_w), bf16), sds((nb, 128), f32), sds((1, width), f32)]
        + [sds((rows, width), bf16)] * n,
        [z_arr, *d_attn, *x_all, h1, qkv, o_heads, l_heads, w_qkv]
        + [seg_col, seg_row, bucket_row, table],
        [
            pltpu.VMEM((rows, 2 * seq_len), f32),
            pltpu.VMEM((rows, 2 * seq_len), f32),
            pltpu.VMEM((heads, seq_len, head_dim), bf16),
            pltpu.VMEM((heads, seq_len, 1), f32),
            pltpu.VMEM((seq_len, 3 * piece_w), bf16),
        ],
        name="attn_bwd",
        micros=20,
    )
    grad_qkv, table_part, gain_one_grad = outs[:3]
    d_normed = shifts(outs[3:], n)

    wide = 3 * piece_w
    table_own = lax.dynamic_update_slice_in_dim(
        jnp.zeros((nb, head_count), f32), table_part[:, :heads], z * heads, axis=1
    )
    small = jnp.concatenate(
        [gain_one_grad.reshape(width), gain_two_grad.reshape(width), table_own.reshape(-1)]
    )
    small = lax.psum(small, "dp")
    grad_qkv, out_units, small = lax.optimization_barrier((grad_qkv, out_units, small))
    small = lax.psum(small, "seq")
    y_own = lax.psum_scatter(
        y_parts.reshape(dps * rows, width), "dp", scatter_dimension=0, tiled=True
    )
    out_units = out_units.reshape(dps, width // dps, width + lanes).astype(f32)
    out_sum = jnp.sum(out_units[:, :, :width], axis=0).astype(bf16)
    square = lax.all_to_all(
        grad_qkv, "dp", split_axis=0, concat_axis=0, tiled=True
    )
    square, y_own, d_normed, small, out_sum = lax.optimization_barrier(
        (square, y_own, d_normed, small, out_sum)
    )
    output = (x1 + y_own.astype(f32)).astype(bf16)
    square = square.reshape(dps, width // dps, wide).astype(f32)
    summed = jnp.concatenate([jnp.sum(square, axis=0).astype(bf16), out_sum], axis=1)
    owned = lax.all_to_all(summed, "seq", split_axis=0, concat_axis=0, tiled=True)
    owned = owned.reshape(n, row_w, wide + width).astype(f32)
    grad_out = jnp.sum(owned[:, :, wide:], axis=0)
    qkv_own = owned[:, :, :wide].reshape(n, row_w, 3, piece_w)
    grad_query, grad_key, grad_value = (
        qkv_own[:, :, i].transpose(1, 0, 2).reshape(row_w, width) for i in range(3)
    )

    stacked = unit_own[:, 2 * unit :].astype(f32).reshape(width // unit, row_d, unit)
    grad_down = jnp.concatenate([stacked[g] for g in range(width // unit)], axis=1)
    folded = out_units[:, :, width:].reshape(dps, 2 * unit // lanes, row_w, lanes)
    per = unit // lanes
    grad_gate, grad_up = (
        jnp.concatenate(
            [folded[d, half_at + i] for d in range(dps) for i in range(per)], axis=1
        )
        for half_at in (0, per)
    )

    (d_inputs,) = pcall(
        final_body(n),
        [sds((rows, width), f32)],
        [z_arr, *d_normed, flat_in, dx1, gain_one],
        name="final",
        micros=0,
    )
    return (
        output.reshape(inputs.shape),
        d_inputs.reshape(inputs.shape),
        grad_query,
        grad_key,
        grad_value,
        grad_out,
        grad_gate,
        grad_up,
        grad_down,
        small[:width],
        small[width : 2 * width],
        small[2 * width :].reshape(nb, head_count),
    )


def pick(
    inputs,
    d_out,
    segments,
    buckets,
    w_query,
    w_key,
    w_value,
    w_out,
    w_gate,
    w_up,
    w_down,
    gain_attn,
    gain_ffn,
    bias_table,
):
    n = lax.axis_size("seq")
    seqs, rows, width = inputs.shape
    row_w, row_d, ff = w_query.shape[0], w_down.shape[0], w_gate.shape[1]
    head_count = bias_table.shape[1]
    dps = lax.axis_size("dp")
    fits = (
        seqs == 1
        and dps == 8
        and head_count % n == 0
        and rows == 256
        and width % 256 == 0
        and width // head_count == 64
        and ff == 256 * dps
        and width == 3 * (ff // dps)
        and row_w * dps == 3 * row_d
        and row_w % 8 == 0
        and row_d % 16 == 0
    )
    plan = fast if fits else local
    return plan(
        inputs,
        d_out,
        segments,
        buckets,
        w_query,
        w_key,
        w_value,
        w_out,
        w_gate,
        w_up,
        w_down,
        gain_attn,
        gain_ffn,
        bias_table,
    )


def solution(mesh):
    return jax.shard_map(
        pick,
        mesh=mesh,
        in_specs=(
            P("dp", "seq", None),
            P("dp", "seq", None),
            P("dp", None),
            P(),
            P(("dp", "seq"), None),
            P(("dp", "seq"), None),
            P(("dp", "seq"), None),
            P(("dp", "seq"), None),
            P(("dp", "seq"), None),
            P(("dp", "seq"), None),
            P(("dp", "seq"), None),
            P(),
            P(),
            P(),
        ),
        out_specs=(
            P("dp", "seq", None),
            P("dp", "seq", None),
            P(("dp", "seq"), None),
            P(("dp", "seq"), None),
            P(("dp", "seq"), None),
            P(("dp", "seq"), None),
            P(("dp", "seq"), None),
            P(("dp", "seq"), None),
            P(("dp", "seq"), None),
            P(),
            P(),
            P(),
        ),
        check_vma=False,
    )
```

```python
import jax
import jax.numpy as jnp
from jax import lax
from jax.experimental import pallas as pl
from jax.experimental.pallas import tpu as pltpu
from jax.sharding import PartitionSpec as P

EPS = 1e-06
MASKED = -1000000000.0
HIGHEST = lax.Precision.HIGHEST
GELU_A = 0.7978845608028654
GELU_B = 0.044715
VMEM_LIMIT = 56 * 1024 * 1024
FLOPS_PER_US = 1_150_000_000
BYTES_PER_US = 3_600_000


def norm_rows(values, gain):
    return values * lax.rsqrt(jnp.mean(values * values, axis=-1, keepdims=True) + EPS) * gain


def geglu(gate_act, up_act):
    return jax.nn.gelu(gate_act, approximate=True) * up_act


def matmul(left, right):
    return jnp.dot(left, right, preferred_element_type=jnp.float32)


def left_matmul(left, right):
    return lax.dot_general(
        left, right, (((0,), (0,)), ((), ())), preferred_element_type=jnp.float32
    )


def right_matmul(left, right):
    return lax.dot_general(
        left, right, (((1,), (1,)), ((), ())), preferred_element_type=jnp.float32
    )


def shifted_bias(per_dist, query_count, key_count):
    head_count, width = per_dist.shape
    flipped = per_dist[:, ::-1]
    tiled = jnp.tile(flipped, (1, query_count + 1))[:, : query_count * (width + 1)]
    rows = tiled.reshape(head_count, query_count, width + 1)[:, :, :key_count]
    return rows[:, :, ::-1]


def diagonal_sums(scores):
    head_count, row_count, col_count = scores.shape
    row_width = row_count + col_count
    padded = jnp.concatenate(
        [jnp.zeros((head_count, row_count, row_count), scores.dtype), scores], axis=2
    )
    flat_rows = jnp.concatenate(
        [
            padded.reshape(head_count, row_count * row_width),
            jnp.zeros((head_count, row_count), scores.dtype),
        ],
        axis=1,
    )
    skewed = flat_rows.reshape(head_count, row_count, row_width + 1)
    return jnp.sum(skewed, axis=1)[:, 1:row_width]


def block_parts(
    queries,
    key_heads,
    value_heads,
    seg_query,
    seg_all,
    buckets,
    table,
    first_row,
    blk_index,
    key_block,
):
    query_count = queries.shape[0]
    seq_len = key_heads.shape[0]
    scale = queries.shape[-1] ** (-0.5)
    key_start = blk_index * key_block
    key_blk = lax.dynamic_slice_in_dim(key_heads, key_start, key_block)
    value_blk = lax.dynamic_slice_in_dim(value_heads, key_start, key_block)
    seg_keys = lax.dynamic_slice_in_dim(seg_all, key_start, key_block)
    dist_base = key_start - first_row - query_count + 1 + seq_len
    window = lax.dynamic_slice_in_dim(buckets, dist_base, query_count + key_block - 1)
    onehot = (window[:, None] == jnp.arange(table.shape[0], dtype=jnp.int32)[None, :]).astype(
        jnp.float32
    )
    per_dist = jnp.dot(onehot, table, precision=HIGHEST).T
    bias_blk = shifted_bias(per_dist, query_count, key_block)
    raw_scores = (
        jnp.einsum("qhd,khd->hqk", queries, key_blk, preferred_element_type=jnp.float32) * scale
        + bias_blk
    )
    same_doc = (seg_query[:, None] == seg_keys[None, :])[None]
    weights_exp = jnp.exp(jnp.where(same_doc, raw_scores, MASKED))
    return (key_blk, value_blk, onehot, weights_exp)


def local(
    inputs,
    d_out,
    segments,
    buckets,
    w_query,
    w_key,
    w_value,
    w_out,
    w_gate,
    w_up,
    w_down,
    gain_attn,
    gain_ffn,
    bias_table,
):
    seq_count, row_count, model_width = inputs.shape
    seq_len = segments.shape[1]
    head_count = bias_table.shape[1]
    head_dim = model_width // head_count
    key_block = min(512, seq_len)
    block_count = seq_len // key_block
    token_count = seq_count * row_count
    scale = head_dim ** (-0.5)
    first_row = lax.axis_index("seq") * row_count
    blk_ids = jnp.arange(block_count, dtype=jnp.int32)
    gathered = (
        lax.all_gather(w_query, ("dp", "seq"), axis=0, tiled=True),
        lax.all_gather(w_key, ("dp", "seq"), axis=0, tiled=True),
        lax.all_gather(w_value, ("dp", "seq"), axis=0, tiled=True),
        lax.all_gather(w_out, ("dp", "seq"), axis=0, tiled=True),
        lax.all_gather(w_gate, ("dp", "seq"), axis=0, tiled=True),
        lax.all_gather(w_up, ("dp", "seq"), axis=0, tiled=True),
        lax.all_gather(w_down, ("dp", "seq"), axis=0, tiled=True),
    )
    full_query, full_key, full_value, full_out, full_gate, full_up, full_down = gathered
    flat_in = inputs.reshape(token_count, model_width).astype(jnp.float32)
    normed = norm_rows(flat_in, gain_attn).astype(jnp.bfloat16)
    queries = matmul(normed, full_query).astype(jnp.bfloat16)
    key_rows = (
        matmul(normed, full_key).astype(jnp.bfloat16).reshape(seq_count, row_count, model_width)
    )
    value_rows = (
        matmul(normed, full_value).astype(jnp.bfloat16).reshape(seq_count, row_count, model_width)
    )
    key_all, value_all = (
        lax.all_gather(key_rows, "seq", axis=1, tiled=True),
        lax.all_gather(value_rows, "seq", axis=1, tiled=True),
    )
    query_heads = queries.reshape(seq_count, row_count, head_count, head_dim)
    key_heads = key_all.reshape(seq_count, seq_len, head_count, head_dim)
    value_heads = value_all.reshape(seq_count, seq_len, head_count, head_dim)
    seg_queries = lax.dynamic_slice_in_dim(segments, first_row, row_count, axis=1)

    def attend(packed):
        query_one, key_one, value_one, seg_query, seg_all = packed

        def step(state_in, blk_index):
            totals, summed = state_in
            _, value_blk, _, weights_exp = block_parts(
                query_one,
                key_one,
                value_one,
                seg_query,
                seg_all,
                buckets,
                bias_table,
                first_row,
                blk_index,
                key_block,
            )
            summed = summed + jnp.einsum(
                "hqk,khd->qhd",
                weights_exp.astype(jnp.bfloat16),
                value_blk,
                preferred_element_type=jnp.float32,
            )
            totals = totals + jnp.sum(weights_exp, axis=-1)
            return ((totals, summed), None)

        start_state = (
            jnp.zeros((head_count, row_count), jnp.float32),
            jnp.zeros((row_count, head_count, head_dim), jnp.float32),
        )
        (totals, summed), _ = lax.scan(step, start_state, blk_ids)
        return (summed / jnp.transpose(totals)[:, :, None], totals)

    attn_f32, totals_all = lax.map(
        attend, (query_heads, key_heads, value_heads, seg_queries, segments)
    )
    attn_rows = attn_f32.reshape(token_count, model_width).astype(jnp.bfloat16)
    mixed_rows = flat_in + matmul(attn_rows, full_out)
    normed_two = norm_rows(mixed_rows, gain_ffn).astype(jnp.bfloat16)
    gate_act = matmul(normed_two, full_gate)
    up_act = matmul(normed_two, full_up)
    hidden = geglu(gate_act, up_act).astype(jnp.bfloat16)
    result = mixed_rows + matmul(hidden, full_down)
    output = result.astype(jnp.bfloat16).reshape(seq_count, row_count, model_width)
    back_weights = (
        lax.all_gather(w_query, ("dp", "seq"), axis=0, tiled=True),
        lax.all_gather(w_key, ("dp", "seq"), axis=0, tiled=True),
        lax.all_gather(w_value, ("dp", "seq"), axis=0, tiled=True),
        lax.all_gather(w_out, ("dp", "seq"), axis=0, tiled=True),
        lax.all_gather(w_gate, ("dp", "seq"), axis=0, tiled=True),
        lax.all_gather(w_up, ("dp", "seq"), axis=0, tiled=True),
        lax.all_gather(w_down, ("dp", "seq"), axis=0, tiled=True),
    )
    back_query, back_key, back_value, back_out, back_gate, back_up, back_down = back_weights
    d_res = d_out.reshape(token_count, model_width)
    grad_down = left_matmul(hidden, d_res)
    d_hidden = right_matmul(d_res, back_down)
    _, geglu_back = jax.vjp(geglu, gate_act, up_act)
    d_gate, d_up = geglu_back(d_hidden)
    d_gate = d_gate.astype(jnp.bfloat16)
    d_up = d_up.astype(jnp.bfloat16)
    grad_gate = left_matmul(normed_two, d_gate)
    grad_up = left_matmul(normed_two, d_up)
    d_normed_two = right_matmul(d_gate, back_gate) + right_matmul(d_up, back_up)
    _, norm_two_back = jax.vjp(norm_rows, mixed_rows, gain_ffn)
    d_mixed_norm, grad_gain_ffn = norm_two_back(d_normed_two)
    d_mixed = d_res.astype(jnp.float32) + d_mixed_norm
    d_branch = d_mixed.astype(jnp.bfloat16)
    grad_out = left_matmul(attn_rows, d_branch)
    d_attn = right_matmul(d_branch, back_out).reshape(seq_count, row_count, head_count, head_dim)
    totals_rows = jnp.transpose(totals_all, (0, 2, 1))
    d_unnorm_all = (d_attn / totals_rows[:, :, :, None]).astype(jnp.bfloat16)
    correction_all = -jnp.sum(d_attn * attn_f32, axis=-1) / totals_rows

    def attend_back(packed):
        query_one, key_one, value_one, seg_query, seg_all, d_unnorm, corr_rows = packed
        correction = jnp.transpose(corr_rows)

        def step(state_in, blk_index):
            d_query, d_table = state_in
            key_blk, value_blk, onehot, weights_exp = block_parts(
                query_one,
                key_one,
                value_one,
                seg_query,
                seg_all,
                buckets,
                bias_table,
                first_row,
                blk_index,
                key_block,
            )
            d_prob = jnp.einsum(
                "qhd,khd->hqk", d_unnorm, value_blk, preferred_element_type=jnp.float32
            )
            d_raw = (weights_exp * (d_prob + correction[:, :, None])).astype(jnp.bfloat16)
            d_query = (
                d_query
                + jnp.einsum("hqk,khd->qhd", d_raw, key_blk, preferred_element_type=jnp.float32)
                * scale
            )
            d_table = d_table + jnp.dot(
                diagonal_sums(d_raw.astype(jnp.float32)), onehot, precision=HIGHEST
            )
            d_key = (
                jnp.einsum("hqk,qhd->khd", d_raw, query_one, preferred_element_type=jnp.float32)
                * scale
            )
            d_value = jnp.einsum(
                "hqk,qhd->khd",
                weights_exp.astype(jnp.bfloat16),
                d_unnorm,
                preferred_element_type=jnp.float32,
            )
            return ((d_query, d_table), (d_key, d_value))

        start_state = (
            jnp.zeros((row_count, head_count, head_dim), jnp.float32),
            jnp.zeros((head_count, bias_table.shape[0]), jnp.float32),
        )
        (d_query, d_table), key_parts = lax.scan(step, start_state, blk_ids)
        d_key, d_value = key_parts
        return (
            d_query,
            d_table,
            d_key.reshape(seq_len, model_width),
            d_value.reshape(seq_len, model_width),
        )

    back_inputs = (
        query_heads,
        key_heads,
        value_heads,
        seg_queries,
        segments,
        d_unnorm_all,
        correction_all,
    )
    d_query_all, d_table_all, d_key_all, d_value_all = lax.map(attend_back, back_inputs)
    d_key_own, d_value_own = (
        lax.psum_scatter(
            d_key_all.astype(jnp.bfloat16), "seq", scatter_dimension=1, tiled=True
        ).astype(jnp.float32),
        lax.psum_scatter(
            d_value_all.astype(jnp.bfloat16), "seq", scatter_dimension=1, tiled=True
        ).astype(jnp.float32),
    )
    d_query_b = d_query_all.reshape(token_count, model_width).astype(jnp.bfloat16)
    d_key_b = d_key_own.reshape(token_count, model_width).astype(jnp.bfloat16)
    d_value_b = d_value_own.reshape(token_count, model_width).astype(jnp.bfloat16)
    grad_query = left_matmul(normed, d_query_b)
    grad_key = left_matmul(normed, d_key_b)
    grad_value = left_matmul(normed, d_value_b)
    d_normed = (
        right_matmul(d_query_b, back_query)
        + right_matmul(d_key_b, back_key)
        + right_matmul(d_value_b, back_value)
    )
    _, norm_one_back = jax.vjp(norm_rows, flat_in, gain_attn)
    d_in_norm, grad_gain_attn = norm_one_back(d_normed)
    d_inputs = (d_mixed + d_in_norm).reshape(seq_count, row_count, model_width)
    owned = (
        lax.psum_scatter(grad_query, ("dp", "seq"), scatter_dimension=0, tiled=True),
        lax.psum_scatter(grad_key, ("dp", "seq"), scatter_dimension=0, tiled=True),
        lax.psum_scatter(grad_value, ("dp", "seq"), scatter_dimension=0, tiled=True),
        lax.psum_scatter(grad_out, ("dp", "seq"), scatter_dimension=0, tiled=True),
        lax.psum_scatter(grad_gate, ("dp", "seq"), scatter_dimension=0, tiled=True),
        lax.psum_scatter(grad_up, ("dp", "seq"), scatter_dimension=0, tiled=True),
        lax.psum_scatter(grad_down, ("dp", "seq"), scatter_dimension=0, tiled=True),
    )
    table_local = jnp.transpose(jnp.sum(d_table_all, axis=0))
    gain_one, gain_two, table_grad = lax.psum(
        (grad_gain_attn, grad_gain_ffn, table_local), ("dp", "seq")
    )
    return (
        output,
        d_inputs,
        owned[0],
        owned[1],
        owned[2],
        owned[3],
        owned[4],
        owned[5],
        owned[6],
        gain_one,
        gain_two,
        table_grad,
    )


def pcall(
    body, outs, ins, scratch=(), grid=None, in_specs=None, out_specs=None, name=None, micros=1
):
    kwargs = {}
    if grid is not None:
        kwargs = dict(grid=grid, in_specs=in_specs, out_specs=out_specs)
    else:
        kwargs = dict(
            in_specs=[pl.BlockSpec(memory_space=pltpu.SMEM)]
            + [pl.BlockSpec(memory_space=pltpu.VMEM)] * (len(ins) - 1),
            out_specs=[pl.BlockSpec(memory_space=pltpu.VMEM)] * len(outs),
        )
    return pl.pallas_call(
        body,
        out_shape=outs,
        scratch_shapes=list(scratch),
        compiler_params=pltpu.CompilerParams(vmem_limit_bytes=VMEM_LIMIT),
        cost_estimate=pl.CostEstimate(
            flops=micros * FLOPS_PER_US, bytes_accessed=micros * BYTES_PER_US, transcendentals=0
        ),
        name=name,
        **kwargs,
    )(*ins)


def toeplitz(bucket_row, table_col, block):
    nb = table_col.shape[0]
    width = bucket_row.shape[1]
    ids = lax.broadcasted_iota(jnp.int32, (nb, width), 0)
    per_dist = jnp.sum(jnp.where(bucket_row == ids, table_col, 0.0), axis=0, keepdims=True)
    return pltpu.roll(
        jnp.broadcast_to(per_dist, (block, width)), 0, 1, stride=1, stride_axis=0
    )


def diagonals(acc):
    rows, width = acc.shape
    while rows > 8:
        rows //= 2
        acc = acc[:rows] + pltpu.roll(acc[rows:], width - rows, 1)
    row = lax.broadcasted_iota(jnp.int32, acc.shape, 0)
    for bit in (1, 2, 4):
        acc = jnp.where((row & bit) != 0, pltpu.roll(acc, width - bit, 1), acc)
    return jnp.sum(acc, axis=0, keepdims=True)


def attn_fwd_body(n, heads, head_dim, seq_len, rows):
    scale = head_dim ** (-0.5)

    def body(z_ref, *refs):
        x_refs = refs[:n]
        w_ref, gain_ref, segc_ref, segr_ref, bk_ref, tab_ref = refs[n : n + 6]
        h1_ref, qkv_ref, o_ref = refs[n + 6 : n + 9]
        piece_refs = refs[n + 9 : 2 * n + 9]
        toe_ref = refs[2 * n + 9]
        z = z_ref[1]
        for k in range(n):
            start = pl.multiple_of(lax.rem(z + (n - k), n) * rows, rows)
            xv = x_refs[k][...].astype(jnp.float32)
            inv = lax.rsqrt(jnp.mean(xv * xv, axis=-1, keepdims=True) + EPS)
            h1 = (xv * inv * gain_ref[...]).astype(jnp.bfloat16)
            h1_ref[pl.ds(start, rows), :] = h1
            qkv = matmul(h1, w_ref[...]).astype(jnp.bfloat16)
            for i in range(3 * heads):
                part = qkv[:, i * head_dim : (i + 1) * head_dim]
                qkv_ref[i, pl.ds(start, rows), :] = part * scale if i < heads else part
        for h in range(heads):
            toe_ref[h] = toeplitz(bk_ref[...], tab_ref[:, h : h + 1], rows)
        for k in range(n):
            start = pl.multiple_of(lax.rem(z + k, n) * rows, rows)
            seg_q = segc_ref[pl.ds(start, rows), :]
            outs = []
            for h in range(heads):
                s = right_matmul(qkv_ref[h, pl.ds(start, rows), :], qkv_ref[heads + h])
                col = pl.multiple_of(seq_len - start, rows)
                s = s + toe_ref[h, :, pl.ds(col, seq_len)]
                e = jnp.where(seg_q == segr_ref[...], jnp.exp(s), 0.0)
                inv = 1.0 / jnp.sum(e, axis=-1, keepdims=True)
                o = matmul(e.astype(jnp.bfloat16), qkv_ref[2 * heads + h]) * inv
                o_ref[h, pl.ds(start, rows), :] = jnp.concatenate(
                    [o, jnp.broadcast_to(inv, o.shape)], axis=1
                )
                outs.append(o)
            piece_refs[k][...] = pack(jnp.concatenate(outs, axis=1)).astype(jnp.bfloat16)

    return body


def attn_bwd_body(n, heads, head_dim, seq_len, rows):
    scale = head_dim ** (-0.5)

    def body(z_ref, *refs):
        da_refs = refs[:n]
        h1_ref, qkv_ref, o_ref, w_ref = refs[n : n + 4]
        segc_ref, segr_ref, bk_ref, tab_ref, gain_ref = refs[n + 4 : n + 9]
        gw_ref, gtab_ref, gg_ref = refs[n + 9 : n + 12]
        piece_refs = refs[n + 12 : 2 * n + 12]
        toe_ref, acc_ref, du_ref, dl_ref, dq_ref = refs[2 * n + 12 :]
        z = z_ref[1]
        for k in range(n):
            start = pl.multiple_of(lax.rem(z + (n - k), n) * rows, rows)
            da = unpack(da_refs[k][...].astype(jnp.float32))
            for h in range(heads):
                dah = da[:, h * head_dim : (h + 1) * head_dim]
                o = o_ref[h, pl.ds(start, rows), :]
                du = dah * o[:, head_dim:]
                du_ref[h, pl.ds(start, rows), :] = du.astype(jnp.bfloat16)
                dl_ref[h, pl.ds(start, rows), :] = -jnp.sum(
                    du * o[:, :head_dim], axis=-1, keepdims=True
                )
        dq_all, dk_all, dv_all = [], [], []
        lane = lax.broadcasted_iota(jnp.int32, gtab_ref.shape, 1)
        gtab = jnp.zeros(gtab_ref.shape, jnp.float32)
        for h in range(heads):
            toe_ref[...] = toeplitz(bk_ref[...], tab_ref[:, h : h + 1], rows)
            acc_ref[...] = jnp.zeros_like(acc_ref)
            dk = jnp.zeros((head_dim, seq_len), jnp.float32)
            dv = jnp.zeros((head_dim, seq_len), jnp.float32)
            for i in range(n):
                block = pl.ds(i * rows, rows)
                q = qkv_ref[h, block, :]
                du = du_ref[h, block, :]
                cols = pl.ds(seq_len - i * rows, seq_len)
                s = right_matmul(q, qkv_ref[heads + h]) + toe_ref[:, cols]
                e = jnp.where(segc_ref[block, :] == segr_ref[...], jnp.exp(s), 0.0)
                dp = right_matmul(du, qkv_ref[2 * heads + h]) + dl_ref[h, block, :]
                ds = (e * dp).astype(jnp.bfloat16)
                acc_ref[:, cols] += ds.astype(jnp.float32)
                dq = matmul(ds, qkv_ref[heads + h]) * scale
                dq_ref[block, h * head_dim : (h + 1) * head_dim] = dq.astype(jnp.bfloat16)
                dk = dk + left_matmul(q, ds)
                dv = dv + left_matmul(du, e.astype(jnp.bfloat16))
            first = (heads + h) * head_dim
            dq_ref[:, first : first + head_dim] = dk.T.astype(jnp.bfloat16)
            first = (2 * heads + h) * head_dim
            dq_ref[:, first : first + head_dim] = dv.T.astype(jnp.bfloat16)
            sums = diagonals(acc_ref[...])
            ids = lax.broadcasted_iota(jnp.int32, (gtab_ref.shape[0], sums.shape[1]), 0)
            col = jnp.sum(jnp.where(bk_ref[...] == ids, sums, 0.0), axis=1, keepdims=True)
            gtab = gtab + jnp.where(lane == h, col, 0.0)
        gtab_ref[...] = gtab
        gw_ref[...] = left_matmul(h1_ref[...], dq_ref[...]).astype(jnp.bfloat16)
        gain = jnp.zeros(gg_ref.shape, jnp.float32)
        for k in range(n):
            start = pl.multiple_of(lax.rem(z + k, n) * rows, rows)
            part = right_matmul(dq_ref[pl.ds(start, rows), :], w_ref[...])
            piece_refs[k][...] = part.astype(jnp.bfloat16)
            h1 = h1_ref[pl.ds(start, rows), :].astype(jnp.float32)
            gain = gain + jnp.sum(part * h1, axis=0, keepdims=True)
        gg_ref[...] = gain / gain_ref[...]

    return body


def pack(rows_in):
    rows = rows_in.shape[0]
    last = rows_in[:, 128:]
    return jnp.concatenate(
        [rows_in[:, :128], jnp.concatenate([last[: rows // 2], last[rows // 2 :]], axis=1)], axis=0
    )


def unpack(packed):
    rows = packed.shape[0] // 3 * 2
    last = packed[rows:]
    return jnp.concatenate(
        [packed[:rows], jnp.concatenate([last[:, :64], last[:, 64:]], axis=0)], axis=1
    )


def proj_body(n, piece_w):
    def body(z_ref, *refs):
        p_refs = refs[:n]
        x_ref, wo_ref, gain_ref, x1_ref, h2_ref = refs[n:]
        z = z_ref[1]
        x1 = x_ref[...].astype(jnp.float32)
        for k in range(n):
            first = pl.multiple_of(lax.rem(z + (n - k), n) * piece_w, piece_w)
            x1 = x1 + matmul(unpack(p_refs[k][...]), wo_ref[pl.ds(first, piece_w), :])
        x1_ref[...] = x1
        inv = lax.rsqrt(jnp.mean(x1 * x1, axis=-1, keepdims=True) + EPS)
        h2_ref[...] = (x1 * inv * gain_ref[...]).astype(jnp.bfloat16)

    return body


def ffn_body(n, dps, rows, width, unit, row_w, row_d):
    steps = dps // 2

    def body(at_ref, *refs):
        w_refs = refs[:n]
        hm_ref, hn_ref, c_ref = refs[n : n + 3]
        y_ref, dm_ref, dn_ref = refs[n + 3 : n + 6]
        grads_refs = refs[n + 6 : 2 * n + 6]
        wide_s, wgu_s, wd_s, gd_s = refs[2 * n + 6 :]
        j = pl.program_id(0)
        mine = lax.rem(at_ref[0] // 2, 2)

        @pl.when(j == 0)
        def _():
            for k in range(n):
                i = lax.rem(at_ref[1] + (n - k), n)
                piece = w_refs[k][:, : 2 * unit].astype(jnp.float32)
                for d in range(dps):
                    first = pl.multiple_of((d * n + i) * row_w, 8)
                    wide_s[pl.ds(first, row_w), :] = piece[d * row_w : (d + 1) * row_w]
                first = pl.multiple_of(i * row_d, row_d)
                for g in range(width // unit):
                    wd_s[pl.ds(first, row_d), g * unit : (g + 1) * unit] = w_refs[k][
                        g * row_d : (g + 1) * row_d, 2 * unit :
                    ]
            wgu_s[...] = wide_s[...].astype(jnp.bfloat16)
            wide_s[...] = jnp.zeros_like(wide_s)
            gd_s[...] = jnp.zeros_like(gd_s)

        def rows_of(h_ref, d_ref):
            h2 = h_ref[...]
            c = jnp.concatenate([c_ref[0, mine, 0], c_ref[0, 1 - mine, 0]], axis=0)
            wgu, wd = wgu_s[...], wd_s[...]
            both = matmul(h2, wgu)
            gate, up = both[:, :unit], both[:, unit:]
            half = 0.5 + 0.5 * jnp.tanh(GELU_A * (gate + GELU_B * gate * gate * gate))
            gelu = gate * half
            slope = half + 2.0 * gelu * (1.0 - half) * (
                GELU_A * (1.0 + 3.0 * GELU_B * gate * gate)
            )
            hidden = (gelu * up).astype(jnp.bfloat16)
            y = matmul(hidden, wd).astype(jnp.bfloat16)
            y_ref[0, mine, 0] = y[:rows]
            y_ref[0, 1 - mine, 0] = y[rows:]
            dz = right_matmul(c, wd)
            dgu = jnp.concatenate(
                [(dz * up * slope).astype(jnp.bfloat16), (dz * gelu).astype(jnp.bfloat16)], axis=1
            )
            d_ref[...] = right_matmul(dgu, wgu).astype(jnp.bfloat16)
            gd_s[...] += left_matmul(hidden, c)
            wide_s[...] += left_matmul(h2, dgu)

        @pl.when(j < steps // 2)
        def _():
            rows_of(hm_ref, dm_ref)

        @pl.when(j >= steps // 2)
        def _():
            rows_of(hn_ref, dn_ref)

        @pl.when(j == steps - 1)
        def _():
            for k in range(n):
                i = lax.rem(at_ref[1] + k, n)
                parts = []
                for d in range(dps):
                    first = pl.multiple_of((d * n + i) * row_w, 8)
                    parts.append(wide_s[pl.ds(first, row_w), :])
                part = jnp.concatenate(parts, axis=0).astype(jnp.bfloat16)
                grads_refs[k][:, : 2 * unit] = part
                first = pl.multiple_of(i * row_d, row_d)
                for g in range(width // unit):
                    grads_refs[k][g * row_d : (g + 1) * row_d, 2 * unit :] = gd_s[
                        pl.ds(first, row_d), g * unit : (g + 1) * unit
                    ].astype(jnp.bfloat16)

    return body


def ffn(n, dps, rows, width, unit, row_w, row_d, at_arr, unit_weights, h_near, h_far, c_all):
    bf16, f32 = jnp.bfloat16, jnp.float32
    sds = jax.ShapeDtypeStruct
    steps = dps // 2
    half = steps // 2
    tall = dps * row_w
    const = lambda shape: pl.BlockSpec(shape, lambda j, at: (0,) * len(shape))
    near = pl.BlockSpec((2 * rows, width), lambda j, at: (jnp.minimum(j, half - 1), 0))
    far = pl.BlockSpec((2 * rows, width), lambda j, at: (jnp.maximum(j - half, 0), 0))
    owned = pl.BlockSpec(
        (1, 2, 1, rows, width),
        lambda j, at: (
            lax.bitwise_xor(at[0] // 4, lax.rem(j, half)),
            0,
            lax.bitwise_xor(lax.rem(at[0], 2), j // half),
            0,
            0,
        ),
    )
    shape = (dps // 4, 2, 2, rows, width)
    outs = pl.pallas_call(
        ffn_body(n, dps, rows, width, unit, row_w, row_d),
        out_shape=[sds(shape, bf16)]
        + [sds((half * 2 * rows, width), bf16)] * 2
        + [sds((tall, 3 * unit), bf16)] * n,
        grid_spec=pltpu.PrefetchScalarGridSpec(
            num_scalar_prefetch=1,
            grid=(steps,),
            in_specs=[const((tall, 3 * unit))] * n + [near, far, owned],
            out_specs=[owned, near, far] + [const((tall, 3 * unit))] * n,
            scratch_shapes=[
                pltpu.VMEM((width, 2 * unit), f32),
                pltpu.VMEM((width, 2 * unit), bf16),
                pltpu.VMEM((unit, width), bf16),
                pltpu.VMEM((unit, width), f32),
            ],
        ),
        compiler_params=pltpu.CompilerParams(vmem_limit_bytes=VMEM_LIMIT),
        cost_estimate=pl.CostEstimate(flops=0, bytes_accessed=0, transcendentals=0),
        name="ffn",
    )(at_arr, *unit_weights, h_near, h_far, c_all.reshape(shape))
    return outs


def dproj_body(n, piece_w, dps, row_w, unit):
    def body(z_ref, *refs):
        p_refs = refs[:n]
        d_refs = refs[n : n + 4]
        x1_ref, c_ref, wo_ref, gain_ref = refs[n + 4 : n + 8]
        u_refs = refs[n + 8 : 2 * n + 8]
        dx1_ref = refs[2 * n + 8]
        da_refs = refs[2 * n + 9 : 3 * n + 9]
        go_ref, gg_ref, down_ref = refs[3 * n + 9 :]
        width = x1_ref.shape[1]
        z = z_ref[1]
        x1 = x1_ref[...]
        inv = lax.rsqrt(jnp.mean(x1 * x1, axis=-1, keepdims=True) + EPS)
        hat = x1 * inv
        dh = d_refs[0][...].astype(jnp.float32)
        for ref in d_refs[1:]:
            dh = dh + ref[...].astype(jnp.float32)
        gg_ref[...] = jnp.sum(dh * hat, axis=0, keepdims=True)
        scaled = dh * gain_ref[...]
        dxn = inv * (scaled - hat * jnp.mean(scaled * hat, axis=-1, keepdims=True))
        dx1 = c_ref[...].astype(jnp.float32) + dxn
        dx1_ref[...] = dx1
        dy = dx1.astype(jnp.bfloat16)
        for k in range(n):
            first = pl.multiple_of(lax.rem(z + k, n) * piece_w, piece_w)
            da = right_matmul(dy, wo_ref[pl.ds(first, piece_w), :])
            da_refs[k][...] = pack(da).astype(jnp.bfloat16)
        for k in range(n):
            first = pl.multiple_of(lax.rem(z + (n - k), n) * piece_w, piece_w)
            part = left_matmul(unpack(p_refs[k][...]), dy).astype(jnp.bfloat16)
            go_ref[pl.ds(first, piece_w), :width] = part
        units = u_refs[0][...].astype(jnp.float32)
        for ref in u_refs[1:]:
            units = units + ref[...].astype(jnp.float32)
        down_ref[...] = units[:, 2 * unit :]
        lanes = go_ref.shape[1] - width
        parts = []
        for d in range(dps):
            for i in range(2 * unit // lanes):
                parts.append(units[d * row_w : (d + 1) * row_w, i * lanes : (i + 1) * lanes])
        go_ref[:, width:] = jnp.concatenate(parts, axis=0).astype(jnp.bfloat16)

    return body


def final_body(n):
    def body(z_ref, *refs):
        part_refs = refs[:n]
        x_ref, dx1_ref, gain_ref, din_ref = refs[n:]
        dh = part_refs[0][...].astype(jnp.float32)
        for k in range(1, n):
            dh = dh + part_refs[k][...].astype(jnp.float32)
        xv = x_ref[...].astype(jnp.float32)
        inv = lax.rsqrt(jnp.mean(xv * xv, axis=-1, keepdims=True) + EPS)
        hat = xv * inv
        scaled = dh * gain_ref[...]
        dxn = inv * (scaled - hat * jnp.mean(scaled * hat, axis=-1, keepdims=True))
        din_ref[...] = dx1_ref[...] + dxn

    return body


def shift(piece, k, n):
    return lax.ppermute(piece, "seq", [(i, (i + k) % n) for i in range(n)])


def shifts(pieces, n):
    return [pieces[0]] + [shift(pieces[k], k, n) for k in range(1, n)]


def fast(
    inputs,
    d_out,
    segments,
    buckets,
    w_query,
    w_key,
    w_value,
    w_out,
    w_gate,
    w_up,
    w_down,
    gain_attn,
    gain_ffn,
    bias_table,
):
    bf16, f32 = jnp.bfloat16, jnp.float32
    n = lax.axis_size("seq")
    both = ("dp", "seq")
    _, rows, width = inputs.shape
    seq_len = segments.shape[1]
    nb, head_count = bias_table.shape
    head_dim = width // head_count
    heads = head_count // n
    piece_w = width // n
    ff = w_gate.shape[1]
    row_w, row_d = w_query.shape[0], w_down.shape[0]
    groups = -(-row_d // row_w)
    z = lax.axis_index("seq")
    at_arr = jnp.stack([lax.axis_index("dp"), z]).astype(jnp.int32)
    sds = jax.ShapeDtypeStruct

    dps = lax.axis_size("dp")
    half = dps // 2
    unit = ff // dps
    flat_in = inputs.reshape(rows, width)
    flat_c = d_out.reshape(rows, width)

    three = []
    for g in range(n):
        cut = slice(g * piece_w, (g + 1) * piece_w)
        three += [w_query[:, cut], w_key[:, cut], w_value[:, cut]]
    three = jnp.concatenate(three, axis=1)
    def swap(rows_in, mask):
        return lax.ppermute(rows_in, "dp", [(i, i ^ mask) for i in range(dps)])

    at_seq = [lax.rem(z + k, n) for k in range(n)]
    three = three.reshape(row_w, n, 3 * piece_w)
    for_them = [
        jnp.concatenate([lax.dynamic_index_in_dim(three, g, 1, keepdims=False), w_out], axis=1)
        for g in at_seq
    ]
    c_all = lax.all_gather(flat_c, "dp", axis=0, tiled=False)
    from_them = shifts(for_them, n)
    pairs = []
    for d in range(dps):
        cut = slice(d * unit, (d + 1) * unit)
        pairs += [w_gate[:, cut], w_up[:, cut]]
    pairs, early = lax.optimization_barrier((jnp.concatenate(pairs, axis=1), flat_in))
    first_step = shift(flat_in, 1, n)
    from_them, later = lax.optimization_barrier((from_them, flat_in))
    x_all = [flat_in, first_step] + [shift(later, k, n) for k in range(2, n)]
    stack = jnp.stack([from_them[(n - k) % n] for k in range(n)])
    stack = jnp.concatenate([stack, stack], axis=0)
    stack = lax.dynamic_slice_in_dim(stack, lax.rem(n - z, n), n, axis=0)
    stack = stack.reshape(n * row_w, 3 * piece_w + width)
    own_cols, out_rows = stack[:, : 3 * piece_w], stack[:, 3 * piece_w :]
    own_units = lax.all_to_all(pairs, "dp", split_axis=1, concat_axis=0, tiled=True)
    stacked = [w_down[:, g * unit : (g + 1) * unit] for g in range(width // unit)]
    unit_part = jnp.concatenate([own_units, jnp.concatenate(stacked, axis=0)], axis=1)
    w_qkv = lax.all_gather(own_cols, "dp", axis=0, tiled=True)
    x_all, w_qkv, unit_part, c_all, out_rows = lax.optimization_barrier(
        (x_all, w_qkv, unit_part, c_all, out_rows)
    )
    full_out = lax.all_gather(out_rows, "dp", axis=0, tiled=True)

    def plane(rows_in, others):
        got = [rows_in] + [swap(rows_in, 2 * i) for i in range(1, half)]
        got, others = lax.optimization_barrier((got, others))
        near = jnp.concatenate(got, axis=0)
        return near, swap(near, 1), others

    def back(near, far):
        both_cores = near.astype(f32) + swap(far, 1).astype(f32)
        parts = both_cores.astype(bf16).reshape(half, rows, width)
        return [parts[0]] + [swap(parts[i], 2 * i) for i in range(1, half)]


    seg_row = segments.reshape(1, seq_len)
    seg_col = segments.reshape(seq_len, 1)
    bucket_row = buckets.reshape(1, 2 * seq_len)
    table = lax.dynamic_slice_in_dim(bias_table, z * heads, heads, axis=1)
    gain_one = gain_attn.reshape(1, width)
    gain_two = gain_ffn.reshape(1, width)

    outs = pcall(
        attn_fwd_body(n, heads, head_dim, seq_len, rows),
        [
            sds((seq_len, width), bf16),
            sds((3 * heads, seq_len, head_dim), bf16),
            sds((heads, seq_len, 2 * head_dim), f32),
        ]
        + [sds((rows // 2 * 3, 128), bf16)] * n,
        [at_arr, *x_all, w_qkv, gain_one, seg_col, seg_row, bucket_row, table],
        [pltpu.VMEM((heads, rows, 2 * seq_len), f32)],
        name="attn_fwd",
        micros=0,
    )
    h1, qkv, o_heads = outs[:3]
    attn = shifts(outs[3:], n)
    attn, unit_part = lax.optimization_barrier((attn, unit_part))
    unit_weights = shifts([unit_part] * n, n)

    x1, h2 = pcall(
        proj_body(n, piece_w),
        [sds((rows, width), f32), sds((rows, width), bf16)],
        [at_arr, *attn, flat_in, full_out, gain_two],
        name="proj",
        micros=0,
    )
    h_near, h_far, (unit_weights, c_all) = plane(h2, (unit_weights, c_all))

    outs = ffn(
        n, dps, rows, width, unit, row_w, row_d, at_arr, unit_weights, h_near, h_far, c_all
    )
    y_parts, d_near, d_far = outs[:3]
    d_parts, unit_got, y_parts = lax.optimization_barrier(
        (back(d_near, d_far), shifts(outs[3:], n), y_parts)
    )
    lanes = 2 * unit * row_w * dps // width
    outs = pcall(
        dproj_body(n, piece_w, dps, row_w, unit),
        [sds((rows, width), f32)]
        + [sds((rows // 2 * 3, 128), bf16)] * n
        + [
            sds((width, width + lanes), bf16),
            sds((1, width), f32),
            sds((dps * row_w, width - 2 * unit), f32),
        ],
        [at_arr, *attn, *d_parts, x1, flat_c, full_out, gain_two, *unit_got],
        name="dproj",
        micros=0,
    )
    dx1 = outs[0]
    d_pieces = outs[1 : n + 1]
    out_units, gain_two_grad, unit_down = outs[n + 1 :]
    d_attn = shifts(d_pieces, n)
    out_units = lax.all_to_all(out_units, "dp", split_axis=0, concat_axis=0, tiled=True)

    outs = pcall(
        attn_bwd_body(n, heads, head_dim, seq_len, rows),
        [sds((width, 3 * piece_w), bf16), sds((nb, 128), f32), sds((1, width), f32)]
        + [sds((rows, width), bf16)] * n,
        [at_arr, *d_attn, h1, qkv, o_heads, w_qkv, seg_col, seg_row, bucket_row, table, gain_one],
        [
            pltpu.VMEM((rows, 2 * seq_len), f32),
            pltpu.VMEM((rows, 2 * seq_len), f32),
            pltpu.VMEM((heads, seq_len, head_dim), bf16),
            pltpu.VMEM((heads, seq_len, 1), f32),
            pltpu.VMEM((seq_len, 3 * piece_w), bf16),
        ],
        name="attn_bwd",
        micros=20,
    )
    grad_qkv, table_part, gain_one_grad = outs[:3]
    d_normed = shifts(outs[3:], n)

    wide = 3 * piece_w
    table_own = lax.dynamic_update_slice_in_dim(
        jnp.zeros((nb, head_count), f32), table_part[:, :heads], z * heads, axis=1
    )
    small = jnp.concatenate(
        [gain_one_grad.reshape(width), gain_two_grad.reshape(width), table_own.reshape(-1)]
    )
    small = lax.psum(small, "dp")
    grad_qkv, out_units, small = lax.optimization_barrier((grad_qkv, out_units, small))
    small = lax.psum(small, "seq")
    y_own = lax.psum_scatter(
        y_parts.reshape(dps * rows, width), "dp", scatter_dimension=0, tiled=True
    )
    out_units = out_units.reshape(dps, width // dps, width + lanes)
    out_sum = jnp.sum(out_units[:, :, :width].astype(f32), axis=0).astype(bf16)
    square = lax.all_to_all(
        grad_qkv, "dp", split_axis=0, concat_axis=0, tiled=True
    )
    square, y_own, d_normed, small, out_sum = lax.optimization_barrier(
        (square, y_own, d_normed, small, out_sum)
    )
    output = (x1 + y_own.astype(f32)).astype(bf16)
    square = square.reshape(dps, width // dps, wide).astype(f32)
    summed = jnp.concatenate([jnp.sum(square, axis=0).astype(bf16), out_sum], axis=1)
    owned = lax.all_to_all(summed, "seq", split_axis=0, concat_axis=0, tiled=True)
    owned = owned.reshape(n, row_w, wide + width).astype(f32)
    grad_out = jnp.sum(owned[:, :, wide:], axis=0)
    qkv_own = owned[:, :, :wide].reshape(n, row_w, 3, piece_w)
    grad_query, grad_key, grad_value = (
        qkv_own[:, :, i].transpose(1, 0, 2).reshape(row_w, width) for i in range(3)
    )

    stacked = unit_down.reshape(width // unit, row_d, unit)
    grad_down = jnp.concatenate([stacked[g] for g in range(width // unit)], axis=1)
    folded = out_units[:, :, width:].astype(f32).reshape(dps, 2 * unit // lanes, row_w, lanes)
    per = unit // lanes
    grad_gate, grad_up = (
        jnp.concatenate(
            [folded[d, half_at + i] for d in range(dps) for i in range(per)], axis=1
        )
        for half_at in (0, per)
    )

    (d_inputs,) = pcall(
        final_body(n),
        [sds((rows, width), f32)],
        [at_arr, *d_normed, flat_in, dx1, gain_one],
        name="final",
        micros=0,
    )
    return (
        output.reshape(inputs.shape),
        d_inputs.reshape(inputs.shape),
        grad_query,
        grad_key,
        grad_value,
        grad_out,
        grad_gate,
        grad_up,
        grad_down,
        small[:width],
        small[width : 2 * width],
        small[2 * width :].reshape(nb, head_count),
    )


def pick(
    inputs,
    d_out,
    segments,
    buckets,
    w_query,
    w_key,
    w_value,
    w_out,
    w_gate,
    w_up,
    w_down,
    gain_attn,
    gain_ffn,
    bias_table,
):
    n = lax.axis_size("seq")
    seqs, rows, width = inputs.shape
    row_w, row_d, ff = w_query.shape[0], w_down.shape[0], w_gate.shape[1]
    head_count = bias_table.shape[1]
    dps = lax.axis_size("dp")
    fits = (
        seqs == 1
        and dps == 8
        and head_count % n == 0
        and width // n == 192
        and rows == 256
        and width % 256 == 0
        and width // head_count == 64
        and ff == 256 * dps
        and width == 3 * (ff // dps)
        and row_w * dps == 3 * row_d
        and row_w % 8 == 0
        and row_d % 16 == 0
    )
    plan = fast if fits else local
    return plan(
        inputs,
        d_out,
        segments,
        buckets,
        w_query,
        w_key,
        w_value,
        w_out,
        w_gate,
        w_up,
        w_down,
        gain_attn,
        gain_ffn,
        bias_table,
    )


def solution(mesh):
    return jax.shard_map(
        pick,
        mesh=mesh,
        in_specs=(
            P("dp", "seq", None),
            P("dp", "seq", None),
            P("dp", None),
            P(),
            P(("dp", "seq"), None),
            P(("dp", "seq"), None),
            P(("dp", "seq"), None),
            P(("dp", "seq"), None),
            P(("dp", "seq"), None),
            P(("dp", "seq"), None),
            P(("dp", "seq"), None),
            P(),
            P(),
            P(),
        ),
        out_specs=(
            P("dp", "seq", None),
            P("dp", "seq", None),
            P(("dp", "seq"), None),
            P(("dp", "seq"), None),
            P(("dp", "seq"), None),
            P(("dp", "seq"), None),
            P(("dp", "seq"), None),
            P(("dp", "seq"), None),
            P(("dp", "seq"), None),
            P(),
            P(),
            P(),
        ),
        check_vma=False,
    )
```

```python
import jax
import jax.numpy as jnp
from jax import lax
from jax.experimental import pallas as pl
from jax.experimental.pallas import tpu as pltpu
from jax.sharding import PartitionSpec as P

EPS = 1e-06
MASKED = -1000000000.0
HIGHEST = lax.Precision.HIGHEST
GELU_A = 0.7978845608028654
GELU_B = 0.044715
VMEM_LIMIT = 56 * 1024 * 1024
FLOPS_PER_US = 1_150_000_000
BYTES_PER_US = 3_600_000


def norm_rows(values, gain):
    return values * lax.rsqrt(jnp.mean(values * values, axis=-1, keepdims=True) + EPS) * gain


def geglu(gate_act, up_act):
    return jax.nn.gelu(gate_act, approximate=True) * up_act


def matmul(left, right):
    return jnp.dot(left, right, preferred_element_type=jnp.float32)


def left_matmul(left, right):
    return lax.dot_general(
        left, right, (((0,), (0,)), ((), ())), preferred_element_type=jnp.float32
    )


def right_matmul(left, right):
    return lax.dot_general(
        left, right, (((1,), (1,)), ((), ())), preferred_element_type=jnp.float32
    )


def shifted_bias(per_dist, query_count, key_count):
    head_count, width = per_dist.shape
    flipped = per_dist[:, ::-1]
    tiled = jnp.tile(flipped, (1, query_count + 1))[:, : query_count * (width + 1)]
    rows = tiled.reshape(head_count, query_count, width + 1)[:, :, :key_count]
    return rows[:, :, ::-1]


def diagonal_sums(scores):
    head_count, row_count, col_count = scores.shape
    row_width = row_count + col_count
    padded = jnp.concatenate(
        [jnp.zeros((head_count, row_count, row_count), scores.dtype), scores], axis=2
    )
    flat_rows = jnp.concatenate(
        [
            padded.reshape(head_count, row_count * row_width),
            jnp.zeros((head_count, row_count), scores.dtype),
        ],
        axis=1,
    )
    skewed = flat_rows.reshape(head_count, row_count, row_width + 1)
    return jnp.sum(skewed, axis=1)[:, 1:row_width]


def block_parts(
    queries,
    key_heads,
    value_heads,
    seg_query,
    seg_all,
    buckets,
    table,
    first_row,
    blk_index,
    key_block,
):
    query_count = queries.shape[0]
    seq_len = key_heads.shape[0]
    scale = queries.shape[-1] ** (-0.5)
    key_start = blk_index * key_block
    key_blk = lax.dynamic_slice_in_dim(key_heads, key_start, key_block)
    value_blk = lax.dynamic_slice_in_dim(value_heads, key_start, key_block)
    seg_keys = lax.dynamic_slice_in_dim(seg_all, key_start, key_block)
    dist_base = key_start - first_row - query_count + 1 + seq_len
    window = lax.dynamic_slice_in_dim(buckets, dist_base, query_count + key_block - 1)
    onehot = (window[:, None] == jnp.arange(table.shape[0], dtype=jnp.int32)[None, :]).astype(
        jnp.float32
    )
    per_dist = jnp.dot(onehot, table, precision=HIGHEST).T
    bias_blk = shifted_bias(per_dist, query_count, key_block)
    raw_scores = (
        jnp.einsum("qhd,khd->hqk", queries, key_blk, preferred_element_type=jnp.float32) * scale
        + bias_blk
    )
    same_doc = (seg_query[:, None] == seg_keys[None, :])[None]
    weights_exp = jnp.exp(jnp.where(same_doc, raw_scores, MASKED))
    return (key_blk, value_blk, onehot, weights_exp)


def local(
    inputs,
    d_out,
    segments,
    buckets,
    w_query,
    w_key,
    w_value,
    w_out,
    w_gate,
    w_up,
    w_down,
    gain_attn,
    gain_ffn,
    bias_table,
):
    seq_count, row_count, model_width = inputs.shape
    seq_len = segments.shape[1]
    head_count = bias_table.shape[1]
    head_dim = model_width // head_count
    key_block = min(512, seq_len)
    block_count = seq_len // key_block
    token_count = seq_count * row_count
    scale = head_dim ** (-0.5)
    first_row = lax.axis_index("seq") * row_count
    blk_ids = jnp.arange(block_count, dtype=jnp.int32)
    gathered = (
        lax.all_gather(w_query, ("dp", "seq"), axis=0, tiled=True),
        lax.all_gather(w_key, ("dp", "seq"), axis=0, tiled=True),
        lax.all_gather(w_value, ("dp", "seq"), axis=0, tiled=True),
        lax.all_gather(w_out, ("dp", "seq"), axis=0, tiled=True),
        lax.all_gather(w_gate, ("dp", "seq"), axis=0, tiled=True),
        lax.all_gather(w_up, ("dp", "seq"), axis=0, tiled=True),
        lax.all_gather(w_down, ("dp", "seq"), axis=0, tiled=True),
    )
    full_query, full_key, full_value, full_out, full_gate, full_up, full_down = gathered
    flat_in = inputs.reshape(token_count, model_width).astype(jnp.float32)
    normed = norm_rows(flat_in, gain_attn).astype(jnp.bfloat16)
    queries = matmul(normed, full_query).astype(jnp.bfloat16)
    key_rows = (
        matmul(normed, full_key).astype(jnp.bfloat16).reshape(seq_count, row_count, model_width)
    )
    value_rows = (
        matmul(normed, full_value).astype(jnp.bfloat16).reshape(seq_count, row_count, model_width)
    )
    key_all, value_all = (
        lax.all_gather(key_rows, "seq", axis=1, tiled=True),
        lax.all_gather(value_rows, "seq", axis=1, tiled=True),
    )
    query_heads = queries.reshape(seq_count, row_count, head_count, head_dim)
    key_heads = key_all.reshape(seq_count, seq_len, head_count, head_dim)
    value_heads = value_all.reshape(seq_count, seq_len, head_count, head_dim)
    seg_queries = lax.dynamic_slice_in_dim(segments, first_row, row_count, axis=1)

    def attend(packed):
        query_one, key_one, value_one, seg_query, seg_all = packed

        def step(state_in, blk_index):
            totals, summed = state_in
            _, value_blk, _, weights_exp = block_parts(
                query_one,
                key_one,
                value_one,
                seg_query,
                seg_all,
                buckets,
                bias_table,
                first_row,
                blk_index,
                key_block,
            )
            summed = summed + jnp.einsum(
                "hqk,khd->qhd",
                weights_exp.astype(jnp.bfloat16),
                value_blk,
                preferred_element_type=jnp.float32,
            )
            totals = totals + jnp.sum(weights_exp, axis=-1)
            return ((totals, summed), None)

        start_state = (
            jnp.zeros((head_count, row_count), jnp.float32),
            jnp.zeros((row_count, head_count, head_dim), jnp.float32),
        )
        (totals, summed), _ = lax.scan(step, start_state, blk_ids)
        return (summed / jnp.transpose(totals)[:, :, None], totals)

    attn_f32, totals_all = lax.map(
        attend, (query_heads, key_heads, value_heads, seg_queries, segments)
    )
    attn_rows = attn_f32.reshape(token_count, model_width).astype(jnp.bfloat16)
    mixed_rows = flat_in + matmul(attn_rows, full_out)
    normed_two = norm_rows(mixed_rows, gain_ffn).astype(jnp.bfloat16)
    gate_act = matmul(normed_two, full_gate)
    up_act = matmul(normed_two, full_up)
    hidden = geglu(gate_act, up_act).astype(jnp.bfloat16)
    result = mixed_rows + matmul(hidden, full_down)
    output = result.astype(jnp.bfloat16).reshape(seq_count, row_count, model_width)
    back_weights = (
        lax.all_gather(w_query, ("dp", "seq"), axis=0, tiled=True),
        lax.all_gather(w_key, ("dp", "seq"), axis=0, tiled=True),
        lax.all_gather(w_value, ("dp", "seq"), axis=0, tiled=True),
        lax.all_gather(w_out, ("dp", "seq"), axis=0, tiled=True),
        lax.all_gather(w_gate, ("dp", "seq"), axis=0, tiled=True),
        lax.all_gather(w_up, ("dp", "seq"), axis=0, tiled=True),
        lax.all_gather(w_down, ("dp", "seq"), axis=0, tiled=True),
    )
    back_query, back_key, back_value, back_out, back_gate, back_up, back_down = back_weights
    d_res = d_out.reshape(token_count, model_width)
    grad_down = left_matmul(hidden, d_res)
    d_hidden = right_matmul(d_res, back_down)
    _, geglu_back = jax.vjp(geglu, gate_act, up_act)
    d_gate, d_up = geglu_back(d_hidden)
    d_gate = d_gate.astype(jnp.bfloat16)
    d_up = d_up.astype(jnp.bfloat16)
    grad_gate = left_matmul(normed_two, d_gate)
    grad_up = left_matmul(normed_two, d_up)
    d_normed_two = right_matmul(d_gate, back_gate) + right_matmul(d_up, back_up)
    _, norm_two_back = jax.vjp(norm_rows, mixed_rows, gain_ffn)
    d_mixed_norm, grad_gain_ffn = norm_two_back(d_normed_two)
    d_mixed = d_res.astype(jnp.float32) + d_mixed_norm
    d_branch = d_mixed.astype(jnp.bfloat16)
    grad_out = left_matmul(attn_rows, d_branch)
    d_attn = right_matmul(d_branch, back_out).reshape(seq_count, row_count, head_count, head_dim)
    totals_rows = jnp.transpose(totals_all, (0, 2, 1))
    d_unnorm_all = (d_attn / totals_rows[:, :, :, None]).astype(jnp.bfloat16)
    correction_all = -jnp.sum(d_attn * attn_f32, axis=-1) / totals_rows

    def attend_back(packed):
        query_one, key_one, value_one, seg_query, seg_all, d_unnorm, corr_rows = packed
        correction = jnp.transpose(corr_rows)

        def step(state_in, blk_index):
            d_query, d_table = state_in
            key_blk, value_blk, onehot, weights_exp = block_parts(
                query_one,
                key_one,
                value_one,
                seg_query,
                seg_all,
                buckets,
                bias_table,
                first_row,
                blk_index,
                key_block,
            )
            d_prob = jnp.einsum(
                "qhd,khd->hqk", d_unnorm, value_blk, preferred_element_type=jnp.float32
            )
            d_raw = (weights_exp * (d_prob + correction[:, :, None])).astype(jnp.bfloat16)
            d_query = (
                d_query
                + jnp.einsum("hqk,khd->qhd", d_raw, key_blk, preferred_element_type=jnp.float32)
                * scale
            )
            d_table = d_table + jnp.dot(
                diagonal_sums(d_raw.astype(jnp.float32)), onehot, precision=HIGHEST
            )
            d_key = (
                jnp.einsum("hqk,qhd->khd", d_raw, query_one, preferred_element_type=jnp.float32)
                * scale
            )
            d_value = jnp.einsum(
                "hqk,qhd->khd",
                weights_exp.astype(jnp.bfloat16),
                d_unnorm,
                preferred_element_type=jnp.float32,
            )
            return ((d_query, d_table), (d_key, d_value))

        start_state = (
            jnp.zeros((row_count, head_count, head_dim), jnp.float32),
            jnp.zeros((head_count, bias_table.shape[0]), jnp.float32),
        )
        (d_query, d_table), key_parts = lax.scan(step, start_state, blk_ids)
        d_key, d_value = key_parts
        return (
            d_query,
            d_table,
            d_key.reshape(seq_len, model_width),
            d_value.reshape(seq_len, model_width),
        )

    back_inputs = (
        query_heads,
        key_heads,
        value_heads,
        seg_queries,
        segments,
        d_unnorm_all,
        correction_all,
    )
    d_query_all, d_table_all, d_key_all, d_value_all = lax.map(attend_back, back_inputs)
    d_key_own, d_value_own = (
        lax.psum_scatter(
            d_key_all.astype(jnp.bfloat16), "seq", scatter_dimension=1, tiled=True
        ).astype(jnp.float32),
        lax.psum_scatter(
            d_value_all.astype(jnp.bfloat16), "seq", scatter_dimension=1, tiled=True
        ).astype(jnp.float32),
    )
    d_query_b = d_query_all.reshape(token_count, model_width).astype(jnp.bfloat16)
    d_key_b = d_key_own.reshape(token_count, model_width).astype(jnp.bfloat16)
    d_value_b = d_value_own.reshape(token_count, model_width).astype(jnp.bfloat16)
    grad_query = left_matmul(normed, d_query_b)
    grad_key = left_matmul(normed, d_key_b)
    grad_value = left_matmul(normed, d_value_b)
    d_normed = (
        right_matmul(d_query_b, back_query)
        + right_matmul(d_key_b, back_key)
        + right_matmul(d_value_b, back_value)
    )
    _, norm_one_back = jax.vjp(norm_rows, flat_in, gain_attn)
    d_in_norm, grad_gain_attn = norm_one_back(d_normed)
    d_inputs = (d_mixed + d_in_norm).reshape(seq_count, row_count, model_width)
    owned = (
        lax.psum_scatter(grad_query, ("dp", "seq"), scatter_dimension=0, tiled=True),
        lax.psum_scatter(grad_key, ("dp", "seq"), scatter_dimension=0, tiled=True),
        lax.psum_scatter(grad_value, ("dp", "seq"), scatter_dimension=0, tiled=True),
        lax.psum_scatter(grad_out, ("dp", "seq"), scatter_dimension=0, tiled=True),
        lax.psum_scatter(grad_gate, ("dp", "seq"), scatter_dimension=0, tiled=True),
        lax.psum_scatter(grad_up, ("dp", "seq"), scatter_dimension=0, tiled=True),
        lax.psum_scatter(grad_down, ("dp", "seq"), scatter_dimension=0, tiled=True),
    )
    table_local = jnp.transpose(jnp.sum(d_table_all, axis=0))
    gain_one, gain_two, table_grad = lax.psum(
        (grad_gain_attn, grad_gain_ffn, table_local), ("dp", "seq")
    )
    return (
        output,
        d_inputs,
        owned[0],
        owned[1],
        owned[2],
        owned[3],
        owned[4],
        owned[5],
        owned[6],
        gain_one,
        gain_two,
        table_grad,
    )


def pcall(
    body, outs, ins, scratch=(), grid=None, in_specs=None, out_specs=None, name=None, micros=1
):
    kwargs = {}
    if grid is not None:
        kwargs = dict(grid=grid, in_specs=in_specs, out_specs=out_specs)
    else:
        kwargs = dict(
            in_specs=[pl.BlockSpec(memory_space=pltpu.SMEM)]
            + [pl.BlockSpec(memory_space=pltpu.VMEM)] * (len(ins) - 1),
            out_specs=[pl.BlockSpec(memory_space=pltpu.VMEM)] * len(outs),
        )
    return pl.pallas_call(
        body,
        out_shape=outs,
        scratch_shapes=list(scratch),
        compiler_params=pltpu.CompilerParams(vmem_limit_bytes=VMEM_LIMIT),
        cost_estimate=pl.CostEstimate(
            flops=micros * FLOPS_PER_US, bytes_accessed=micros * BYTES_PER_US, transcendentals=0
        ),
        name=name,
        **kwargs,
    )(*ins)


def toeplitz(bucket_row, table_col, block):
    nb = table_col.shape[0]
    width = bucket_row.shape[1]
    ids = lax.broadcasted_iota(jnp.int32, (nb, width), 0)
    per_dist = jnp.sum(jnp.where(bucket_row == ids, table_col, 0.0), axis=0, keepdims=True)
    return pltpu.roll(
        jnp.broadcast_to(per_dist, (block, width)), 0, 1, stride=1, stride_axis=0
    )


def diagonals(acc):
    rows, width = acc.shape
    while rows > 8:
        rows //= 2
        acc = acc[:rows] + pltpu.roll(acc[rows:], width - rows, 1)
    row = lax.broadcasted_iota(jnp.int32, acc.shape, 0)
    for bit in (1, 2, 4):
        acc = jnp.where((row & bit) != 0, pltpu.roll(acc, width - bit, 1), acc)
    return jnp.sum(acc, axis=0, keepdims=True)


def attn_fwd_body(n, heads, head_dim, seq_len, rows):
    scale = head_dim ** (-0.5)

    def body(z_ref, *refs):
        x_refs = refs[:n]
        w_ref, gain_ref, segc_ref, segr_ref, bk_ref, tab_ref = refs[n : n + 6]
        h1_ref, qkv_ref, o_ref = refs[n + 6 : n + 9]
        piece_refs = refs[n + 9 : 2 * n + 9]
        toe_ref = refs[2 * n + 9]
        z = z_ref[1]
        for k in range(n):
            start = pl.multiple_of(lax.rem(z + (n - k), n) * rows, rows)
            xv = x_refs[k][...].astype(jnp.float32)
            inv = lax.rsqrt(jnp.mean(xv * xv, axis=-1, keepdims=True) + EPS)
            h1 = (xv * inv * gain_ref[...]).astype(jnp.bfloat16)
            h1_ref[pl.ds(start, rows), :] = h1
            qkv = matmul(h1, w_ref[...]).astype(jnp.bfloat16)
            for i in range(3 * heads):
                part = qkv[:, i * head_dim : (i + 1) * head_dim]
                qkv_ref[i, pl.ds(start, rows), :] = part * scale if i < heads else part
        for h in range(heads):
            toe_ref[h] = toeplitz(bk_ref[...], tab_ref[:, h : h + 1], rows)
        cuts = [pl.ds(seq_len - i * rows, seq_len) for i in range(n)]
        same = segc_ref[...] == segr_ref[...]
        for h in range(heads):
            bias = jnp.concatenate([toe_ref[h, :, cut] for cut in cuts], axis=0)
            s = right_matmul(qkv_ref[h], qkv_ref[heads + h]) + bias
            e = jnp.where(same, jnp.exp(s), 0.0)
            inv = 1.0 / jnp.sum(e, axis=-1, keepdims=True)
            o = matmul(e.astype(jnp.bfloat16), qkv_ref[2 * heads + h]) * inv
            o_ref[h] = jnp.concatenate([o, jnp.broadcast_to(inv, o.shape)], axis=1)
        for k in range(n):
            block = pl.ds(pl.multiple_of(lax.rem(z + k, n) * rows, rows), rows)
            outs = [o_ref[h, block, :head_dim] for h in range(heads)]
            piece_refs[k][...] = pack(jnp.concatenate(outs, axis=1)).astype(jnp.bfloat16)

    return body


def attn_bwd_body(n, heads, head_dim, seq_len, rows):
    scale = head_dim ** (-0.5)

    def body(z_ref, *refs):
        da_refs = refs[:n]
        h1_ref, qkv_ref, o_ref, w_ref = refs[n : n + 4]
        segc_ref, segr_ref, bk_ref, tab_ref, gain_ref = refs[n + 4 : n + 9]
        gw_ref, gtab_ref, gg_ref = refs[n + 9 : n + 12]
        piece_refs = refs[n + 12 : 2 * n + 12]
        toe_ref, acc_ref, du_ref, dl_ref, dq_ref = refs[2 * n + 12 :]
        z = z_ref[1]
        for k in range(n):
            start = pl.multiple_of(lax.rem(z + (n - k), n) * rows, rows)
            da = unpack(da_refs[k][...].astype(jnp.float32))
            for h in range(heads):
                dah = da[:, h * head_dim : (h + 1) * head_dim]
                o = o_ref[h, pl.ds(start, rows), :]
                du = dah * o[:, head_dim:]
                du_ref[h, pl.ds(start, rows), :] = du.astype(jnp.bfloat16)
                dl_ref[h, pl.ds(start, rows), :] = -jnp.sum(
                    du * o[:, :head_dim], axis=-1, keepdims=True
                )
        dq_all, dk_all, dv_all = [], [], []
        lane = lax.broadcasted_iota(jnp.int32, gtab_ref.shape, 1)
        gtab = jnp.zeros(gtab_ref.shape, jnp.float32)
        for h in range(heads):
            toe_ref[...] = toeplitz(bk_ref[...], tab_ref[:, h : h + 1], rows)
            acc_ref[...] = jnp.zeros_like(acc_ref)
            q, du = qkv_ref[h], du_ref[h]
            cuts = [pl.ds(seq_len - i * rows, seq_len) for i in range(n)]
            bias = jnp.concatenate([toe_ref[:, cut] for cut in cuts], axis=0)
            s = right_matmul(q, qkv_ref[heads + h]) + bias
            e = jnp.where(segc_ref[...] == segr_ref[...], jnp.exp(s), 0.0)
            dp = right_matmul(du, qkv_ref[2 * heads + h]) + dl_ref[h]
            ds = (e * dp).astype(jnp.bfloat16)
            for i, cut in enumerate(cuts):
                acc_ref[:, cut] += ds[i * rows : (i + 1) * rows].astype(jnp.float32)
            dq = matmul(ds, qkv_ref[heads + h]) * scale
            dq_ref[:, h * head_dim : (h + 1) * head_dim] = dq.astype(jnp.bfloat16)
            dk = left_matmul(q, ds)
            dv = left_matmul(du, e.astype(jnp.bfloat16))
            first = (heads + h) * head_dim
            dq_ref[:, first : first + head_dim] = dk.T.astype(jnp.bfloat16)
            first = (2 * heads + h) * head_dim
            dq_ref[:, first : first + head_dim] = dv.T.astype(jnp.bfloat16)
            sums = diagonals(acc_ref[...])
            ids = lax.broadcasted_iota(jnp.int32, (gtab_ref.shape[0], sums.shape[1]), 0)
            col = jnp.sum(jnp.where(bk_ref[...] == ids, sums, 0.0), axis=1, keepdims=True)
            gtab = gtab + jnp.where(lane == h, col, 0.0)
        gtab_ref[...] = gtab
        gw_ref[...] = left_matmul(h1_ref[...], dq_ref[...]).astype(jnp.bfloat16)
        gain = jnp.zeros(gg_ref.shape, jnp.float32)
        for k in range(n):
            start = pl.multiple_of(lax.rem(z + k, n) * rows, rows)
            part = right_matmul(dq_ref[pl.ds(start, rows), :], w_ref[...])
            piece_refs[k][...] = part.astype(jnp.bfloat16)
            h1 = h1_ref[pl.ds(start, rows), :].astype(jnp.float32)
            gain = gain + jnp.sum(part * h1, axis=0, keepdims=True)
        gg_ref[...] = gain / gain_ref[...]

    return body


def pack(rows_in):
    rows = rows_in.shape[0]
    last = rows_in[:, 128:]
    return jnp.concatenate(
        [rows_in[:, :128], jnp.concatenate([last[: rows // 2], last[rows // 2 :]], axis=1)], axis=0
    )


def unpack(packed):
    rows = packed.shape[0] // 3 * 2
    last = packed[rows:]
    return jnp.concatenate(
        [packed[:rows], jnp.concatenate([last[:, :64], last[:, 64:]], axis=0)], axis=1
    )


def proj_body(n, piece_w):
    def body(z_ref, *refs):
        p_refs = refs[:n]
        x_ref, wo_ref, gain_ref, x1_ref, h2_ref = refs[n:]
        z = z_ref[1]
        x1 = x_ref[...].astype(jnp.float32)
        for k in range(n):
            first = pl.multiple_of(lax.rem(z + (n - k), n) * piece_w, piece_w)
            x1 = x1 + matmul(unpack(p_refs[k][...]), wo_ref[pl.ds(first, piece_w), :])
        x1_ref[...] = x1
        inv = lax.rsqrt(jnp.mean(x1 * x1, axis=-1, keepdims=True) + EPS)
        h2_ref[...] = (x1 * inv * gain_ref[...]).astype(jnp.bfloat16)

    return body


def ffn_body(n, dps, rows, width, unit, row_w, row_d):
    steps = dps // 2

    def body(at_ref, *refs):
        w_refs = refs[:n]
        hm_ref, hn_ref, c_ref = refs[n : n + 3]
        y_ref, dm_ref, dn_ref = refs[n + 3 : n + 6]
        grads_refs = refs[n + 6 : 2 * n + 6]
        wide_s, wgu_s, wd_s, gd_s = refs[2 * n + 6 :]
        j = pl.program_id(0)
        mine = lax.rem(at_ref[0] // 2, 2)

        @pl.when(j == 0)
        def _():
            for k in range(n):
                i = lax.rem(at_ref[1] + (n - k), n)
                piece = w_refs[k][:, : 2 * unit].astype(jnp.float32)
                for d in range(dps):
                    first = pl.multiple_of((d * n + i) * row_w, 8)
                    wide_s[pl.ds(first, row_w), :] = piece[d * row_w : (d + 1) * row_w]
                first = pl.multiple_of(i * row_d, row_d)
                for g in range(width // unit):
                    wd_s[pl.ds(first, row_d), g * unit : (g + 1) * unit] = w_refs[k][
                        g * row_d : (g + 1) * row_d, 2 * unit :
                    ]
            wgu_s[...] = wide_s[...].astype(jnp.bfloat16)
            wide_s[...] = jnp.zeros_like(wide_s)
            gd_s[...] = jnp.zeros_like(gd_s)

        def rows_of(h_ref, d_ref):
            h2 = h_ref[...]
            c = jnp.concatenate([c_ref[0, mine, 0], c_ref[0, 1 - mine, 0]], axis=0)
            wgu, wd = wgu_s[...], wd_s[...]
            both = matmul(h2, wgu)
            gate, up = both[:, :unit], both[:, unit:]
            half = 0.5 + 0.5 * jnp.tanh(GELU_A * (gate + GELU_B * gate * gate * gate))
            gelu = gate * half
            slope = half + 2.0 * gelu * (1.0 - half) * (
                GELU_A * (1.0 + 3.0 * GELU_B * gate * gate)
            )
            hidden = (gelu * up).astype(jnp.bfloat16)
            y = matmul(hidden, wd).astype(jnp.bfloat16)
            y_ref[0, mine, 0] = y[:rows]
            y_ref[0, 1 - mine, 0] = y[rows:]
            dz = right_matmul(c, wd)
            dgu = jnp.concatenate(
                [(dz * up * slope).astype(jnp.bfloat16), (dz * gelu).astype(jnp.bfloat16)], axis=1
            )
            d_ref[...] = right_matmul(dgu, wgu).astype(jnp.bfloat16)
            gd_s[...] += left_matmul(hidden, c)
            wide_s[...] += left_matmul(h2, dgu)

        @pl.when(j < steps // 2)
        def _():
            rows_of(hm_ref, dm_ref)

        @pl.when(j >= steps // 2)
        def _():
            rows_of(hn_ref, dn_ref)

        @pl.when(j == steps - 1)
        def _():
            for k in range(n):
                i = lax.rem(at_ref[1] + k, n)
                parts = []
                for d in range(dps):
                    first = pl.multiple_of((d * n + i) * row_w, 8)
                    parts.append(wide_s[pl.ds(first, row_w), :])
                part = jnp.concatenate(parts, axis=0).astype(jnp.bfloat16)
                grads_refs[k][:, : 2 * unit] = part
                first = pl.multiple_of(i * row_d, row_d)
                for g in range(width // unit):
                    grads_refs[k][g * row_d : (g + 1) * row_d, 2 * unit :] = gd_s[
                        pl.ds(first, row_d), g * unit : (g + 1) * unit
                    ].astype(jnp.bfloat16)

    return body


def ffn(n, dps, rows, width, unit, row_w, row_d, at_arr, unit_weights, h_near, h_far, c_all):
    bf16, f32 = jnp.bfloat16, jnp.float32
    sds = jax.ShapeDtypeStruct
    steps = dps // 2
    half = steps // 2
    tall = dps * row_w
    const = lambda shape: pl.BlockSpec(shape, lambda j, at: (0,) * len(shape))
    near = pl.BlockSpec((2 * rows, width), lambda j, at: (jnp.minimum(j, half - 1), 0))
    far = pl.BlockSpec((2 * rows, width), lambda j, at: (jnp.maximum(j - half, 0), 0))
    owned = pl.BlockSpec(
        (1, 2, 1, rows, width),
        lambda j, at: (
            lax.bitwise_xor(at[0] // 4, lax.rem(j, half)),
            0,
            lax.bitwise_xor(lax.rem(at[0], 2), j // half),
            0,
            0,
        ),
    )
    shape = (dps // 4, 2, 2, rows, width)
    outs = pl.pallas_call(
        ffn_body(n, dps, rows, width, unit, row_w, row_d),
        out_shape=[sds(shape, bf16)]
        + [sds((half * 2 * rows, width), bf16)] * 2
        + [sds((tall, 3 * unit), bf16)] * n,
        grid_spec=pltpu.PrefetchScalarGridSpec(
            num_scalar_prefetch=1,
            grid=(steps,),
            in_specs=[const((tall, 3 * unit))] * n + [near, far, owned],
            out_specs=[owned, near, far] + [const((tall, 3 * unit))] * n,
            scratch_shapes=[
                pltpu.VMEM((width, 2 * unit), f32),
                pltpu.VMEM((width, 2 * unit), bf16),
                pltpu.VMEM((unit, width), bf16),
                pltpu.VMEM((unit, width), f32),
            ],
        ),
        compiler_params=pltpu.CompilerParams(vmem_limit_bytes=VMEM_LIMIT),
        cost_estimate=pl.CostEstimate(flops=0, bytes_accessed=0, transcendentals=0),
        name="ffn",
    )(at_arr, *unit_weights, h_near, h_far, c_all.reshape(shape))
    return outs


def dproj_body(n, piece_w, dps, row_w, unit):
    def body(z_ref, *refs):
        p_refs = refs[:n]
        d_refs = refs[n : n + 4]
        x1_ref, c_ref, wo_ref, gain_ref = refs[n + 4 : n + 8]
        u_refs = refs[n + 8 : 2 * n + 8]
        dx1_ref = refs[2 * n + 8]
        da_refs = refs[2 * n + 9 : 3 * n + 9]
        go_ref, gg_ref, down_ref = refs[3 * n + 9 :]
        width = x1_ref.shape[1]
        z = z_ref[1]
        x1 = x1_ref[...]
        inv = lax.rsqrt(jnp.mean(x1 * x1, axis=-1, keepdims=True) + EPS)
        hat = x1 * inv
        dh = d_refs[0][...].astype(jnp.float32)
        for ref in d_refs[1:]:
            dh = dh + ref[...].astype(jnp.float32)
        gg_ref[...] = jnp.sum(dh * hat, axis=0, keepdims=True)
        scaled = dh * gain_ref[...]
        dxn = inv * (scaled - hat * jnp.mean(scaled * hat, axis=-1, keepdims=True))
        dx1 = c_ref[...].astype(jnp.float32) + dxn
        dx1_ref[...] = dx1
        dy = dx1.astype(jnp.bfloat16)
        for k in range(n):
            first = pl.multiple_of(lax.rem(z + k, n) * piece_w, piece_w)
            da = right_matmul(dy, wo_ref[pl.ds(first, piece_w), :])
            da_refs[k][...] = pack(da).astype(jnp.bfloat16)
        for k in range(n):
            first = pl.multiple_of(lax.rem(z + (n - k), n) * piece_w, piece_w)
            part = left_matmul(unpack(p_refs[k][...]), dy).astype(jnp.bfloat16)
            go_ref[pl.ds(first, piece_w), :width] = part
        units = u_refs[0][...].astype(jnp.float32)
        for ref in u_refs[1:]:
            units = units + ref[...].astype(jnp.float32)
        down_ref[...] = units[:, 2 * unit :]
        lanes = go_ref.shape[1] - width
        parts = []
        for d in range(dps):
            for i in range(2 * unit // lanes):
                parts.append(units[d * row_w : (d + 1) * row_w, i * lanes : (i + 1) * lanes])
        go_ref[:, width:] = jnp.concatenate(parts, axis=0).astype(jnp.bfloat16)

    return body


def final_body(n):
    def body(z_ref, *refs):
        part_refs = refs[:n]
        x_ref, dx1_ref, gain_ref, din_ref = refs[n:]
        dh = part_refs[0][...].astype(jnp.float32)
        for k in range(1, n):
            dh = dh + part_refs[k][...].astype(jnp.float32)
        xv = x_ref[...].astype(jnp.float32)
        inv = lax.rsqrt(jnp.mean(xv * xv, axis=-1, keepdims=True) + EPS)
        hat = xv * inv
        scaled = dh * gain_ref[...]
        dxn = inv * (scaled - hat * jnp.mean(scaled * hat, axis=-1, keepdims=True))
        din_ref[...] = dx1_ref[...] + dxn

    return body


def shift(piece, k, n):
    return lax.ppermute(piece, "seq", [(i, (i + k) % n) for i in range(n)])


def shifts(pieces, n):
    return [pieces[0]] + [shift(pieces[k], k, n) for k in range(1, n)]


def fast(
    inputs,
    d_out,
    segments,
    buckets,
    w_query,
    w_key,
    w_value,
    w_out,
    w_gate,
    w_up,
    w_down,
    gain_attn,
    gain_ffn,
    bias_table,
):
    bf16, f32 = jnp.bfloat16, jnp.float32
    n = lax.axis_size("seq")
    both = ("dp", "seq")
    _, rows, width = inputs.shape
    seq_len = segments.shape[1]
    nb, head_count = bias_table.shape
    head_dim = width // head_count
    heads = head_count // n
    piece_w = width // n
    ff = w_gate.shape[1]
    row_w, row_d = w_query.shape[0], w_down.shape[0]
    groups = -(-row_d // row_w)
    z = lax.axis_index("seq")
    at_arr = jnp.stack([lax.axis_index("dp"), z]).astype(jnp.int32)
    sds = jax.ShapeDtypeStruct

    dps = lax.axis_size("dp")
    half = dps // 2
    unit = ff // dps
    flat_in = inputs.reshape(rows, width)
    flat_c = d_out.reshape(rows, width)

    three = []
    for g in range(n):
        cut = slice(g * piece_w, (g + 1) * piece_w)
        three += [w_query[:, cut], w_key[:, cut], w_value[:, cut]]
    three = jnp.concatenate(three, axis=1)
    def swap(rows_in, mask):
        return lax.ppermute(rows_in, "dp", [(i, i ^ mask) for i in range(dps)])

    at_seq = [lax.rem(z + k, n) for k in range(n)]
    three = three.reshape(row_w, n, 3 * piece_w)
    for_them = [
        jnp.concatenate([lax.dynamic_index_in_dim(three, g, 1, keepdims=False), w_out], axis=1)
        for g in at_seq
    ]
    c_all = lax.all_gather(flat_c, "dp", axis=0, tiled=False)
    from_them = shifts(for_them, n)
    pairs = []
    for d in range(dps):
        cut = slice(d * unit, (d + 1) * unit)
        pairs += [w_gate[:, cut], w_up[:, cut]]
    pairs, early = lax.optimization_barrier((jnp.concatenate(pairs, axis=1), flat_in))
    first_step = shift(flat_in, 1, n)
    from_them, later = lax.optimization_barrier((from_them, flat_in))
    x_all = [flat_in, first_step] + [shift(later, k, n) for k in range(2, n)]
    stack = jnp.stack([from_them[(n - k) % n] for k in range(n)])
    stack = jnp.concatenate([stack, stack], axis=0)
    stack = lax.dynamic_slice_in_dim(stack, lax.rem(n - z, n), n, axis=0)
    stack = stack.reshape(n * row_w, 3 * piece_w + width)
    own_cols, out_rows = stack[:, : 3 * piece_w], stack[:, 3 * piece_w :]
    own_units = lax.all_to_all(pairs, "dp", split_axis=1, concat_axis=0, tiled=True)
    stacked = [w_down[:, g * unit : (g + 1) * unit] for g in range(width // unit)]
    unit_part = jnp.concatenate([own_units, jnp.concatenate(stacked, axis=0)], axis=1)
    w_qkv = lax.all_gather(own_cols, "dp", axis=0, tiled=True)
    seg_row = segments.reshape(1, seq_len)
    seg_col = segments.reshape(seq_len, 1)
    bucket_row = buckets.reshape(1, 2 * seq_len)
    table = lax.dynamic_slice_in_dim(bias_table, z * heads, heads, axis=1)
    unit_first = shift(unit_part, 1, n)
    small_ins = (at_arr, seg_row, seg_col, bucket_row, table)
    x_all, w_qkv, unit_part, c_all, out_rows, small_ins = lax.optimization_barrier(
        (x_all, w_qkv, unit_part, c_all, out_rows, small_ins)
    )
    at_arr, seg_row, seg_col, bucket_row, table = small_ins
    full_out = lax.all_gather(out_rows, "dp", axis=0, tiled=True)

    def plane(rows_in, others):
        got = [rows_in] + [swap(rows_in, 2 * i) for i in range(1, half)]
        got, others = lax.optimization_barrier((got, others))
        near = jnp.concatenate(got, axis=0)
        return near, swap(near, 1), others

    def back(near, far):
        both_cores = near.astype(f32) + swap(far, 1).astype(f32)
        parts = both_cores.astype(bf16).reshape(half, rows, width)
        return [parts[0]] + [swap(parts[i], 2 * i) for i in range(1, half)]


    gain_one = gain_attn.reshape(1, width)
    gain_two = gain_ffn.reshape(1, width)

    outs = pcall(
        attn_fwd_body(n, heads, head_dim, seq_len, rows),
        [
            sds((seq_len, width), bf16),
            sds((3 * heads, seq_len, head_dim), bf16),
            sds((heads, seq_len, 2 * head_dim), f32),
        ]
        + [sds((rows // 2 * 3, 128), bf16)] * n,
        [at_arr, *x_all, w_qkv, gain_one, seg_col, seg_row, bucket_row, table],
        [pltpu.VMEM((heads, rows, 2 * seq_len), f32)],
        name="attn_fwd",
        micros=0,
    )
    h1, qkv, o_heads = outs[:3]
    pieces, unit_first = lax.optimization_barrier((outs[3:], unit_first))
    attn = shifts(pieces, n)
    attn, unit_part = lax.optimization_barrier((attn, unit_part))
    unit_weights = [unit_part, unit_first] + [shift(unit_part, k, n) for k in range(2, n)]

    x1, h2 = pcall(
        proj_body(n, piece_w),
        [sds((rows, width), f32), sds((rows, width), bf16)],
        [at_arr, *attn, flat_in, full_out, gain_two],
        name="proj",
        micros=0,
    )
    h_near, h_far, (unit_weights, c_all) = plane(h2, (unit_weights, c_all))

    outs = ffn(
        n, dps, rows, width, unit, row_w, row_d, at_arr, unit_weights, h_near, h_far, c_all
    )
    y_parts, d_near, d_far = outs[:3]
    d_parts, unit_got, y_parts = lax.optimization_barrier(
        (back(d_near, d_far), shifts(outs[3:], n), y_parts)
    )
    lanes = 2 * unit * row_w * dps // width
    outs = pcall(
        dproj_body(n, piece_w, dps, row_w, unit),
        [sds((rows, width), f32)]
        + [sds((rows // 2 * 3, 128), bf16)] * n
        + [
            sds((width, width + lanes), bf16),
            sds((1, width), f32),
            sds((dps * row_w, width - 2 * unit), f32),
        ],
        [at_arr, *attn, *d_parts, x1, flat_c, full_out, gain_two, *unit_got],
        name="dproj",
        micros=0,
    )
    dx1 = outs[0]
    d_pieces = outs[1 : n + 1]
    out_units, gain_two_grad, unit_down = outs[n + 1 :]
    d_attn = shifts(d_pieces, n)
    out_units = lax.all_to_all(out_units, "dp", split_axis=0, concat_axis=0, tiled=True)

    outs = pcall(
        attn_bwd_body(n, heads, head_dim, seq_len, rows),
        [sds((width, 3 * piece_w), bf16), sds((nb, 128), f32), sds((1, width), f32)]
        + [sds((rows, width), bf16)] * n,
        [at_arr, *d_attn, h1, qkv, o_heads, w_qkv, seg_col, seg_row, bucket_row, table, gain_one],
        [
            pltpu.VMEM((rows, 2 * seq_len), f32),
            pltpu.VMEM((rows, 2 * seq_len), f32),
            pltpu.VMEM((heads, seq_len, head_dim), bf16),
            pltpu.VMEM((heads, seq_len, 1), f32),
            pltpu.VMEM((seq_len, 3 * piece_w), bf16),
        ],
        name="attn_bwd",
        micros=20,
    )
    grad_qkv, table_part, gain_one_grad = outs[:3]
    d_normed = shifts(outs[3:], n)

    wide = 3 * piece_w
    table_own = lax.dynamic_update_slice_in_dim(
        jnp.zeros((nb, head_count), f32), table_part[:, :heads], z * heads, axis=1
    )
    small = jnp.concatenate(
        [gain_one_grad.reshape(width), gain_two_grad.reshape(width), table_own.reshape(-1)]
    )
    small = lax.psum(small, "dp")
    grad_qkv, out_units, small = lax.optimization_barrier((grad_qkv, out_units, small))
    small = lax.psum(small, "seq")
    y_own = lax.psum_scatter(
        y_parts.reshape(dps * rows, width), "dp", scatter_dimension=0, tiled=True
    )
    out_units = out_units.reshape(dps, width // dps, width + lanes)
    out_sum = jnp.sum(out_units[:, :, :width].astype(f32), axis=0).astype(bf16)
    square = lax.all_to_all(
        grad_qkv, "dp", split_axis=0, concat_axis=0, tiled=True
    )
    square, y_own, d_normed, small, out_sum = lax.optimization_barrier(
        (square, y_own, d_normed, small, out_sum)
    )
    output = (x1 + y_own.astype(f32)).astype(bf16)
    square = square.reshape(dps, width // dps, wide).astype(f32)
    summed = jnp.concatenate([jnp.sum(square, axis=0).astype(bf16), out_sum], axis=1)
    owned = lax.all_to_all(summed, "seq", split_axis=0, concat_axis=0, tiled=True)
    owned = owned.reshape(n, row_w, wide + width).astype(f32)
    grad_out = jnp.sum(owned[:, :, wide:], axis=0)
    qkv_own = owned[:, :, :wide].reshape(n, row_w, 3, piece_w)
    grad_query, grad_key, grad_value = (
        qkv_own[:, :, i].transpose(1, 0, 2).reshape(row_w, width) for i in range(3)
    )

    stacked = unit_down.reshape(width // unit, row_d, unit)
    grad_down = jnp.concatenate([stacked[g] for g in range(width // unit)], axis=1)
    folded = out_units[:, :, width:].astype(f32).reshape(dps, 2 * unit // lanes, row_w, lanes)
    per = unit // lanes
    grad_gate, grad_up = (
        jnp.concatenate(
            [folded[d, half_at + i] for d in range(dps) for i in range(per)], axis=1
        )
        for half_at in (0, per)
    )

    (d_inputs,) = pcall(
        final_body(n),
        [sds((rows, width), f32)],
        [at_arr, *d_normed, flat_in, dx1, gain_one],
        name="final",
        micros=0,
    )
    return (
        output.reshape(inputs.shape),
        d_inputs.reshape(inputs.shape),
        grad_query,
        grad_key,
        grad_value,
        grad_out,
        grad_gate,
        grad_up,
        grad_down,
        small[:width],
        small[width : 2 * width],
        small[2 * width :].reshape(nb, head_count),
    )


def pick(
    inputs,
    d_out,
    segments,
    buckets,
    w_query,
    w_key,
    w_value,
    w_out,
    w_gate,
    w_up,
    w_down,
    gain_attn,
    gain_ffn,
    bias_table,
):
    n = lax.axis_size("seq")
    seqs, rows, width = inputs.shape
    row_w, row_d, ff = w_query.shape[0], w_down.shape[0], w_gate.shape[1]
    head_count = bias_table.shape[1]
    dps = lax.axis_size("dp")
    fits = (
        seqs == 1
        and dps == 8
        and head_count % n == 0
        and width // n == 192
        and rows == 256
        and width % 256 == 0
        and width // head_count == 64
        and ff == 256 * dps
        and width == 3 * (ff // dps)
        and row_w * dps == 3 * row_d
        and row_w % 8 == 0
        and row_d % 16 == 0
    )
    plan = fast if fits else local
    return plan(
        inputs,
        d_out,
        segments,
        buckets,
        w_query,
        w_key,
        w_value,
        w_out,
        w_gate,
        w_up,
        w_down,
        gain_attn,
        gain_ffn,
        bias_table,
    )


def solution(mesh):
    return jax.shard_map(
        pick,
        mesh=mesh,
        in_specs=(
            P("dp", "seq", None),
            P("dp", "seq", None),
            P("dp", None),
            P(),
            P(("dp", "seq"), None),
            P(("dp", "seq"), None),
            P(("dp", "seq"), None),
            P(("dp", "seq"), None),
            P(("dp", "seq"), None),
            P(("dp", "seq"), None),
            P(("dp", "seq"), None),
            P(),
            P(),
            P(),
        ),
        out_specs=(
            P("dp", "seq", None),
            P("dp", "seq", None),
            P(("dp", "seq"), None),
            P(("dp", "seq"), None),
            P(("dp", "seq"), None),
            P(("dp", "seq"), None),
            P(("dp", "seq"), None),
            P(("dp", "seq"), None),
            P(("dp", "seq"), None),
            P(),
            P(),
            P(),
        ),
        check_vma=False,
    )
```

```python
import jax
import jax.numpy as jnp
from jax import lax
from jax.experimental import pallas as pl
from jax.experimental.pallas import tpu as pltpu
from jax.sharding import PartitionSpec as P

EPS = 1e-06
MASKED = -1000000000.0
HIGHEST = lax.Precision.HIGHEST
GELU_A = 0.7978845608028654
GELU_B = 0.044715
VMEM_LIMIT = 56 * 1024 * 1024
FLOPS_PER_US = 1_150_000_000
BYTES_PER_US = 3_600_000


def norm_rows(values, gain):
    return values * lax.rsqrt(jnp.mean(values * values, axis=-1, keepdims=True) + EPS) * gain


def geglu(gate_act, up_act):
    return jax.nn.gelu(gate_act, approximate=True) * up_act


def matmul(left, right):
    return jnp.dot(left, right, preferred_element_type=jnp.float32)


def left_matmul(left, right):
    return lax.dot_general(
        left, right, (((0,), (0,)), ((), ())), preferred_element_type=jnp.float32
    )


def right_matmul(left, right):
    return lax.dot_general(
        left, right, (((1,), (1,)), ((), ())), preferred_element_type=jnp.float32
    )


def shifted_bias(per_dist, query_count, key_count):
    head_count, width = per_dist.shape
    flipped = per_dist[:, ::-1]
    tiled = jnp.tile(flipped, (1, query_count + 1))[:, : query_count * (width + 1)]
    rows = tiled.reshape(head_count, query_count, width + 1)[:, :, :key_count]
    return rows[:, :, ::-1]


def diagonal_sums(scores):
    head_count, row_count, col_count = scores.shape
    row_width = row_count + col_count
    padded = jnp.concatenate(
        [jnp.zeros((head_count, row_count, row_count), scores.dtype), scores], axis=2
    )
    flat_rows = jnp.concatenate(
        [
            padded.reshape(head_count, row_count * row_width),
            jnp.zeros((head_count, row_count), scores.dtype),
        ],
        axis=1,
    )
    skewed = flat_rows.reshape(head_count, row_count, row_width + 1)
    return jnp.sum(skewed, axis=1)[:, 1:row_width]


def block_parts(
    queries,
    key_heads,
    value_heads,
    seg_query,
    seg_all,
    buckets,
    table,
    first_row,
    blk_index,
    key_block,
):
    query_count = queries.shape[0]
    seq_len = key_heads.shape[0]
    scale = queries.shape[-1] ** (-0.5)
    key_start = blk_index * key_block
    key_blk = lax.dynamic_slice_in_dim(key_heads, key_start, key_block)
    value_blk = lax.dynamic_slice_in_dim(value_heads, key_start, key_block)
    seg_keys = lax.dynamic_slice_in_dim(seg_all, key_start, key_block)
    dist_base = key_start - first_row - query_count + 1 + seq_len
    window = lax.dynamic_slice_in_dim(buckets, dist_base, query_count + key_block - 1)
    onehot = (window[:, None] == jnp.arange(table.shape[0], dtype=jnp.int32)[None, :]).astype(
        jnp.float32
    )
    per_dist = jnp.dot(onehot, table, precision=HIGHEST).T
    bias_blk = shifted_bias(per_dist, query_count, key_block)
    raw_scores = (
        jnp.einsum("qhd,khd->hqk", queries, key_blk, preferred_element_type=jnp.float32) * scale
        + bias_blk
    )
    same_doc = (seg_query[:, None] == seg_keys[None, :])[None]
    weights_exp = jnp.exp(jnp.where(same_doc, raw_scores, MASKED))
    return (key_blk, value_blk, onehot, weights_exp)


def local(
    inputs,
    d_out,
    segments,
    buckets,
    w_query,
    w_key,
    w_value,
    w_out,
    w_gate,
    w_up,
    w_down,
    gain_attn,
    gain_ffn,
    bias_table,
):
    seq_count, row_count, model_width = inputs.shape
    seq_len = segments.shape[1]
    head_count = bias_table.shape[1]
    head_dim = model_width // head_count
    key_block = min(512, seq_len)
    block_count = seq_len // key_block
    token_count = seq_count * row_count
    scale = head_dim ** (-0.5)
    first_row = lax.axis_index("seq") * row_count
    blk_ids = jnp.arange(block_count, dtype=jnp.int32)
    gathered = (
        lax.all_gather(w_query, ("dp", "seq"), axis=0, tiled=True),
        lax.all_gather(w_key, ("dp", "seq"), axis=0, tiled=True),
        lax.all_gather(w_value, ("dp", "seq"), axis=0, tiled=True),
        lax.all_gather(w_out, ("dp", "seq"), axis=0, tiled=True),
        lax.all_gather(w_gate, ("dp", "seq"), axis=0, tiled=True),
        lax.all_gather(w_up, ("dp", "seq"), axis=0, tiled=True),
        lax.all_gather(w_down, ("dp", "seq"), axis=0, tiled=True),
    )
    full_query, full_key, full_value, full_out, full_gate, full_up, full_down = gathered
    flat_in = inputs.reshape(token_count, model_width).astype(jnp.float32)
    normed = norm_rows(flat_in, gain_attn).astype(jnp.bfloat16)
    queries = matmul(normed, full_query).astype(jnp.bfloat16)
    key_rows = (
        matmul(normed, full_key).astype(jnp.bfloat16).reshape(seq_count, row_count, model_width)
    )
    value_rows = (
        matmul(normed, full_value).astype(jnp.bfloat16).reshape(seq_count, row_count, model_width)
    )
    key_all, value_all = (
        lax.all_gather(key_rows, "seq", axis=1, tiled=True),
        lax.all_gather(value_rows, "seq", axis=1, tiled=True),
    )
    query_heads = queries.reshape(seq_count, row_count, head_count, head_dim)
    key_heads = key_all.reshape(seq_count, seq_len, head_count, head_dim)
    value_heads = value_all.reshape(seq_count, seq_len, head_count, head_dim)
    seg_queries = lax.dynamic_slice_in_dim(segments, first_row, row_count, axis=1)

    def attend(packed):
        query_one, key_one, value_one, seg_query, seg_all = packed

        def step(state_in, blk_index):
            totals, summed = state_in
            _, value_blk, _, weights_exp = block_parts(
                query_one,
                key_one,
                value_one,
                seg_query,
                seg_all,
                buckets,
                bias_table,
                first_row,
                blk_index,
                key_block,
            )
            summed = summed + jnp.einsum(
                "hqk,khd->qhd",
                weights_exp.astype(jnp.bfloat16),
                value_blk,
                preferred_element_type=jnp.float32,
            )
            totals = totals + jnp.sum(weights_exp, axis=-1)
            return ((totals, summed), None)

        start_state = (
            jnp.zeros((head_count, row_count), jnp.float32),
            jnp.zeros((row_count, head_count, head_dim), jnp.float32),
        )
        (totals, summed), _ = lax.scan(step, start_state, blk_ids)
        return (summed / jnp.transpose(totals)[:, :, None], totals)

    attn_f32, totals_all = lax.map(
        attend, (query_heads, key_heads, value_heads, seg_queries, segments)
    )
    attn_rows = attn_f32.reshape(token_count, model_width).astype(jnp.bfloat16)
    mixed_rows = flat_in + matmul(attn_rows, full_out)
    normed_two = norm_rows(mixed_rows, gain_ffn).astype(jnp.bfloat16)
    gate_act = matmul(normed_two, full_gate)
    up_act = matmul(normed_two, full_up)
    hidden = geglu(gate_act, up_act).astype(jnp.bfloat16)
    result = mixed_rows + matmul(hidden, full_down)
    output = result.astype(jnp.bfloat16).reshape(seq_count, row_count, model_width)
    back_weights = (
        lax.all_gather(w_query, ("dp", "seq"), axis=0, tiled=True),
        lax.all_gather(w_key, ("dp", "seq"), axis=0, tiled=True),
        lax.all_gather(w_value, ("dp", "seq"), axis=0, tiled=True),
        lax.all_gather(w_out, ("dp", "seq"), axis=0, tiled=True),
        lax.all_gather(w_gate, ("dp", "seq"), axis=0, tiled=True),
        lax.all_gather(w_up, ("dp", "seq"), axis=0, tiled=True),
        lax.all_gather(w_down, ("dp", "seq"), axis=0, tiled=True),
    )
    back_query, back_key, back_value, back_out, back_gate, back_up, back_down = back_weights
    d_res = d_out.reshape(token_count, model_width)
    grad_down = left_matmul(hidden, d_res)
    d_hidden = right_matmul(d_res, back_down)
    _, geglu_back = jax.vjp(geglu, gate_act, up_act)
    d_gate, d_up = geglu_back(d_hidden)
    d_gate = d_gate.astype(jnp.bfloat16)
    d_up = d_up.astype(jnp.bfloat16)
    grad_gate = left_matmul(normed_two, d_gate)
    grad_up = left_matmul(normed_two, d_up)
    d_normed_two = right_matmul(d_gate, back_gate) + right_matmul(d_up, back_up)
    _, norm_two_back = jax.vjp(norm_rows, mixed_rows, gain_ffn)
    d_mixed_norm, grad_gain_ffn = norm_two_back(d_normed_two)
    d_mixed = d_res.astype(jnp.float32) + d_mixed_norm
    d_branch = d_mixed.astype(jnp.bfloat16)
    grad_out = left_matmul(attn_rows, d_branch)
    d_attn = right_matmul(d_branch, back_out).reshape(seq_count, row_count, head_count, head_dim)
    totals_rows = jnp.transpose(totals_all, (0, 2, 1))
    d_unnorm_all = (d_attn / totals_rows[:, :, :, None]).astype(jnp.bfloat16)
    correction_all = -jnp.sum(d_attn * attn_f32, axis=-1) / totals_rows

    def attend_back(packed):
        query_one, key_one, value_one, seg_query, seg_all, d_unnorm, corr_rows = packed
        correction = jnp.transpose(corr_rows)

        def step(state_in, blk_index):
            d_query, d_table = state_in
            key_blk, value_blk, onehot, weights_exp = block_parts(
                query_one,
                key_one,
                value_one,
                seg_query,
                seg_all,
                buckets,
                bias_table,
                first_row,
                blk_index,
                key_block,
            )
            d_prob = jnp.einsum(
                "qhd,khd->hqk", d_unnorm, value_blk, preferred_element_type=jnp.float32
            )
            d_raw = (weights_exp * (d_prob + correction[:, :, None])).astype(jnp.bfloat16)
            d_query = (
                d_query
                + jnp.einsum("hqk,khd->qhd", d_raw, key_blk, preferred_element_type=jnp.float32)
                * scale
            )
            d_table = d_table + jnp.dot(
                diagonal_sums(d_raw.astype(jnp.float32)), onehot, precision=HIGHEST
            )
            d_key = (
                jnp.einsum("hqk,qhd->khd", d_raw, query_one, preferred_element_type=jnp.float32)
                * scale
            )
            d_value = jnp.einsum(
                "hqk,qhd->khd",
                weights_exp.astype(jnp.bfloat16),
                d_unnorm,
                preferred_element_type=jnp.float32,
            )
            return ((d_query, d_table), (d_key, d_value))

        start_state = (
            jnp.zeros((row_count, head_count, head_dim), jnp.float32),
            jnp.zeros((head_count, bias_table.shape[0]), jnp.float32),
        )
        (d_query, d_table), key_parts = lax.scan(step, start_state, blk_ids)
        d_key, d_value = key_parts
        return (
            d_query,
            d_table,
            d_key.reshape(seq_len, model_width),
            d_value.reshape(seq_len, model_width),
        )

    back_inputs = (
        query_heads,
        key_heads,
        value_heads,
        seg_queries,
        segments,
        d_unnorm_all,
        correction_all,
    )
    d_query_all, d_table_all, d_key_all, d_value_all = lax.map(attend_back, back_inputs)
    d_key_own, d_value_own = (
        lax.psum_scatter(
            d_key_all.astype(jnp.bfloat16), "seq", scatter_dimension=1, tiled=True
        ).astype(jnp.float32),
        lax.psum_scatter(
            d_value_all.astype(jnp.bfloat16), "seq", scatter_dimension=1, tiled=True
        ).astype(jnp.float32),
    )
    d_query_b = d_query_all.reshape(token_count, model_width).astype(jnp.bfloat16)
    d_key_b = d_key_own.reshape(token_count, model_width).astype(jnp.bfloat16)
    d_value_b = d_value_own.reshape(token_count, model_width).astype(jnp.bfloat16)
    grad_query = left_matmul(normed, d_query_b)
    grad_key = left_matmul(normed, d_key_b)
    grad_value = left_matmul(normed, d_value_b)
    d_normed = (
        right_matmul(d_query_b, back_query)
        + right_matmul(d_key_b, back_key)
        + right_matmul(d_value_b, back_value)
    )
    _, norm_one_back = jax.vjp(norm_rows, flat_in, gain_attn)
    d_in_norm, grad_gain_attn = norm_one_back(d_normed)
    d_inputs = (d_mixed + d_in_norm).reshape(seq_count, row_count, model_width)
    owned = (
        lax.psum_scatter(grad_query, ("dp", "seq"), scatter_dimension=0, tiled=True),
        lax.psum_scatter(grad_key, ("dp", "seq"), scatter_dimension=0, tiled=True),
        lax.psum_scatter(grad_value, ("dp", "seq"), scatter_dimension=0, tiled=True),
        lax.psum_scatter(grad_out, ("dp", "seq"), scatter_dimension=0, tiled=True),
        lax.psum_scatter(grad_gate, ("dp", "seq"), scatter_dimension=0, tiled=True),
        lax.psum_scatter(grad_up, ("dp", "seq"), scatter_dimension=0, tiled=True),
        lax.psum_scatter(grad_down, ("dp", "seq"), scatter_dimension=0, tiled=True),
    )
    table_local = jnp.transpose(jnp.sum(d_table_all, axis=0))
    gain_one, gain_two, table_grad = lax.psum(
        (grad_gain_attn, grad_gain_ffn, table_local), ("dp", "seq")
    )
    return (
        output,
        d_inputs,
        owned[0],
        owned[1],
        owned[2],
        owned[3],
        owned[4],
        owned[5],
        owned[6],
        gain_one,
        gain_two,
        table_grad,
    )


def pcall(
    body, outs, ins, scratch=(), grid=None, in_specs=None, out_specs=None, name=None, micros=1
):
    kwargs = {}
    if grid is not None:
        kwargs = dict(grid=grid, in_specs=in_specs, out_specs=out_specs)
    else:
        kwargs = dict(
            in_specs=[pl.BlockSpec(memory_space=pltpu.SMEM)]
            + [pl.BlockSpec(memory_space=pltpu.VMEM)] * (len(ins) - 1),
            out_specs=[pl.BlockSpec(memory_space=pltpu.VMEM)] * len(outs),
        )
    return pl.pallas_call(
        body,
        out_shape=outs,
        scratch_shapes=list(scratch),
        compiler_params=pltpu.CompilerParams(vmem_limit_bytes=VMEM_LIMIT),
        cost_estimate=pl.CostEstimate(
            flops=micros * FLOPS_PER_US, bytes_accessed=micros * BYTES_PER_US, transcendentals=0
        ),
        name=name,
        **kwargs,
    )(*ins)


def toeplitz(bucket_row, table_col, block):
    nb = table_col.shape[0]
    width = bucket_row.shape[1]
    ids = lax.broadcasted_iota(jnp.int32, (nb, width), 0)
    per_dist = jnp.sum(jnp.where(bucket_row == ids, table_col, 0.0), axis=0, keepdims=True)
    return pltpu.roll(
        jnp.broadcast_to(per_dist, (block, width)), 0, 1, stride=1, stride_axis=0
    )


def diagonals(acc):
    rows, width = acc.shape
    while rows > 8:
        rows //= 2
        acc = acc[:rows] + pltpu.roll(acc[rows:], width - rows, 1)
    row = lax.broadcasted_iota(jnp.int32, acc.shape, 0)
    for bit in (1, 2, 4):
        acc = jnp.where((row & bit) != 0, pltpu.roll(acc, width - bit, 1), acc)
    return jnp.sum(acc, axis=0, keepdims=True)


def attn_fwd_body(n, heads, head_dim, seq_len, rows):
    scale = head_dim ** (-0.5)

    def body(z_ref, *refs):
        x_refs = refs[:n]
        w_ref, gain_ref, segc_ref, segr_ref, bk_ref, tab_ref = refs[n : n + 6]
        h1_ref, qkv_ref, o_ref = refs[n + 6 : n + 9]
        piece_refs = refs[n + 9 : 2 * n + 9]
        toe_ref = refs[2 * n + 9]
        z = z_ref[1]
        for k in range(n):
            start = pl.multiple_of(lax.rem(z + (n - k), n) * rows, rows)
            xv = x_refs[k][...].astype(jnp.float32)
            inv = lax.rsqrt(jnp.mean(xv * xv, axis=-1, keepdims=True) + EPS)
            h1 = (xv * inv * gain_ref[...]).astype(jnp.bfloat16)
            h1_ref[pl.ds(start, rows), :] = h1
            qkv = matmul(h1, w_ref[...]).astype(jnp.bfloat16)
            for i in range(3 * heads):
                part = qkv[:, i * head_dim : (i + 1) * head_dim]
                qkv_ref[i, pl.ds(start, rows), :] = part * scale if i < heads else part
        for h in range(heads):
            toe_ref[h] = toeplitz(bk_ref[...], tab_ref[:, h : h + 1], rows)
        cuts = [pl.ds(seq_len - i * rows, seq_len) for i in range(n)]
        same = segc_ref[...] == segr_ref[...]
        for h in range(heads):
            bias = jnp.concatenate([toe_ref[h, :, cut] for cut in cuts], axis=0)
            s = right_matmul(qkv_ref[h], qkv_ref[heads + h]) + bias
            e = jnp.where(same, jnp.exp(s), 0.0)
            inv = 1.0 / jnp.sum(e, axis=-1, keepdims=True)
            o = matmul(e.astype(jnp.bfloat16), qkv_ref[2 * heads + h]) * inv
            o_ref[h] = jnp.concatenate([o, jnp.broadcast_to(inv, o.shape)], axis=1)
        for k in range(n):
            block = pl.ds(pl.multiple_of(lax.rem(z + k, n) * rows, rows), rows)
            outs = [o_ref[h, block, :head_dim] for h in range(heads)]
            piece_refs[k][...] = pack(jnp.concatenate(outs, axis=1)).astype(jnp.bfloat16)

    return body


def attn_bwd_body(n, heads, head_dim, seq_len, rows):
    scale = head_dim ** (-0.5)

    def body(z_ref, *refs):
        da_refs = refs[:n]
        h1_ref, qkv_ref, o_ref, w_ref = refs[n : n + 4]
        segc_ref, segr_ref, bk_ref, tab_ref, gain_ref = refs[n + 4 : n + 9]
        gw_ref, gtab_ref, gg_ref = refs[n + 9 : n + 12]
        piece_refs = refs[n + 12 : 2 * n + 12]
        toe_ref, acc_ref, du_ref, dl_ref, dq_ref = refs[2 * n + 12 :]
        z = z_ref[1]
        for k in range(n):
            start = pl.multiple_of(lax.rem(z + (n - k), n) * rows, rows)
            da = unpack(da_refs[k][...].astype(jnp.float32))
            for h in range(heads):
                dah = da[:, h * head_dim : (h + 1) * head_dim]
                o = o_ref[h, pl.ds(start, rows), :]
                du = dah * o[:, head_dim:]
                du_ref[h, pl.ds(start, rows), :] = du.astype(jnp.bfloat16)
                dl_ref[h, pl.ds(start, rows), :] = -jnp.sum(
                    du * o[:, :head_dim], axis=-1, keepdims=True
                )
        dq_all, dk_all, dv_all = [], [], []
        lane = lax.broadcasted_iota(jnp.int32, gtab_ref.shape, 1)
        gtab = jnp.zeros(gtab_ref.shape, jnp.float32)
        for h in range(heads):
            toe_ref[...] = toeplitz(bk_ref[...], tab_ref[:, h : h + 1], rows)
            acc_ref[...] = jnp.zeros_like(acc_ref)
            q, du = qkv_ref[h], du_ref[h]
            cuts = [pl.ds(seq_len - i * rows, seq_len) for i in range(n)]
            bias = jnp.concatenate([toe_ref[:, cut] for cut in cuts], axis=0)
            s = right_matmul(q, qkv_ref[heads + h]) + bias
            e = jnp.where(segc_ref[...] == segr_ref[...], jnp.exp(s), 0.0)
            dp = right_matmul(du, qkv_ref[2 * heads + h]) + dl_ref[h]
            ds = (e * dp).astype(jnp.bfloat16)
            for i, cut in enumerate(cuts):
                acc_ref[:, cut] += ds[i * rows : (i + 1) * rows].astype(jnp.float32)
            dq = matmul(ds, qkv_ref[heads + h]) * scale
            dq_ref[:, h * head_dim : (h + 1) * head_dim] = dq.astype(jnp.bfloat16)
            dk = left_matmul(q, ds)
            dv = left_matmul(du, e.astype(jnp.bfloat16))
            first = (heads + h) * head_dim
            dq_ref[:, first : first + head_dim] = dk.T.astype(jnp.bfloat16)
            first = (2 * heads + h) * head_dim
            dq_ref[:, first : first + head_dim] = dv.T.astype(jnp.bfloat16)
            sums = diagonals(acc_ref[...])
            ids = lax.broadcasted_iota(jnp.int32, (gtab_ref.shape[0], sums.shape[1]), 0)
            col = jnp.sum(jnp.where(bk_ref[...] == ids, sums, 0.0), axis=1, keepdims=True)
            gtab = gtab + jnp.where(lane == h, col, 0.0)
        gtab_ref[...] = gtab
        gw_ref[...] = left_matmul(h1_ref[...], dq_ref[...]).astype(jnp.bfloat16)
        gain = jnp.zeros(gg_ref.shape, jnp.float32)
        for k in range(n):
            start = pl.multiple_of(lax.rem(z + k, n) * rows, rows)
            part = right_matmul(dq_ref[pl.ds(start, rows), :], w_ref[...])
            piece_refs[k][...] = part.astype(jnp.bfloat16)
            h1 = h1_ref[pl.ds(start, rows), :].astype(jnp.float32)
            gain = gain + jnp.sum(part * h1, axis=0, keepdims=True)
        gg_ref[...] = gain / gain_ref[...]

    return body


def pack(rows_in):
    rows = rows_in.shape[0]
    last = rows_in[:, 128:]
    return jnp.concatenate(
        [rows_in[:, :128], jnp.concatenate([last[: rows // 2], last[rows // 2 :]], axis=1)], axis=0
    )


def unpack(packed):
    rows = packed.shape[0] // 3 * 2
    last = packed[rows:]
    return jnp.concatenate(
        [packed[:rows], jnp.concatenate([last[:, :64], last[:, 64:]], axis=0)], axis=1
    )


def proj_body(n, piece_w):
    def body(z_ref, *refs):
        p_refs = refs[:n]
        x_ref, wo_ref, gain_ref, x1_ref, h2_ref = refs[n:]
        z = z_ref[1]
        x1 = x_ref[...].astype(jnp.float32)
        for k in range(n):
            first = pl.multiple_of(lax.rem(z + (n - k), n) * piece_w, piece_w)
            x1 = x1 + matmul(unpack(p_refs[k][...]), wo_ref[pl.ds(first, piece_w), :])
        x1_ref[...] = x1
        inv = lax.rsqrt(jnp.mean(x1 * x1, axis=-1, keepdims=True) + EPS)
        h2_ref[...] = (x1 * inv * gain_ref[...]).astype(jnp.bfloat16)

    return body


def ffn_body(n, dps, rows, width, unit, row_w, row_d):
    steps = dps // 2

    def body(at_ref, *refs):
        w_refs = refs[:n]
        h_refs, c_ref = refs[n : n + dps], refs[n + dps]
        y_ref, dm_ref, dn_ref = refs[n + dps + 1 : n + dps + 4]
        grads_refs = refs[n + dps + 4 : 2 * n + dps + 4]
        wide_s, wgu_s, wd_s, gd_s = refs[2 * n + dps + 4 :]
        j = pl.program_id(0)
        mine = lax.rem(at_ref[0] // 2, 2)

        @pl.when(j == 0)
        def _():
            for k in range(n):
                i = lax.rem(at_ref[1] + (n - k), n)
                piece = w_refs[k][:, : 2 * unit].astype(jnp.float32)
                for d in range(dps):
                    first = pl.multiple_of((d * n + i) * row_w, 8)
                    wide_s[pl.ds(first, row_w), :] = piece[d * row_w : (d + 1) * row_w]
                first = pl.multiple_of(i * row_d, row_d)
                for g in range(width // unit):
                    wd_s[pl.ds(first, row_d), g * unit : (g + 1) * unit] = w_refs[k][
                        g * row_d : (g + 1) * row_d, 2 * unit :
                    ]
            wgu_s[...] = wide_s[...].astype(jnp.bfloat16)
            wide_s[...] = jnp.zeros_like(wide_s)
            gd_s[...] = jnp.zeros_like(gd_s)

        def rows_of(h_pair, d_ref):
            h2 = jnp.concatenate([h_pair[0][...], h_pair[1][...]], axis=0)
            c = jnp.concatenate([c_ref[0, mine, 0], c_ref[0, 1 - mine, 0]], axis=0)
            wgu, wd = wgu_s[...], wd_s[...]
            both = matmul(h2, wgu)
            gate, up = both[:, :unit], both[:, unit:]
            half = 0.5 + 0.5 * jnp.tanh(GELU_A * (gate + GELU_B * gate * gate * gate))
            gelu = gate * half
            slope = half + 2.0 * gelu * (1.0 - half) * (
                GELU_A * (1.0 + 3.0 * GELU_B * gate * gate)
            )
            hidden = (gelu * up).astype(jnp.bfloat16)
            y = matmul(hidden, wd).astype(jnp.bfloat16)
            y_ref[0, mine, 0] = y[:rows]
            y_ref[0, 1 - mine, 0] = y[rows:]
            dz = right_matmul(c, wd)
            dgu = jnp.concatenate(
                [(dz * up * slope).astype(jnp.bfloat16), (dz * gelu).astype(jnp.bfloat16)], axis=1
            )
            d_ref[...] = right_matmul(dgu, wgu).astype(jnp.bfloat16)
            gd_s[...] += left_matmul(hidden, c)
            wide_s[...] += left_matmul(h2, dgu)

        for step in range(steps):

            @pl.when(j == step)
            def _():
                rows_of(h_refs[2 * step : 2 * step + 2], dm_ref if step < steps // 2 else dn_ref)

        @pl.when(j == steps - 1)
        def _():
            for k in range(n):
                i = lax.rem(at_ref[1] + k, n)
                parts = []
                for d in range(dps):
                    first = pl.multiple_of((d * n + i) * row_w, 8)
                    parts.append(wide_s[pl.ds(first, row_w), :])
                part = jnp.concatenate(parts, axis=0).astype(jnp.bfloat16)
                grads_refs[k][:, : 2 * unit] = part
                first = pl.multiple_of(i * row_d, row_d)
                for g in range(width // unit):
                    grads_refs[k][g * row_d : (g + 1) * row_d, 2 * unit :] = gd_s[
                        pl.ds(first, row_d), g * unit : (g + 1) * unit
                    ].astype(jnp.bfloat16)

    return body


def ffn(n, dps, rows, width, unit, row_w, row_d, at_arr, unit_weights, h_blocks, c_all):
    bf16, f32 = jnp.bfloat16, jnp.float32
    sds = jax.ShapeDtypeStruct
    steps = dps // 2
    half = steps // 2
    tall = dps * row_w
    const = lambda shape: pl.BlockSpec(shape, lambda j, at: (0,) * len(shape))
    near = pl.BlockSpec((2 * rows, width), lambda j, at: (jnp.minimum(j, half - 1), 0))
    far = pl.BlockSpec((2 * rows, width), lambda j, at: (jnp.maximum(j - half, 0), 0))
    owned = pl.BlockSpec(
        (1, 2, 1, rows, width),
        lambda j, at: (
            lax.bitwise_xor(at[0] // 4, lax.rem(j, half)),
            0,
            lax.bitwise_xor(lax.rem(at[0], 2), j // half),
            0,
            0,
        ),
    )
    shape = (dps // 4, 2, 2, rows, width)
    outs = pl.pallas_call(
        ffn_body(n, dps, rows, width, unit, row_w, row_d),
        out_shape=[sds(shape, bf16)]
        + [sds((half * 2 * rows, width), bf16)] * 2
        + [sds((tall, 3 * unit), bf16)] * n,
        grid_spec=pltpu.PrefetchScalarGridSpec(
            num_scalar_prefetch=1,
            grid=(steps,),
            in_specs=[const((tall, 3 * unit))] * n + [const((rows, width))] * dps + [owned],
            out_specs=[owned, near, far] + [const((tall, 3 * unit))] * n,
            scratch_shapes=[
                pltpu.VMEM((width, 2 * unit), f32),
                pltpu.VMEM((width, 2 * unit), bf16),
                pltpu.VMEM((unit, width), bf16),
                pltpu.VMEM((unit, width), f32),
            ],
        ),
        compiler_params=pltpu.CompilerParams(vmem_limit_bytes=VMEM_LIMIT),
        cost_estimate=pl.CostEstimate(flops=0, bytes_accessed=0, transcendentals=0),
        name="ffn",
    )(at_arr, *unit_weights, *h_blocks, c_all.reshape(shape))
    return outs


def dproj_body(n, piece_w, dps, row_w, unit):
    def body(z_ref, *refs):
        p_refs = refs[:n]
        d_refs = refs[n : n + 4]
        x1_ref, c_ref, wo_ref, gain_ref = refs[n + 4 : n + 8]
        u_refs = refs[n + 8 : 2 * n + 8]
        dx1_ref = refs[2 * n + 8]
        da_refs = refs[2 * n + 9 : 3 * n + 9]
        go_ref, gg_ref, down_ref = refs[3 * n + 9 :]
        width = x1_ref.shape[1]
        z = z_ref[1]
        x1 = x1_ref[...]
        inv = lax.rsqrt(jnp.mean(x1 * x1, axis=-1, keepdims=True) + EPS)
        hat = x1 * inv
        dh = d_refs[0][...].astype(jnp.float32)
        for ref in d_refs[1:]:
            dh = dh + ref[...].astype(jnp.float32)
        gg_ref[...] = jnp.sum(dh * hat, axis=0, keepdims=True)
        scaled = dh * gain_ref[...]
        dxn = inv * (scaled - hat * jnp.mean(scaled * hat, axis=-1, keepdims=True))
        dx1 = c_ref[...].astype(jnp.float32) + dxn
        dx1_ref[...] = dx1
        dy = dx1.astype(jnp.bfloat16)
        for k in range(n):
            first = pl.multiple_of(lax.rem(z + k, n) * piece_w, piece_w)
            da = right_matmul(dy, wo_ref[pl.ds(first, piece_w), :])
            da_refs[k][...] = pack(da).astype(jnp.bfloat16)
        for k in range(n):
            first = pl.multiple_of(lax.rem(z + (n - k), n) * piece_w, piece_w)
            part = left_matmul(unpack(p_refs[k][...]), dy).astype(jnp.bfloat16)
            go_ref[pl.ds(first, piece_w), :width] = part
        units = u_refs[0][...].astype(jnp.float32)
        for ref in u_refs[1:]:
            units = units + ref[...].astype(jnp.float32)
        down_ref[...] = units[:, 2 * unit :]
        lanes = go_ref.shape[1] - width
        parts = []
        for d in range(dps):
            for i in range(2 * unit // lanes):
                parts.append(units[d * row_w : (d + 1) * row_w, i * lanes : (i + 1) * lanes])
        go_ref[:, width:] = jnp.concatenate(parts, axis=0).astype(jnp.bfloat16)

    return body


def final_body(n):
    def body(z_ref, *refs):
        part_refs = refs[:n]
        x_ref, dx1_ref, gain_ref, din_ref = refs[n:]
        dh = part_refs[0][...].astype(jnp.float32)
        for k in range(1, n):
            dh = dh + part_refs[k][...].astype(jnp.float32)
        xv = x_ref[...].astype(jnp.float32)
        inv = lax.rsqrt(jnp.mean(xv * xv, axis=-1, keepdims=True) + EPS)
        hat = xv * inv
        scaled = dh * gain_ref[...]
        dxn = inv * (scaled - hat * jnp.mean(scaled * hat, axis=-1, keepdims=True))
        din_ref[...] = dx1_ref[...] + dxn

    return body


def shift(piece, k, n):
    return lax.ppermute(piece, "seq", [(i, (i + k) % n) for i in range(n)])


def shifts(pieces, n):
    return [pieces[0]] + [shift(pieces[k], k, n) for k in range(1, n)]


def fast(
    inputs,
    d_out,
    segments,
    buckets,
    w_query,
    w_key,
    w_value,
    w_out,
    w_gate,
    w_up,
    w_down,
    gain_attn,
    gain_ffn,
    bias_table,
):
    bf16, f32 = jnp.bfloat16, jnp.float32
    n = lax.axis_size("seq")
    both = ("dp", "seq")
    _, rows, width = inputs.shape
    seq_len = segments.shape[1]
    nb, head_count = bias_table.shape
    head_dim = width // head_count
    heads = head_count // n
    piece_w = width // n
    ff = w_gate.shape[1]
    row_w, row_d = w_query.shape[0], w_down.shape[0]
    groups = -(-row_d // row_w)
    z = lax.axis_index("seq")
    at_arr = jnp.stack([lax.axis_index("dp"), z]).astype(jnp.int32)
    sds = jax.ShapeDtypeStruct

    dps = lax.axis_size("dp")
    half = dps // 2
    unit = ff // dps
    flat_in = inputs.reshape(rows, width)
    flat_c = d_out.reshape(rows, width)

    three = []
    for g in range(n):
        cut = slice(g * piece_w, (g + 1) * piece_w)
        three += [w_query[:, cut], w_key[:, cut], w_value[:, cut]]
    three = jnp.concatenate(three, axis=1)
    def swap(rows_in, mask):
        return lax.ppermute(rows_in, "dp", [(i, i ^ mask) for i in range(dps)])

    at_seq = [lax.rem(z + k, n) for k in range(n)]
    three = three.reshape(row_w, n, 3 * piece_w)
    for_them = [
        jnp.concatenate([lax.dynamic_index_in_dim(three, g, 1, keepdims=False), w_out], axis=1)
        for g in at_seq
    ]
    c_all = lax.all_gather(flat_c, "dp", axis=0, tiled=False)
    from_them = shifts(for_them, n)
    pairs = []
    for d in range(dps):
        cut = slice(d * unit, (d + 1) * unit)
        pairs += [w_gate[:, cut], w_up[:, cut]]
    pairs, early = lax.optimization_barrier((jnp.concatenate(pairs, axis=1), flat_in))
    first_step = shift(flat_in, 1, n)
    from_them, later = lax.optimization_barrier((from_them, flat_in))
    x_all = [flat_in, first_step] + [shift(later, k, n) for k in range(2, n)]
    stack = jnp.stack([from_them[(n - k) % n] for k in range(n)])
    stack = jnp.concatenate([stack, stack], axis=0)
    stack = lax.dynamic_slice_in_dim(stack, lax.rem(n - z, n), n, axis=0)
    stack = stack.reshape(n * row_w, 3 * piece_w + width)
    own_cols, out_rows = stack[:, : 3 * piece_w], stack[:, 3 * piece_w :]
    own_units = lax.all_to_all(pairs, "dp", split_axis=1, concat_axis=0, tiled=True)
    stacked = [w_down[:, g * unit : (g + 1) * unit] for g in range(width // unit)]
    unit_part = jnp.concatenate([own_units, jnp.concatenate(stacked, axis=0)], axis=1)
    w_qkv = lax.all_gather(own_cols, "dp", axis=0, tiled=True)
    seg_row = segments.reshape(1, seq_len)
    seg_col = segments.reshape(seq_len, 1)
    bucket_row = buckets.reshape(1, 2 * seq_len)
    table = lax.dynamic_slice_in_dim(bias_table, z * heads, heads, axis=1)
    unit_first = shift(unit_part, 1, n)
    small_ins = (at_arr, seg_row, seg_col, bucket_row, table)
    x_all, w_qkv, unit_part, c_all, out_rows, small_ins = lax.optimization_barrier(
        (x_all, w_qkv, unit_part, c_all, out_rows, small_ins)
    )
    at_arr, seg_row, seg_col, bucket_row, table = small_ins
    full_out = lax.all_gather(out_rows, "dp", axis=0, tiled=True)

    def back(near, far):
        both_cores = near.astype(f32) + swap(far, 1).astype(f32)
        parts = both_cores.astype(bf16).reshape(half, rows, width)
        return [parts[0]] + [swap(parts[i], 2 * i) for i in range(1, half)]


    gain_one = gain_attn.reshape(1, width)
    gain_two = gain_ffn.reshape(1, width)

    outs = pcall(
        attn_fwd_body(n, heads, head_dim, seq_len, rows),
        [
            sds((seq_len, width), bf16),
            sds((3 * heads, seq_len, head_dim), bf16),
            sds((heads, seq_len, 2 * head_dim), f32),
        ]
        + [sds((rows // 2 * 3, 128), bf16)] * n,
        [at_arr, *x_all, w_qkv, gain_one, seg_col, seg_row, bucket_row, table],
        [pltpu.VMEM((heads, rows, 2 * seq_len), f32)],
        name="attn_fwd",
        micros=0,
    )
    h1, qkv, o_heads = outs[:3]
    pieces, unit_first = lax.optimization_barrier((outs[3:], unit_first))
    attn = shifts(pieces, n)
    attn, unit_part = lax.optimization_barrier((attn, unit_part))
    unit_weights = [unit_part, unit_first] + [shift(unit_part, k, n) for k in range(2, n)]

    x1, h2 = pcall(
        proj_body(n, piece_w),
        [sds((rows, width), f32), sds((rows, width), bf16)],
        [at_arr, *attn, flat_in, full_out, gain_two],
        name="proj",
        micros=0,
    )
    near = [h2] + [swap(h2, 2 * i) for i in range(1, half)]
    far = [swap(near[0], 1)]
    near, unit_weights, c_all = lax.optimization_barrier((near, unit_weights, c_all))
    h_blocks = near + far + [swap(rows_in, 1) for rows_in in near[1:]]

    outs = ffn(
        n, dps, rows, width, unit, row_w, row_d, at_arr, unit_weights, h_blocks, c_all
    )
    y_parts, d_near, d_far = outs[:3]
    d_parts, unit_got, y_parts = lax.optimization_barrier(
        (back(d_near, d_far), shifts(outs[3:], n), y_parts)
    )
    lanes = 2 * unit * row_w * dps // width
    outs = pcall(
        dproj_body(n, piece_w, dps, row_w, unit),
        [sds((rows, width), f32)]
        + [sds((rows // 2 * 3, 128), bf16)] * n
        + [
            sds((width, width + lanes), bf16),
            sds((1, width), f32),
            sds((dps * row_w, width - 2 * unit), f32),
        ],
        [at_arr, *attn, *d_parts, x1, flat_c, full_out, gain_two, *unit_got],
        name="dproj",
        micros=0,
    )
    dx1 = outs[0]
    d_pieces = outs[1 : n + 1]
    out_units, gain_two_grad, unit_down = outs[n + 1 :]
    d_attn = shifts(d_pieces, n)
    out_units = lax.all_to_all(out_units, "dp", split_axis=0, concat_axis=0, tiled=True)

    outs = pcall(
        attn_bwd_body(n, heads, head_dim, seq_len, rows),
        [sds((width, 3 * piece_w), bf16), sds((nb, 128), f32), sds((1, width), f32)]
        + [sds((rows, width), bf16)] * n,
        [at_arr, *d_attn, h1, qkv, o_heads, w_qkv, seg_col, seg_row, bucket_row, table, gain_one],
        [
            pltpu.VMEM((rows, 2 * seq_len), f32),
            pltpu.VMEM((rows, 2 * seq_len), f32),
            pltpu.VMEM((heads, seq_len, head_dim), bf16),
            pltpu.VMEM((heads, seq_len, 1), f32),
            pltpu.VMEM((seq_len, 3 * piece_w), bf16),
        ],
        name="attn_bwd",
        micros=20,
    )
    grad_qkv, table_part, gain_one_grad = outs[:3]
    d_normed = shifts(outs[3:], n)

    wide = 3 * piece_w
    table_own = lax.dynamic_update_slice_in_dim(
        jnp.zeros((nb, head_count), f32), table_part[:, :heads], z * heads, axis=1
    )
    small = jnp.concatenate(
        [gain_one_grad.reshape(width), gain_two_grad.reshape(width), table_own.reshape(-1)]
    )
    small = lax.psum(small, "dp")
    grad_qkv, out_units, small = lax.optimization_barrier((grad_qkv, out_units, small))
    small = lax.psum(small, "seq")
    y_own = lax.psum_scatter(
        y_parts.reshape(dps * rows, width), "dp", scatter_dimension=0, tiled=True
    )
    out_units = out_units.reshape(dps, width // dps, width + lanes)
    out_sum = jnp.sum(out_units[:, :, :width].astype(f32), axis=0).astype(bf16)
    square = lax.all_to_all(
        grad_qkv, "dp", split_axis=0, concat_axis=0, tiled=True
    )
    square, y_own, d_normed, small, out_sum = lax.optimization_barrier(
        (square, y_own, d_normed, small, out_sum)
    )
    output = (x1 + y_own.astype(f32)).astype(bf16)
    square = square.reshape(dps, width // dps, wide).astype(f32)
    summed = jnp.concatenate([jnp.sum(square, axis=0).astype(bf16), out_sum], axis=1)
    owned = lax.all_to_all(summed, "seq", split_axis=0, concat_axis=0, tiled=True)
    owned = owned.reshape(n, row_w, wide + width).astype(f32)
    grad_out = jnp.sum(owned[:, :, wide:], axis=0)
    qkv_own = owned[:, :, :wide].reshape(n, row_w, 3, piece_w)
    grad_query, grad_key, grad_value = (
        qkv_own[:, :, i].transpose(1, 0, 2).reshape(row_w, width) for i in range(3)
    )

    stacked = unit_down.reshape(width // unit, row_d, unit)
    grad_down = jnp.concatenate([stacked[g] for g in range(width // unit)], axis=1)
    folded = out_units[:, :, width:].astype(f32).reshape(dps, 2 * unit // lanes, row_w, lanes)
    per = unit // lanes
    grad_gate, grad_up = (
        jnp.concatenate(
            [folded[d, half_at + i] for d in range(dps) for i in range(per)], axis=1
        )
        for half_at in (0, per)
    )

    (d_inputs,) = pcall(
        final_body(n),
        [sds((rows, width), f32)],
        [at_arr, *d_normed, flat_in, dx1, gain_one],
        name="final",
        micros=0,
    )
    return (
        output.reshape(inputs.shape),
        d_inputs.reshape(inputs.shape),
        grad_query,
        grad_key,
        grad_value,
        grad_out,
        grad_gate,
        grad_up,
        grad_down,
        small[:width],
        small[width : 2 * width],
        small[2 * width :].reshape(nb, head_count),
    )


def pick(
    inputs,
    d_out,
    segments,
    buckets,
    w_query,
    w_key,
    w_value,
    w_out,
    w_gate,
    w_up,
    w_down,
    gain_attn,
    gain_ffn,
    bias_table,
):
    n = lax.axis_size("seq")
    seqs, rows, width = inputs.shape
    row_w, row_d, ff = w_query.shape[0], w_down.shape[0], w_gate.shape[1]
    head_count = bias_table.shape[1]
    dps = lax.axis_size("dp")
    fits = (
        seqs == 1
        and dps == 8
        and head_count % n == 0
        and width // n == 192
        and rows == 256
        and width % 256 == 0
        and width // head_count == 64
        and ff == 256 * dps
        and width == 3 * (ff // dps)
        and row_w * dps == 3 * row_d
        and row_w % 8 == 0
        and row_d % 16 == 0
    )
    plan = fast if fits else local
    return plan(
        inputs,
        d_out,
        segments,
        buckets,
        w_query,
        w_key,
        w_value,
        w_out,
        w_gate,
        w_up,
        w_down,
        gain_attn,
        gain_ffn,
        bias_table,
    )


def solution(mesh):
    return jax.shard_map(
        pick,
        mesh=mesh,
        in_specs=(
            P("dp", "seq", None),
            P("dp", "seq", None),
            P("dp", None),
            P(),
            P(("dp", "seq"), None),
            P(("dp", "seq"), None),
            P(("dp", "seq"), None),
            P(("dp", "seq"), None),
            P(("dp", "seq"), None),
            P(("dp", "seq"), None),
            P(("dp", "seq"), None),
            P(),
            P(),
            P(),
        ),
        out_specs=(
            P("dp", "seq", None),
            P("dp", "seq", None),
            P(("dp", "seq"), None),
            P(("dp", "seq"), None),
            P(("dp", "seq"), None),
            P(("dp", "seq"), None),
            P(("dp", "seq"), None),
            P(("dp", "seq"), None),
            P(("dp", "seq"), None),
            P(),
            P(),
            P(),
        ),
        check_vma=False,
    )
```
